512 devices in a mesh: blk: 64 (over x, y_hi, z), head: 8 (over y_lo, core).
Axes of the slice: x: 4, y: 8 (y_hi: 2, y_lo: 4; y = y_hi * 4 + y_lo), z: 8, core: 2. Of those that a mesh axis runs over, the one named last changes fastest.
Arguments:
- query_rows: bfloat16 [16384, 2048], P('blk', 'head'), may hold values from -10 to 10
- key_rows: bfloat16 [16384, 2048], P('blk', 'head'), may hold values from -10 to 10
- value_rows: bfloat16 [16384, 2048], P('blk', 'head'), may hold values from -6 to 6
- grad_out: bfloat16 [16384, 4096], P('blk', 'head'), may hold values from -6 to 6
- out_weight: bfloat16 [2048, 4096], P('head'), may hold values from -0.09375 to 0.09375
- mask_types: int32 [128, 128], replicated, may hold values from 0 to 2, as said below
- drop_seed: int32 [1], replicated, may hold values from 0 to 1048575
Outputs:
- grad_query: bfloat16 [16384, 2048], P('blk', 'head')
- grad_key: bfloat16 [16384, 2048], P('blk', 'head')
- grad_value: bfloat16 [16384, 2048], P('blk', 'head')
The draws below stay inside these ranges and needn't reach their ends.
Inputs may be any that keep to these rules, and one draw needn't show every extreme that they name: Blocks are runs of 128 positions. The sequence is cut into documents of whole blocks, each 1 to 4 blocks long, and some document has exactly 4 blocks. Images are pairs of blocks 2m and 2m + 1 of one document. mask_types[a, b] is 0 where blocks a and b lie in different documents; inside a document it is 2 for b < a, 2 for b = a in an image, 1 for b = a in text, 2 for b = a + 1 in one image, and 0 for other b > a. So a position sees keys only of its own shard of 256 positions and of up to 2 earlier ones.
All inputs are finite; a program needn't handle non-finite values.
Results may differ from the reference program's by a relative error of at most 0.029.
Values may be sent and summed in bfloat16 or wider, within the bound.
No kernel may reach another device: no remote copies, remote signals or barrier semaphores. Data moves between devices by JAX's collectives and lax.ppermute only.
A program may use at most 64 MiB of HBM per device.

```python
import jax
import jax.numpy as jnp
from jax import lax

D = 4096
DH = 128
ROWS_DEV = 256
MB = 128
REACH = 2
H_ALL = 16
HD = 2048
SEQ = 16384
NBLOCKS = 128
DOC_BLOCKS = 4
N_BLK = 64


def paired_rows(key):
    folded = jax.random.fold_in(key, 17)
    subkeys = jax.random.split(folded, 2)
    query_draw = jnp.clip(jax.random.normal(subkeys[0], (SEQ, HD), jnp.float32), -6.0, 6.0)
    key_draw = jnp.clip(jax.random.normal(subkeys[1], (SEQ, HD), jnp.float32), -6.0, 6.0)
    return (query_draw, key_draw)


def draw_query_rows(key, part):
    return paired_rows(key)[0].astype(jnp.bfloat16)


def draw_key_rows(key, part):
    return paired_rows(key)[1].astype(jnp.bfloat16)


def draw_mask_types(key, part):
    subkeys = jax.random.split(jax.random.fold_in(key, 5), 2)
    lengths = jax.random.randint(subkeys[0], (NBLOCKS,), 1, DOC_BLOCKS + 1, dtype=jnp.int32)
    lengths = lengths.at[0].set(DOC_BLOCKS)
    starts = jnp.cumsum(lengths) - lengths
    blocks = jnp.arange(NBLOCKS, dtype=jnp.int32)
    doc_id = jnp.sum((starts[None, :] <= blocks[:, None]).astype(jnp.int32), axis=1)
    image_flag = jax.random.randint(subkeys[1], (NBLOCKS // 2,), 0, 3, dtype=jnp.int32) == 0
    image_pair = image_flag & (doc_id[0::2] == doc_id[1::2])
    is_image = jnp.repeat(image_pair, 2)
    pair_id = blocks // 2
    same_doc = doc_id[:, None] == doc_id[None, :]
    same_image = is_image[:, None] & is_image[None, :] & (pair_id[:, None] == pair_id[None, :])
    diagonal = jnp.where(is_image[:, None], 2, 1)
    later = jnp.where(same_image, 2, 0)
    inside = jnp.where(blocks[None, :] < blocks[:, None], 2, jnp.where(blocks[None, :] == blocks[:, None], diagonal, later))
    return jnp.where(same_doc, inside, 0).astype(jnp.int32)


def level_of(rng, dims, pieces, low, high):
    gain = 1.0
    for dim, parts in pieces:
        heights = jax.random.uniform(jax.random.fold_in(jax.random.fold_in(rng, 6), dim), (parts,), jnp.float32, low / len(pieces), high / len(pieces))
        gain = gain * jnp.repeat(jnp.exp(heights), dims[dim] // parts).reshape((-1,) + (1,) * (len(dims) - 1 - dim))
    return gain


def centred(stream_key, dims, width, most, cuts=(), held_as=jnp.bfloat16):
    result = jax.random.normal(stream_key, dims, jnp.float32) * width
    if len(cuts) > 0:
        result = level_of(stream_key, dims, cuts, -0.22, 0.18) * result
    return jnp.clip(result, min=-most, max=most).astype(held_as)


def setup_inputs(seed: int = 0) -> dict:
    key_list = jax.random.split(jax.random.key(seed), 8)
    query_rows = draw_query_rows(jax.random.fold_in(key_list[7], 71), 0)
    key_rows = draw_key_rows(jax.random.fold_in(key_list[7], 71), 0)
    value_rows = centred(key_list[2], (SEQ, HD), 1.0, 6.0, ((0, 64), (1, 8)))
    grad_out = centred(key_list[3], (SEQ, D), 1.0, 6.0, ((0, 64), (1, 8)))
    out_weight = centred(key_list[4], (HD, D), D ** -0.5, 0.09375, ((0, 8),))
    mask_types = draw_mask_types(jax.random.fold_in(key_list[7], 71), 0)
    drop_seed = jax.random.randint(key_list[6], (1,), 0, 1048576).astype(jnp.int32)
    return dict(query_rows=query_rows, key_rows=key_rows, value_rows=value_rows, grad_out=grad_out, out_weight=out_weight, mask_types=mask_types, drop_seed=drop_seed)


drop_level = 6554
keep_scale = 65536.0 / 58982.0
mix_one = 73244475
mix_two = 295559667
mix_three = 668265263


def mixhash(seed_word, head_index, query_pos, key_pos):
    hashed = query_pos * mix_one + key_pos * mix_two + head_index * mix_three + seed_word
    hashed = hashed ^ lax.shift_right_logical(hashed, jnp.int32(16))
    hashed = hashed * mix_one
    hashed = hashed ^ lax.shift_right_logical(hashed, jnp.int32(16))
    hashed = hashed * mix_one
    hashed = hashed ^ lax.shift_right_logical(hashed, jnp.int32(16))
    return ((hashed & 65535) >= drop_level).astype(jnp.float32)


def visible(table_tile, query_pos, key_pos):
    return (table_tile == 2) | ((table_tile == 1) & (key_pos[None, :] <= query_pos[:, None]))


def expand(block_table):
    count_rows, count_cols = block_table.shape
    spread = jnp.broadcast_to(block_table[:, None, :, None], (count_rows, MB, count_cols, MB))
    return spread.reshape(count_rows * MB, count_cols * MB)


def reference(query_rows, key_rows, value_rows, grad_out, out_weight, mask_types, drop_seed):
    score_scale = DH ** -0.5
    margin = REACH * ROWS_DEV
    window = (REACH + 1) * ROWS_DEV
    block_rows = ROWS_DEV // MB
    block_margin = margin // MB
    window_blocks = window // MB
    seed_word = drop_seed[0]
    head_ids = jnp.arange(H_ALL, dtype=jnp.int32)
    grad_attn = jnp.dot(grad_out, out_weight.T, preferred_element_type=jnp.float32).astype(jnp.bfloat16)
    before_pad = ((margin, 0), (0, 0))
    keys_pad = jnp.pad(key_rows, before_pad)
    values_pad = jnp.pad(value_rows, before_pad)
    table_cols = jnp.pad(mask_types, ((0, 0), (block_margin, 0)))
    tiles = jnp.arange(N_BLK, dtype=jnp.int32)

    def heads_of(block_rows_in):
        return block_rows_in.astype(jnp.float32).reshape(block_rows_in.shape[0], H_ALL, DH)

    def query_tile(tile_index):
        first_row = tile_index * ROWS_DEV
        query_tile_rows = heads_of(lax.dynamic_slice_in_dim(query_rows, first_row, ROWS_DEV, 0))
        grad_tile = heads_of(lax.dynamic_slice_in_dim(grad_attn, first_row, ROWS_DEV, 0))
        key_window = heads_of(lax.dynamic_slice_in_dim(keys_pad, first_row, window, 0))
        value_window = heads_of(lax.dynamic_slice_in_dim(values_pad, first_row, window, 0))
        near_table = lax.dynamic_slice(table_cols, (tile_index * block_rows, tile_index * block_rows), (block_rows, window_blocks))
        query_pos = first_row + jnp.arange(ROWS_DEV, dtype=jnp.int32)
        key_pos = first_row - margin + jnp.arange(window, dtype=jnp.int32)
        allowed = visible(expand(near_table), query_pos, key_pos)[None]
        scores = jnp.einsum('qhd,khd->hqk', query_tile_rows, key_window) * score_scale
        masked = jnp.where(allowed, scores, -jnp.inf)
        row_max = jnp.max(masked, axis=2, keepdims=True)
        log_total = row_max + jnp.log(jnp.sum(jnp.exp(masked - row_max), axis=2, keepdims=True))
        attn_prob = jnp.where(allowed, jnp.exp(scores - log_total), 0.0)
        keep_mask = mixhash(seed_word, head_ids[:, None, None], query_pos[None, :, None], key_pos[None, None, :]) * keep_scale
        dropped = (attn_prob * keep_mask).astype(jnp.bfloat16)
        attended = jnp.einsum('hqk,khd->qhd', dropped.astype(jnp.float32), value_window).astype(jnp.bfloat16)
        row_dot = jnp.sum(grad_tile * attended.astype(jnp.float32), axis=2)
        grad_prob = jnp.einsum('qhd,khd->hqk', grad_tile, value_window)
        dscore = (attn_prob * (grad_prob * keep_mask - row_dot.T[:, :, None])).astype(jnp.bfloat16)
        query_grad = jnp.einsum('hqk,khd->qhd', dscore.astype(jnp.float32), key_window) * score_scale
        return query_grad.reshape(ROWS_DEV, H_ALL * DH).astype(jnp.bfloat16), log_total[:, :, 0].T, row_dot

    query_grads, log_totals, row_dots = lax.map(query_tile, tiles)
    grad_query = query_grads.reshape(SEQ, H_ALL * DH)
    log_totals = log_totals.reshape(SEQ, H_ALL)
    row_dots = row_dots.reshape(SEQ, H_ALL)
    after_pad = ((0, margin), (0, 0))
    queries_pad = jnp.pad(query_rows, after_pad)
    grads_pad = jnp.pad(grad_attn, after_pad)
    totals_pad = jnp.pad(log_totals, after_pad)
    dots_pad = jnp.pad(row_dots, after_pad)
    table_rows = jnp.pad(mask_types, ((0, block_margin), (0, 0)))

    def key_tile(tile_index):
        first_row = tile_index * ROWS_DEV
        key_tile_rows = heads_of(lax.dynamic_slice_in_dim(key_rows, first_row, ROWS_DEV, 0))
        value_tile_rows = heads_of(lax.dynamic_slice_in_dim(value_rows, first_row, ROWS_DEV, 0))
        query_window = heads_of(lax.dynamic_slice_in_dim(queries_pad, first_row, window, 0))
        grad_window = heads_of(lax.dynamic_slice_in_dim(grads_pad, first_row, window, 0))
        total_window = lax.dynamic_slice_in_dim(totals_pad, first_row, window, 0)
        dot_window = lax.dynamic_slice_in_dim(dots_pad, first_row, window, 0)
        far_table = lax.dynamic_slice(table_rows, (tile_index * block_rows, tile_index * block_rows), (window_blocks, block_rows))
        query_pos = first_row + jnp.arange(window, dtype=jnp.int32)
        key_pos = first_row + jnp.arange(ROWS_DEV, dtype=jnp.int32)
        allowed = visible(expand(far_table), query_pos, key_pos)[None]
        scores = jnp.einsum('qhd,khd->hqk', query_window, key_tile_rows) * score_scale
        attn_prob = jnp.where(allowed, jnp.exp(scores - total_window.T[:, :, None]), 0.0)
        keep_mask = mixhash(seed_word, head_ids[:, None, None], query_pos[None, :, None], key_pos[None, None, :]) * keep_scale
        dropped = (attn_prob * keep_mask).astype(jnp.bfloat16)
        value_grad = jnp.einsum('hqk,qhd->khd', dropped.astype(jnp.float32), grad_window)
        grad_prob = jnp.einsum('qhd,khd->hqk', grad_window, value_tile_rows)
        dscore = (attn_prob * (grad_prob * keep_mask - dot_window.T[:, :, None])).astype(jnp.bfloat16)
        key_grad = jnp.einsum('hqk,qhd->khd', dscore.astype(jnp.float32), query_window) * score_scale
        return (key_grad.reshape(ROWS_DEV, H_ALL * DH).astype(jnp.bfloat16),
                value_grad.reshape(ROWS_DEV, H_ALL * DH).astype(jnp.bfloat16))

    key_grads, value_grads = lax.map(key_tile, tiles)
    return grad_query, key_grads.reshape(SEQ, H_ALL * DH), value_grads.reshape(SEQ, H_ALL * DH)
```

```python
import jax
import jax.numpy as jnp
from jax import lax
from jax.experimental import pallas as pl
from jax.experimental.pallas import tpu as pltpu
from jax.sharding import PartitionSpec as P

DH = 128
MB = 128
HEADS = 2
ROWS = 256
SLOTS = 5
WIN = SLOTS * MB
FAR = 3 * MB
WIDE = HEADS * DH

drop_level = 6554
keep_scale = 65536.0 / 58982.0
mix_one = 73244475
mix_two = 295559667
mix_three = 668265263
score_scale = DH**-0.5
hidden = -1e30

VMEM = pl.BlockSpec(memory_space=pltpu.VMEM)
SMEM = pl.BlockSpec(memory_space=pltpu.SMEM)


def bf16(value):
    return value.astype(jnp.bfloat16)


def f32(value):
    return value.astype(jnp.float32)


def dot_last(left, right):
    return lax.dot_general(
        left, right, (((1,), (1,)), ((), ())), preferred_element_type=jnp.float32
    )


def dot_first(left, right):
    return lax.dot_general(
        left, right, (((0,), (0,)), ((), ())), preferred_element_type=jnp.float32
    )


def dot(left, right):
    return jnp.dot(left, right, preferred_element_type=jnp.float32)


def bound_of(table, query_block, key_block):
    last = table.shape[0] - 1
    inside = (key_block >= 0) & (query_block <= last)
    kind = table[jnp.minimum(query_block, last), jnp.maximum(key_block, 0)]
    far = jnp.int32(1 << 20)
    bound = jnp.where(kind == 2, far, jnp.where(kind == 1, (query_block - key_block) * MB, -far))
    return jnp.where(inside, bound, -far)


def kept(seed, head, query_block, key_block):
    base = query_block * MB * mix_one + key_block * MB * mix_two + head * mix_three + seed
    rows = lax.broadcasted_iota(jnp.int32, (MB, MB), 0) * mix_one
    cols = lax.broadcasted_iota(jnp.int32, (MB, MB), 1) * mix_two
    hashed = (rows + cols) + base
    for _ in range(2):
        hashed = hashed ^ lax.shift_right_logical(hashed, jnp.int32(16))
        hashed = hashed * mix_one
    hashed = hashed ^ lax.shift_right_logical(hashed, jnp.int32(16))
    return (hashed & 65535) >= drop_level


def column_minus_row():
    return lax.broadcasted_iota(jnp.int32, (MB, MB), 1) - lax.broadcasted_iota(
        jnp.int32, (MB, MB), 0
    )


def forward_kernel(
    table, seed, query, key, value, near, far, signed, message, key_win, value_win
):
    shard = lax.axis_index("blk")
    first_head = lax.axis_index("head") * HEADS
    key_win[0:MB] = far[0:MB]
    key_win[MB:FAR] = near[0:ROWS]
    key_win[FAR:] = key[...]
    value_win[0:MB] = far[MB:]
    value_win[MB:FAR] = near[ROWS:]
    value_win[FAR:] = value[...]
    message[:, 0:WIDE] = query[...]
    ahead = column_minus_row()
    lane = lax.broadcasted_iota(jnp.int32, (MB, MB), 1)
    for block in range(2):
        rows = pl.ds(block * MB, MB)
        query_block = shard * 2 + block
        stats = jnp.zeros((MB, MB), jnp.float32)
        for head in range(HEADS):
            cols = pl.ds(head * DH, DH)
            scores = dot_last(query[rows, cols], key_win[:, cols])
            tiles = []
            for slot in range(block, SLOTS):
                bound = bound_of(table, query_block, shard * 2 - 3 + slot)
                tile = scores[:, slot * MB : (slot + 1) * MB] * score_scale
                tiles.append(jnp.where(ahead <= bound, tile, hidden))
            top = tiles[0]
            for tile in tiles[1:]:
                top = jnp.maximum(top, tile)
            top = jnp.max(top, axis=1, keepdims=True)
            tiles = [jnp.exp(tile - top) for tile in tiles]
            total = tiles[0]
            for tile in tiles[1:]:
                total = total + tile
            total = jnp.sum(total, axis=1, keepdims=True)
            inverse = 1.0 / total
            log_total = top + jnp.log(total)
            drops = []
            for slot in range(block, SLOTS):
                prob = tiles[slot - block] * inverse
                keep = kept(seed[0], first_head + head, query_block, shard * 2 - 3 + slot)
                signed[head, rows, slot * MB : (slot + 1) * MB] = jnp.where(keep, prob, -prob)
                drops.append(bf16(jnp.where(keep, prob * keep_scale, 0.0)))
            if block > 0:
                signed[head, rows, 0:MB] = jnp.zeros((MB, MB), jnp.float32)
            attended = dot(jnp.concatenate(drops, axis=1), value_win[block * MB :, cols])
            message[rows, WIDE + head * DH : WIDE + (head + 1) * DH] = bf16(attended)
            rest = log_total
            for part in range(3):
                piece = f32(bf16(rest))
                stats = jnp.where(lane == head * 3 + part, piece, stats)
                rest = rest - piece
        message[rows, 2 * WIDE :] = bf16(stats)


def later_kernel(table, seed, key, near, far, signed):
    shard = lax.axis_index("blk")
    first_head = lax.axis_index("head") * HEADS
    ahead = column_minus_row()
    for block in range(3):
        source, first = (near, block * MB) if block < 2 else (far, 0)
        query_block = shard * 2 + 2 + block
        for head in range(HEADS):
            cols = pl.ds(head * DH, DH)
            scores = dot_last(source[first : first + MB, cols], key[:, cols]) * score_scale
            stats = f32(source[first : first + MB, 2 * WIDE :])
            log_total = stats[:, 3 * head : 3 * head + 1]
            log_total = log_total + stats[:, 3 * head + 1 : 3 * head + 2]
            log_total = log_total + stats[:, 3 * head + 2 : 3 * head + 3]
            for slot in range(2):
                bound = bound_of(table, query_block, shard * 2 + slot)
                tile = scores[:, slot * MB : (slot + 1) * MB] - log_total
                prob = jnp.exp(jnp.where(ahead <= bound, tile, hidden))
                keep = kept(seed[0], first_head + head, query_block, shard * 2 + slot)
                signed[head, block * MB : (block + 1) * MB, slot * MB : (slot + 1) * MB] = (
                    jnp.where(keep, prob, -prob)
                )


def project_other_kernel(gathered, weight, out):
    width = gathered.shape[2]
    total = dot_last(gathered[0], weight[:, 0:width])
    for part in range(1, gathered.shape[0]):
        total = total + dot_last(gathered[part], weight[:, part * width : (part + 1) * width])
    out[...] = total


def project_own_kernel(gathered, weight, out):
    width = gathered.shape[2]
    core = lax.rem(lax.axis_index("head"), 2)
    total = None
    for part in range(gathered.shape[0]):
        first = pl.multiple_of((part * 2 + core) * width, width)
        term = dot_last(gathered[part], weight[:, pl.ds(first, width)])
        total = term if total is None else total + term
    out[...] = total


def dscore_of(signed, grad_prob, row_dot):
    scaled = jnp.where(signed > 0.0, grad_prob * keep_scale, 0.0)
    return bf16(jnp.abs(signed) * (scaled - row_dot))


def dropped_of(signed):
    return bf16(jnp.maximum(signed, 0.0) * keep_scale)


def own_kernel(signed, message, grad, key_win, value_win, grad_query, key_part, value_part):
    for head in range(HEADS):
        cols = pl.ds(head * DH, DH)
        grad_head = grad[:, cols]
        attended = message[:, WIDE + head * DH : WIDE + (head + 1) * DH]
        row_dot = jnp.sum(f32(grad_head) * f32(attended), axis=1, keepdims=True)
        grad_prob = dot_last(grad_head, value_win[:, cols])
        probs = signed[head]
        dscore = dscore_of(probs, grad_prob, row_dot)
        grad_query[:, cols] = bf16(dot(dscore, key_win[:, cols]) * score_scale)
        key_part[:, cols] = dot_first(dscore[:, FAR:], message[:, cols])
        value_part[:, cols] = dot_first(dropped_of(probs[:, FAR:]), grad_head)


def finish_kernel(
    signed, key, value, near, far, grad_near, grad_far, key_part, value_part, grad_key, grad_value
):
    for head in range(HEADS):
        cols = pl.ds(head * DH, DH)
        key_sum = key_part[:, cols]
        value_sum = value_part[:, cols]
        for source, grads, first, count in ((near, grad_near, 0, ROWS), (far, grad_far, ROWS, MB)):
            grad_head = grads[:, cols]
            attended = source[:, WIDE + head * DH : WIDE + (head + 1) * DH]
            row_dot = jnp.sum(f32(grad_head) * f32(attended), axis=1, keepdims=True)
            grad_prob = dot_last(grad_head, value[:, cols])
            probs = signed[head, first : first + count]
            dscore = dscore_of(probs, grad_prob, row_dot)
            key_sum = key_sum + dot_first(dscore, source[:, cols])
            value_sum = value_sum + dot_first(dropped_of(probs), grad_head)
        grad_key[:, cols] = bf16(key_sum * score_scale)
        grad_value[:, cols] = bf16(value_sum)


def call(kernel, specs, outs, flops, *args):
    shapes = [jax.ShapeDtypeStruct(shape, dtype) for shape, dtype in outs]
    moved = sum(a.size * a.dtype.itemsize for a in args)
    moved += sum(s.size * s.dtype.itemsize for s in shapes)
    return pl.pallas_call(
        kernel,
        out_shape=shapes,
        in_specs=specs,
        out_specs=[VMEM] * len(shapes),
        compiler_params=pltpu.CompilerParams(vmem_limit_bytes=32 << 20),
        cost_estimate=pl.CostEstimate(flops=flops, bytes_accessed=moved, transcendentals=0),
    )(*args)


def shifted(value, steps):
    count = lax.axis_size("blk")
    pairs = [(source, source + steps) for source in range(count) if 0 <= source + steps < count]
    return lax.ppermute(value, "blk", pairs)


def other_core(value):
    count = lax.axis_size("head")
    return lax.ppermute(value, "head", [(source, source ^ 1) for source in range(count)])


def on_device(query_rows, key_rows, value_rows, grad_out, out_weight, mask_types, drop_seed):
    half, full = jnp.bfloat16, jnp.float32
    count = lax.axis_size("head")
    core = lax.rem(lax.axis_index("head"), 2)
    groups = [list(range(first, count, 2)) for first in range(2)]
    gathered = lax.all_gather(grad_out, "head", axis=0, axis_index_groups=groups)
    width = grad_out.shape[1]
    far_keys = shifted(jnp.concatenate((key_rows[MB:], value_rows[MB:])), 2)
    near_keys = shifted(jnp.concatenate((key_rows, value_rows)), 1)
    by_part = out_weight.reshape(WIDE, count // 2, 2, width)
    theirs = lax.dynamic_index_in_dim(by_part, 1 - core, 2, keepdims=False)
    other_weight = other_core(theirs.reshape(WIDE, (count // 2) * width))
    tile = 2 * MB * MB * DH
    signed, message, key_win, value_win = call(
        forward_kernel,
        [SMEM, SMEM] + [VMEM] * 5,
        [
            ((HEADS, ROWS, WIN), full),
            ((ROWS, 2 * WIDE + MB), half),
            ((WIN, WIDE), half),
            ((WIN, WIDE), half),
        ],
        40 * tile,
        mask_types, drop_seed, query_rows, key_rows, value_rows, near_keys, far_keys,
    )
    far_message = shifted(message[:MB], -2)
    near_message = shifted(message, -1)
    (later,) = call(
        later_kernel,
        [SMEM, SMEM] + [VMEM] * 3,
        [((HEADS, FAR, ROWS), full)],
        24 * tile,
        mask_types, drop_seed, key_rows, near_message, far_message,
    )
    flops = 2 * ROWS * WIDE * width * (count // 2)
    shape = [((ROWS, WIDE), full)]
    (sent,) = call(project_other_kernel, [VMEM] * 2, shape, flops, gathered, other_weight)
    received = other_core(sent)
    (own,) = call(project_own_kernel, [VMEM] * 2, shape, flops, gathered, out_weight)
    grad_attn = (own + received).astype(half)
    grad_far = shifted(grad_attn[:MB], -2)
    grad_near = shifted(grad_attn, -1)
    grad_query, key_part, value_part = call(
        own_kernel,
        [VMEM] * 5,
        [((ROWS, WIDE), half), ((ROWS, WIDE), full), ((ROWS, WIDE), full)],
        80 * tile,
        signed, message, grad_attn, key_win, value_win,
    )
    grad_key, grad_value = call(
        finish_kernel,
        [VMEM] * 9,
        [((ROWS, WIDE), half), ((ROWS, WIDE), half)],
        40 * tile,
        later, key_rows, value_rows, near_message, far_message, grad_near, grad_far,
        key_part, value_part,
    )
    return (grad_query, grad_key, grad_value)


def solution(mesh):
    split = P("blk", "head")
    return jax.shard_map(
        on_device,
        mesh=mesh,
        in_specs=(split, split, split, split, P("head", None), P(), P()),
        out_specs=(split, split, split),
        check_vma=False,
    )
```

```python
import jax
import jax.numpy as jnp
from jax import lax
from jax.experimental import pallas as pl
from jax.experimental.pallas import tpu as pltpu
from jax.sharding import PartitionSpec as P

DH = 128
MB = 128
HEADS = 2
ROWS = 256
SLOTS = 5
WIN = SLOTS * MB
FAR = 3 * MB
WIDE = HEADS * DH

drop_level = 6554
keep_scale = 65536.0 / 58982.0
mix_one = 73244475
mix_two = 295559667
mix_three = 668265263
score_scale = DH**-0.5
hidden = -1e30

VMEM = pl.BlockSpec(memory_space=pltpu.VMEM)
SMEM = pl.BlockSpec(memory_space=pltpu.SMEM)


def bf16(value):
    return value.astype(jnp.bfloat16)


def f32(value):
    return value.astype(jnp.float32)


def dot_last(left, right):
    return lax.dot_general(
        left, right, (((1,), (1,)), ((), ())), preferred_element_type=jnp.float32
    )


def dot_first(left, right):
    return lax.dot_general(
        left, right, (((0,), (0,)), ((), ())), preferred_element_type=jnp.float32
    )


def dot(left, right):
    return jnp.dot(left, right, preferred_element_type=jnp.float32)


def bound_of(table, query_block, key_block):
    last = table.shape[0] - 1
    inside = (key_block >= 0) & (query_block <= last)
    kind = table[jnp.minimum(query_block, last), jnp.maximum(key_block, 0)]
    far = jnp.int32(1 << 20)
    bound = jnp.where(kind == 2, far, jnp.where(kind == 1, (query_block - key_block) * MB, -far))
    return jnp.where(inside, bound, -far)


def kept(seed, head, query_block, key_block):
    base = query_block * MB * mix_one + key_block * MB * mix_two + head * mix_three + seed
    rows = lax.broadcasted_iota(jnp.int32, (MB, MB), 0) * mix_one
    cols = lax.broadcasted_iota(jnp.int32, (MB, MB), 1) * mix_two
    hashed = (rows + cols) + base
    for _ in range(2):
        hashed = hashed ^ lax.shift_right_logical(hashed, jnp.int32(16))
        hashed = hashed * mix_one
    hashed = hashed ^ lax.shift_right_logical(hashed, jnp.int32(16))
    return (hashed & 65535) >= drop_level


def column_minus_row():
    return lax.broadcasted_iota(jnp.int32, (MB, MB), 1) - lax.broadcasted_iota(
        jnp.int32, (MB, MB), 0
    )


def forward_kernel(
    table, seed, query, key, value, near, far, signed, message, key_win, value_win
):
    shard = lax.axis_index("blk")
    first_head = lax.axis_index("head") * HEADS
    key_win[0:MB] = far[0:MB]
    key_win[MB:FAR] = near[0:ROWS]
    key_win[FAR:] = key[...]
    value_win[0:MB] = far[MB:]
    value_win[MB:FAR] = near[ROWS:]
    value_win[FAR:] = value[...]
    message[:, 0:WIDE] = query[...]
    ahead = column_minus_row()
    lane = lax.broadcasted_iota(jnp.int32, (MB, MB), 1)
    for block in range(2):
        rows = pl.ds(block * MB, MB)
        query_block = shard * 2 + block
        stats = jnp.zeros((MB, MB), jnp.float32)
        for head in range(HEADS):
            cols = pl.ds(head * DH, DH)
            scores = dot_last(query[rows, cols], key_win[:, cols])
            tiles = []
            for slot in range(block, SLOTS):
                bound = bound_of(table, query_block, shard * 2 - 3 + slot)
                tile = scores[:, slot * MB : (slot + 1) * MB] * score_scale
                tiles.append(jnp.where(ahead <= bound, tile, hidden))
            top = tiles[0]
            for tile in tiles[1:]:
                top = jnp.maximum(top, tile)
            top = jnp.max(top, axis=1, keepdims=True)
            tiles = [jnp.exp(tile - top) for tile in tiles]
            total = tiles[0]
            for tile in tiles[1:]:
                total = total + tile
            total = jnp.sum(total, axis=1, keepdims=True)
            inverse = 1.0 / total
            log_total = top + jnp.log(total)
            drops = []
            for slot in range(block, SLOTS):
                prob = tiles[slot - block] * inverse
                keep = kept(seed[0], first_head + head, query_block, shard * 2 - 3 + slot)
                signed[head, rows, slot * MB : (slot + 1) * MB] = jnp.where(keep, prob, -prob)
                drops.append(bf16(jnp.where(keep, prob * keep_scale, 0.0)))
            if block > 0:
                signed[head, rows, 0:MB] = jnp.zeros((MB, MB), jnp.float32)
            attended = dot(jnp.concatenate(drops, axis=1), value_win[block * MB :, cols])
            message[rows, WIDE + head * DH : WIDE + (head + 1) * DH] = bf16(attended)
            rest = log_total
            for part in range(3):
                piece = f32(bf16(rest))
                stats = jnp.where(lane == head * 3 + part, piece, stats)
                rest = rest - piece
        message[rows, 2 * WIDE :] = bf16(stats)


def later_kernel(table, seed, key, near, far, signed):
    shard = lax.axis_index("blk")
    first_head = lax.axis_index("head") * HEADS
    ahead = column_minus_row()
    for block in range(3):
        source, first = (near, block * MB) if block < 2 else (far, 0)
        query_block = shard * 2 + 2 + block
        for head in range(HEADS):
            cols = pl.ds(head * DH, DH)
            scores = dot_last(source[first : first + MB, cols], key[:, cols]) * score_scale
            stats = f32(source[first : first + MB, 2 * WIDE :])
            log_total = stats[:, 3 * head : 3 * head + 1]
            log_total = log_total + stats[:, 3 * head + 1 : 3 * head + 2]
            log_total = log_total + stats[:, 3 * head + 2 : 3 * head + 3]
            for slot in range(2):
                bound = bound_of(table, query_block, shard * 2 + slot)
                tile = scores[:, slot * MB : (slot + 1) * MB] - log_total
                prob = jnp.exp(jnp.where(ahead <= bound, tile, hidden))
                keep = kept(seed[0], first_head + head, query_block, shard * 2 + slot)
                signed[head, block * MB : (block + 1) * MB, slot * MB : (slot + 1) * MB] = (
                    jnp.where(keep, prob, -prob)
                )


def cut_kernel(weight, out):
    core = lax.rem(lax.axis_index("head"), 2)
    parts = lax.axis_size("head") // 2
    width = out.shape[1] // parts
    for part in range(parts):
        first = pl.multiple_of((part * 2 + 1 - core) * width, width)
        out[:, part * width : (part + 1) * width] = weight[:, pl.ds(first, width)]


def project_other_kernel(gathered, weight, out):
    width = gathered.shape[2]
    total = dot_last(gathered[0], weight[:, 0:width])
    for part in range(1, gathered.shape[0]):
        total = total + dot_last(gathered[part], weight[:, part * width : (part + 1) * width])
    out[...] = total


def project_own_kernel(gathered, weight, out):
    width = gathered.shape[2]
    core = lax.rem(lax.axis_index("head"), 2)
    total = None
    for part in range(gathered.shape[0]):
        first = pl.multiple_of((part * 2 + core) * width, width)
        term = dot_last(gathered[part], weight[:, pl.ds(first, width)])
        total = term if total is None else total + term
    out[...] = total


def dscore_of(signed, grad_prob, row_dot):
    scaled = jnp.where(signed > 0.0, grad_prob * keep_scale, 0.0)
    return bf16(jnp.abs(signed) * (scaled - row_dot))


def dropped_of(signed):
    return bf16(jnp.maximum(signed, 0.0) * keep_scale)


def own_kernel(signed, message, grad, key_win, value_win, grad_query, key_part, value_part):
    for head in range(HEADS):
        cols = pl.ds(head * DH, DH)
        grad_head = grad[:, cols]
        attended = message[:, WIDE + head * DH : WIDE + (head + 1) * DH]
        row_dot = jnp.sum(f32(grad_head) * f32(attended), axis=1, keepdims=True)
        grad_prob = dot_last(grad_head, value_win[:, cols])
        probs = signed[head]
        dscore = dscore_of(probs, grad_prob, row_dot)
        grad_query[:, cols] = bf16(dot(dscore, key_win[:, cols]) * score_scale)
        key_part[:, cols] = dot_first(dscore[:, FAR:], message[:, cols])
        value_part[:, cols] = dot_first(dropped_of(probs[:, FAR:]), grad_head)


def finish_kernel(
    signed, key, value, near, far, grad_near, grad_far, key_part, value_part, grad_key, grad_value
):
    for head in range(HEADS):
        cols = pl.ds(head * DH, DH)
        key_sum = key_part[:, cols]
        value_sum = value_part[:, cols]
        for source, grads, first, count in ((near, grad_near, 0, ROWS), (far, grad_far, ROWS, MB)):
            grad_head = grads[:, cols]
            attended = source[:, WIDE + head * DH : WIDE + (head + 1) * DH]
            row_dot = jnp.sum(f32(grad_head) * f32(attended), axis=1, keepdims=True)
            grad_prob = dot_last(grad_head, value[:, cols])
            probs = signed[head, first : first + count]
            dscore = dscore_of(probs, grad_prob, row_dot)
            key_sum = key_sum + dot_first(dscore, source[:, cols])
            value_sum = value_sum + dot_first(dropped_of(probs), grad_head)
        grad_key[:, cols] = bf16(key_sum * score_scale)
        grad_value[:, cols] = bf16(value_sum)


def call(kernel, specs, outs, flops, *args):
    shapes = [jax.ShapeDtypeStruct(shape, dtype) for shape, dtype in outs]
    moved = sum(a.size * a.dtype.itemsize for a in args)
    moved += sum(s.size * s.dtype.itemsize for s in shapes)
    return pl.pallas_call(
        kernel,
        out_shape=shapes,
        in_specs=specs,
        out_specs=[VMEM] * len(shapes),
        compiler_params=pltpu.CompilerParams(vmem_limit_bytes=16 << 20),
        cost_estimate=pl.CostEstimate(flops=flops, bytes_accessed=moved, transcendentals=0),
    )(*args)


def shifted(value, steps):
    count = lax.axis_size("blk")
    pairs = [(source, source + steps) for source in range(count) if 0 <= source + steps < count]
    return lax.ppermute(value, "blk", pairs)


def other_core(value):
    count = lax.axis_size("head")
    return lax.ppermute(value, "head", [(source, source ^ 1) for source in range(count)])


def on_device(query_rows, key_rows, value_rows, grad_out, out_weight, mask_types, drop_seed):
    half, full = jnp.bfloat16, jnp.float32
    count = lax.axis_size("head")
    groups = [list(range(first, count, 2)) for first in range(2)]
    gathered = lax.all_gather(grad_out, "head", axis=0, axis_index_groups=groups)
    width = grad_out.shape[1]
    near_keys = shifted(jnp.concatenate((key_rows, value_rows)), 1)
    far_keys = shifted(jnp.concatenate((key_rows[MB:], value_rows[MB:])), 2)
    (theirs,) = call(
        cut_kernel, [VMEM], [((WIDE, (count // 2) * width), half)], 0, out_weight
    )
    tile = 2 * MB * MB * DH
    signed, message, key_win, value_win = call(
        forward_kernel,
        [SMEM, SMEM] + [VMEM] * 5,
        [
            ((HEADS, ROWS, WIN), full),
            ((ROWS, 2 * WIDE + MB), half),
            ((WIN, WIDE), half),
            ((WIN, WIDE), half),
        ],
        40 * tile,
        mask_types, drop_seed, query_rows, key_rows, value_rows, near_keys, far_keys,
    )
    near_message = shifted(message, -1)
    far_message = shifted(message[:MB], -2)
    other_weight = other_core(theirs)
    gathered, near_message, far_message = lax.optimization_barrier(
        (gathered, near_message, far_message)
    )
    (later,) = call(
        later_kernel,
        [SMEM, SMEM] + [VMEM] * 3,
        [((HEADS, FAR, ROWS), full)],
        24 * tile,
        mask_types, drop_seed, key_rows, near_message, far_message,
    )
    flops = 2 * ROWS * WIDE * width * (count // 2)
    shape = [((ROWS, WIDE), full)]
    (sent,) = call(project_other_kernel, [VMEM] * 2, shape, flops, gathered, other_weight)
    received = other_core(sent)
    (own,) = call(project_own_kernel, [VMEM] * 2, shape, flops, gathered, out_weight)
    grad_attn = (own + received).astype(half)
    grad_far = shifted(grad_attn[:MB], -2)
    grad_near = shifted(grad_attn, -1)
    grad_query, key_part, value_part = call(
        own_kernel,
        [VMEM] * 5,
        [((ROWS, WIDE), half), ((ROWS, WIDE), full), ((ROWS, WIDE), full)],
        80 * tile,
        signed, message, grad_attn, key_win, value_win,
    )
    grad_key, grad_value = call(
        finish_kernel,
        [VMEM] * 9,
        [((ROWS, WIDE), half), ((ROWS, WIDE), half)],
        40 * tile,
        later, key_rows, value_rows, near_message, far_message, grad_near, grad_far,
        key_part, value_part,
    )
    return (grad_query, grad_key, grad_value)


def solution(mesh):
    split = P("blk", "head")
    return jax.shard_map(
        on_device,
        mesh=mesh,
        in_specs=(split, split, split, split, P("head", None), P(), P()),
        out_specs=(split, split, split),
        check_vma=False,
    )
```

```python
import jax
import jax.numpy as jnp
from jax import lax
from jax.experimental import pallas as pl
from jax.experimental.pallas import tpu as pltpu
from jax.sharding import PartitionSpec as P

DH = 128
MB = 128
HEADS = 2
ROWS = 256
SLOTS = 5
WIN = SLOTS * MB
FAR = 3 * MB
WIDE = HEADS * DH
EXTRA = 16

drop_level = 6554
keep_scale = 65536.0 / 58982.0
mix_one = 73244475
mix_two = 295559667
mix_three = 668265263
score_scale = DH**-0.5
hidden = -1e30

VMEM = pl.BlockSpec(memory_space=pltpu.VMEM)
HBM = pl.BlockSpec(memory_space=pltpu.MemorySpace.HBM)
SMEM = pl.BlockSpec(memory_space=pltpu.SMEM)


def bf16(value):
    return value.astype(jnp.bfloat16)


def f32(value):
    return value.astype(jnp.float32)


def dot_last(left, right):
    return lax.dot_general(
        left, right, (((1,), (1,)), ((), ())), preferred_element_type=jnp.float32
    )


def dot_first(left, right):
    return lax.dot_general(
        left, right, (((0,), (0,)), ((), ())), preferred_element_type=jnp.float32
    )


def dot(left, right):
    return jnp.dot(left, right, preferred_element_type=jnp.float32)


def bound_of(table, query_block, key_block):
    last = table.shape[0] - 1
    inside = (key_block >= 0) & (query_block <= last)
    kind = table[jnp.minimum(query_block, last), jnp.maximum(key_block, 0)]
    far = jnp.int32(1 << 20)
    bound = jnp.where(kind == 2, far, jnp.where(kind == 1, (query_block - key_block) * MB, -far))
    return jnp.where(inside, bound, -far)


def kept(seed, head, query_block, key_block, query_axis):
    base = query_block * MB * mix_one + key_block * MB * mix_two + head * mix_three + seed
    rows = lax.broadcasted_iota(jnp.int32, (MB, MB), query_axis) * mix_one
    cols = lax.broadcasted_iota(jnp.int32, (MB, MB), 1 - query_axis) * mix_two
    hashed = (rows + cols) + base
    for _ in range(2):
        hashed = hashed ^ lax.shift_right_logical(hashed, jnp.int32(16))
        hashed = hashed * mix_one
    hashed = hashed ^ lax.shift_right_logical(hashed, jnp.int32(16))
    return (hashed & 65535) >= drop_level


def key_minus_query(query_axis):
    return lax.broadcasted_iota(jnp.int32, (MB, MB), 1 - query_axis) - lax.broadcasted_iota(
        jnp.int32, (MB, MB), query_axis
    )


def put_parts(stats, lane, first, column):
    rest = column
    for part in range(3):
        piece = f32(bf16(rest))
        stats = jnp.where(lane == first + part, piece, stats)
        rest = rest - piece
    return stats


def take_parts(stats, first):
    return stats[first : first + 1] + stats[first + 1 : first + 2] + stats[first + 2 : first + 3]


def forward_kernel(
    table, seed, query, key, value, near, far, signed, attended, stats, key_win, value_win
):
    shard = lax.axis_index("blk")
    first_head = lax.axis_index("head") * HEADS
    key_win[0:MB] = far[0:MB]
    key_win[MB:FAR] = near[0:ROWS]
    key_win[FAR:] = key[...]
    value_win[0:MB] = far[MB:]
    value_win[MB:FAR] = near[ROWS:]
    value_win[FAR:] = value[...]
    ahead = key_minus_query(0)
    lane = lax.broadcasted_iota(jnp.int32, (MB, MB), 1)
    for block in range(2):
        rows = pl.ds(block * MB, MB)
        query_block = shard * 2 + block
        parts = jnp.zeros((MB, MB), jnp.float32)
        for head in range(HEADS):
            cols = pl.ds(head * DH, DH)
            scores = dot_last(query[rows, cols], key_win[:, cols])
            tiles = []
            for slot in range(block, SLOTS):
                bound = bound_of(table, query_block, shard * 2 - 3 + slot)
                tile = scores[:, slot * MB : (slot + 1) * MB] * score_scale
                tiles.append(jnp.where(ahead <= bound, tile, hidden))
            top = tiles[0]
            for tile in tiles[1:]:
                top = jnp.maximum(top, tile)
            top = jnp.max(top, axis=1, keepdims=True)
            tiles = [jnp.exp(tile - top) for tile in tiles]
            total = tiles[0]
            for tile in tiles[1:]:
                total = total + tile
            total = jnp.sum(total, axis=1, keepdims=True)
            inverse = 1.0 / total
            log_total = top + jnp.log(total)
            drops = []
            for slot in range(block, SLOTS):
                prob = tiles[slot - block] * inverse
                keep = kept(seed[0], first_head + head, query_block, shard * 2 - 3 + slot, 0)
                signed[head, rows, slot * MB : (slot + 1) * MB] = jnp.where(keep, prob, -prob)
                drops.append(bf16(jnp.where(keep, prob * keep_scale, 0.0)))
            if block > 0:
                signed[head, rows, 0:MB] = jnp.zeros((MB, MB), jnp.float32)
            mixed = dot(jnp.concatenate(drops, axis=1), value_win[block * MB :, cols])
            attended[rows, cols] = bf16(mixed)
            parts = put_parts(parts, lane, 3 * head, log_total)
        stats[rows] = parts


def later_kernel(table, seed, key, near, far, scores, keeps):
    shard = lax.axis_index("blk")
    first_head = lax.axis_index("head") * HEADS
    ahead = key_minus_query(1)
    for block in range(3):
        source, first = (near, block * MB) if block < 2 else (far, 0)
        across = slice(block * MB, (block + 1) * MB)
        query_block = shard * 2 + 2 + block
        for head in range(HEADS):
            cols = pl.ds(head * DH, DH)
            tiles = dot_last(key[:, cols], source[first : first + MB, cols]) * score_scale
            for slot in range(2):
                down = slice(slot * MB, (slot + 1) * MB)
                bound = bound_of(table, query_block, shard * 2 + slot)
                scores[head, down, across] = jnp.where(ahead <= bound, tiles[down], hidden)
                keep = kept(seed[0], first_head + head, query_block, shard * 2 + slot, 1)
                keeps[head, down, across] = jnp.where(keep, jnp.float32(keep_scale), 0.0)


def cut_kernel(weight, out):
    core = lax.rem(lax.axis_index("head"), 2)
    parts = lax.axis_size("head") // 2
    width = out.shape[1] // parts
    for part in range(parts):
        first = pl.multiple_of((part * 2 + 1 - core) * width, width)
        out[:, part * width : (part + 1) * width] = weight[:, pl.ds(first, width)]


def project_other_kernel(gathered, weight, out, held, theirs, sems, weight_sem):
    parts, _, width = gathered.shape
    copies = [
        pltpu.make_async_copy(gathered.at[part], held.at[part], sems.at[part])
        for part in range(parts)
    ]
    whole = pltpu.make_async_copy(weight, theirs, weight_sem)
    whole.start()
    for copy in copies:
        copy.start()
    whole.wait()
    total = None
    for part in range(parts):
        copies[part].wait()
        term = dot_last(held[part], theirs[:, part * width : (part + 1) * width])
        total = term if total is None else total + term
    out[...] = total


def project_own_kernel(gathered, weight, out):
    parts, _, width = gathered.shape
    core = lax.rem(lax.axis_index("head"), 2)
    total = None
    for part in range(parts):
        first = pl.multiple_of((part * 2 + core) * width, width)
        term = dot_last(gathered[part], weight[:, pl.ds(first, width)])
        total = term if total is None else total + term
    out[...] = total


def rows_kernel(own, received, attended, stats, near, far):
    grad = bf16(own[...] + received[...])
    near[0:ROWS] = grad
    far[0:MB] = grad[0:MB]
    lane = lax.broadcasted_iota(jnp.int32, (MB, MB), 1)
    for block in range(2):
        rows = slice(block * MB, (block + 1) * MB)
        parts = stats[rows]
        for head in range(HEADS):
            cols = slice(head * DH, (head + 1) * DH)
            row_dot = jnp.sum(
                f32(grad[rows, cols]) * f32(attended[rows, cols]), axis=1, keepdims=True
            )
            parts = put_parts(parts, lane, 6 + 3 * head, row_dot)
        across = bf16(parts.T[0:EXTRA])
        near[ROWS:, rows] = across
        far[MB:, rows] = across


def own_kernel(
    signed, attended, query, grad, key_win, value_win, grad_query, key_part, value_part
):
    for head in range(HEADS):
        cols = pl.ds(head * DH, DH)
        grad_head = grad[0:ROWS, cols]
        row_dot = jnp.sum(f32(grad_head) * f32(attended[:, cols]), axis=1, keepdims=True)
        grad_prob = dot_last(grad_head, value_win[:, cols])
        probs = signed[head]
        scaled = jnp.where(probs > 0.0, grad_prob * keep_scale, 0.0)
        dscore = bf16(jnp.abs(probs) * (scaled - row_dot))
        dropped = bf16(jnp.maximum(probs[:, FAR:], 0.0) * keep_scale)
        grad_query[:, cols] = bf16(dot(dscore, key_win[:, cols]) * score_scale)
        key_part[:, cols] = dot_first(dscore[:, FAR:], query[:, cols])
        value_part[:, cols] = dot_first(dropped, grad_head)


def finish_kernel(
    scores, keeps, value, near_query, far_query, near_grad, far_grad, key_part, value_part,
    grad_key, grad_value,
):
    for head in range(HEADS):
        cols = pl.ds(head * DH, DH)
        key_sum = key_part[:, cols]
        value_sum = value_part[:, cols]
        for queries, grads, first, count in (
            (near_query, near_grad, 0, ROWS), (far_query, far_grad, ROWS, MB)
        ):
            across = slice(first, first + count)
            grad_head = grads[0:count, cols]
            stats = f32(grads[count:, 0:count])
            prob = jnp.exp(scores[head, :, across] - take_parts(stats, 3 * head))
            keep = keeps[head, :, across]
            grad_prob = dot_last(value[:, cols], grad_head)
            dscore = bf16(prob * (grad_prob * keep - take_parts(stats, 6 + 3 * head)))
            key_sum = key_sum + dot(dscore, queries[:, cols])
            value_sum = value_sum + dot(bf16(prob * keep), grad_head)
        grad_key[:, cols] = bf16(key_sum * score_scale)
        grad_value[:, cols] = bf16(value_sum)


def call(kernel, specs, outs, flops, *args, scratch=(), grant=16):
    shapes = [jax.ShapeDtypeStruct(shape, dtype) for shape, dtype in outs]
    moved = sum(a.size * a.dtype.itemsize for a in args)
    moved += sum(s.size * s.dtype.itemsize for s in shapes)
    return pl.pallas_call(
        kernel,
        out_shape=shapes,
        in_specs=specs,
        out_specs=[VMEM] * len(shapes),
        scratch_shapes=scratch,
        compiler_params=pltpu.CompilerParams(vmem_limit_bytes=grant << 20),
        cost_estimate=pl.CostEstimate(flops=flops, bytes_accessed=moved, transcendentals=0),
    )(*args)


def shifted(value, steps):
    count = lax.axis_size("blk")
    pairs = [(source, source + steps) for source in range(count) if 0 <= source + steps < count]
    return lax.ppermute(value, "blk", pairs)


def other_core(value):
    count = lax.axis_size("head")
    return lax.ppermute(value, "head", [(source, source ^ 1) for source in range(count)])


def on_device(query_rows, key_rows, value_rows, grad_out, out_weight, mask_types, drop_seed):
    half, full = jnp.bfloat16, jnp.float32
    count = lax.axis_size("head")
    parts, width = count // 2, grad_out.shape[1]
    groups = [list(range(first, count, 2)) for first in range(2)]
    gathered = lax.all_gather(grad_out, "head", axis=0, axis_index_groups=groups)
    near_keys = shifted(jnp.concatenate((key_rows, value_rows)), 1)
    far_keys = shifted(jnp.concatenate((key_rows[MB:], value_rows[MB:])), 2)
    near_query = shifted(query_rows, -1)
    far_query = shifted(query_rows[:MB], -2)
    (theirs,) = call(cut_kernel, [VMEM], [((WIDE, parts * width), half)], 0, out_weight)
    other_weight = other_core(theirs)
    tile = 2 * MB * MB * DH
    signed, attended, stats, key_win, value_win = call(
        forward_kernel,
        [SMEM, SMEM] + [VMEM] * 5,
        [
            ((HEADS, ROWS, WIN), full),
            ((ROWS, WIDE), half),
            ((ROWS, MB), full),
            ((WIN, WIDE), half),
            ((WIN, WIDE), half),
        ],
        40 * tile,
        mask_types, drop_seed, query_rows, key_rows, value_rows, near_keys, far_keys,
    )
    scores, keeps = call(
        later_kernel,
        [SMEM, SMEM] + [VMEM] * 3,
        [((HEADS, ROWS, FAR), full), ((HEADS, ROWS, FAR), full)],
        24 * tile,
        mask_types, drop_seed, key_rows, near_query, far_query,
    )
    gathered, attended, scores = lax.optimization_barrier((gathered, attended, scores))
    flops = 2 * ROWS * WIDE * width * parts
    (sent,) = call(
        project_other_kernel,
        [HBM] * 2,
        [((ROWS, WIDE), full)],
        flops,
        gathered, other_weight,
        scratch=[
            pltpu.VMEM((parts, ROWS, width), half),
            pltpu.VMEM((WIDE, parts * width), half),
            pltpu.SemaphoreType.DMA((parts,)),
            pltpu.SemaphoreType.DMA,
        ],
        grant=56,
    )
    received = other_core(sent)
    (own,) = call(
        project_own_kernel, [VMEM] * 2, [((ROWS, WIDE), full)], flops, gathered, out_weight
    )
    near_rows, far_rows = call(
        rows_kernel,
        [VMEM] * 4,
        [((ROWS + EXTRA, WIDE), half), ((MB + EXTRA, WIDE), half)],
        0,
        own, received, attended, stats,
    )
    near_grad = shifted(near_rows, -1)
    far_grad = shifted(far_rows, -2)
    grad_query, key_part, value_part = call(
        own_kernel,
        [VMEM] * 6,
        [((ROWS, WIDE), half), ((ROWS, WIDE), full), ((ROWS, WIDE), full)],
        80 * tile,
        signed, attended, query_rows, near_rows, key_win, value_win,
    )
    grad_key, grad_value = call(
        finish_kernel,
        [VMEM] * 9,
        [((ROWS, WIDE), half), ((ROWS, WIDE), half)],
        40 * tile,
        scores, keeps, value_rows, near_query, far_query, near_grad, far_grad, key_part, value_part,
    )
    return (grad_query, grad_key, grad_value)


def solution(mesh):
    split = P("blk", "head")
    return jax.shard_map(
        on_device,
        mesh=mesh,
        in_specs=(split, split, split, split, P("head", None), P(), P()),
        out_specs=(split, split, split),
        check_vma=False,
    )
```

```python
import jax
import jax.numpy as jnp
from jax import lax
from jax.experimental import pallas as pl
from jax.experimental.pallas import tpu as pltpu
from jax.sharding import PartitionSpec as P

DH = 128
MB = 128
HEADS = 2
ROWS = 256
SLOTS = 5
WIN = SLOTS * MB
FAR = 3 * MB
WIDE = HEADS * DH
EXTRA = 16

drop_level = 6554
keep_scale = 65536.0 / 58982.0
mix_one = 73244475
mix_two = 295559667
mix_three = 668265263
score_scale = DH**-0.5
hidden = -1e30

VMEM = pl.BlockSpec(memory_space=pltpu.VMEM)
SMEM = pl.BlockSpec(memory_space=pltpu.SMEM)


def bf16(value):
    return value.astype(jnp.bfloat16)


def f32(value):
    return value.astype(jnp.float32)


def dot_last(left, right):
    return lax.dot_general(
        left, right, (((1,), (1,)), ((), ())), preferred_element_type=jnp.float32
    )


def dot_first(left, right):
    return lax.dot_general(
        left, right, (((0,), (0,)), ((), ())), preferred_element_type=jnp.float32
    )


def dot(left, right):
    return jnp.dot(left, right, preferred_element_type=jnp.float32)


def bound_of(table, query_block, key_block):
    last = table.shape[0] - 1
    inside = (key_block >= 0) & (query_block <= last)
    kind = table[jnp.minimum(query_block, last), jnp.maximum(key_block, 0)]
    far = jnp.int32(1 << 20)
    bound = jnp.where(kind == 2, far, jnp.where(kind == 1, (query_block - key_block) * MB, -far))
    return jnp.where(inside, bound, -far)


def kept(seed, head, query_block, key_block, query_axis):
    base = query_block * MB * mix_one + key_block * MB * mix_two + head * mix_three + seed
    rows = lax.broadcasted_iota(jnp.int32, (MB, MB), query_axis) * mix_one
    cols = lax.broadcasted_iota(jnp.int32, (MB, MB), 1 - query_axis) * mix_two
    hashed = (rows + cols) + base
    for _ in range(2):
        hashed = hashed ^ lax.shift_right_logical(hashed, jnp.int32(16))
        hashed = hashed * mix_one
    hashed = hashed ^ lax.shift_right_logical(hashed, jnp.int32(16))
    return (hashed & 65535) >= drop_level


def key_minus_query(query_axis):
    return lax.broadcasted_iota(jnp.int32, (MB, MB), 1 - query_axis) - lax.broadcasted_iota(
        jnp.int32, (MB, MB), query_axis
    )


def put_parts(stats, lane, first, column):
    rest = column
    for part in range(3):
        piece = f32(bf16(rest))
        stats = jnp.where(lane == first + part, piece, stats)
        rest = rest - piece
    return stats


def take_parts(stats, first):
    return stats[first : first + 1] + stats[first + 1 : first + 2] + stats[first + 2 : first + 3]


def forward_kernel(
    table, seed, query, key, value, near, far, signed, attended, stats, key_win, value_win
):
    shard = lax.axis_index("blk")
    first_head = lax.axis_index("head") * HEADS
    key_win[0:MB] = far[0:MB]
    key_win[MB:FAR] = near[0:ROWS]
    key_win[FAR:] = key[...]
    value_win[0:MB] = far[MB:]
    value_win[MB:FAR] = near[ROWS:]
    value_win[FAR:] = value[...]
    ahead = key_minus_query(0)
    lane = lax.broadcasted_iota(jnp.int32, (MB, MB), 1)
    for block in range(2):
        rows = pl.ds(block * MB, MB)
        query_block = shard * 2 + block
        parts = jnp.zeros((MB, MB), jnp.float32)
        for head in range(HEADS):
            cols = pl.ds(head * DH, DH)
            scores = dot_last(query[rows, cols], key_win[:, cols])
            tiles = []
            for slot in range(block, SLOTS):
                bound = bound_of(table, query_block, shard * 2 - 3 + slot)
                tile = scores[:, slot * MB : (slot + 1) * MB] * score_scale
                tiles.append(jnp.where(ahead <= bound, tile, hidden))
            top = tiles[0]
            for tile in tiles[1:]:
                top = jnp.maximum(top, tile)
            top = jnp.max(top, axis=1, keepdims=True)
            tiles = [jnp.exp(tile - top) for tile in tiles]
            total = tiles[0]
            for tile in tiles[1:]:
                total = total + tile
            total = jnp.sum(total, axis=1, keepdims=True)
            inverse = 1.0 / total
            log_total = top + jnp.log(total)
            drops = []
            for slot in range(block, SLOTS):
                prob = tiles[slot - block] * inverse
                keep = kept(seed[0], first_head + head, query_block, shard * 2 - 3 + slot, 0)
                signed[head, rows, slot * MB : (slot + 1) * MB] = jnp.where(keep, prob, -prob)
                drops.append(bf16(jnp.where(keep, prob * keep_scale, 0.0)))
            if block > 0:
                signed[head, rows, 0:MB] = jnp.zeros((MB, MB), jnp.float32)
            mixed = dot(jnp.concatenate(drops, axis=1), value_win[block * MB :, cols])
            attended[rows, cols] = bf16(mixed)
            parts = put_parts(parts, lane, 3 * head, log_total)
        stats[rows] = parts


def later_kernel(table, seed, key, near, far, scores, keeps):
    shard = lax.axis_index("blk")
    first_head = lax.axis_index("head") * HEADS
    ahead = key_minus_query(1)
    for block in range(3):
        source, first = (near, block * MB) if block < 2 else (far, 0)
        across = slice(block * MB, (block + 1) * MB)
        query_block = shard * 2 + 2 + block
        for head in range(HEADS):
            cols = pl.ds(head * DH, DH)
            tiles = dot_last(key[:, cols], source[first : first + MB, cols]) * score_scale
            for slot in range(2):
                down = slice(slot * MB, (slot + 1) * MB)
                bound = bound_of(table, query_block, shard * 2 + slot)
                scores[head, down, across] = jnp.where(ahead <= bound, tiles[down], hidden)
                keep = kept(seed[0], first_head + head, query_block, shard * 2 + slot, 1)
                keeps[head, down, across] = jnp.where(keep, jnp.float32(keep_scale), 0.0)


def project(total, gathered, weight, core):
    parts, _, width = gathered.shape
    for part in range(parts):
        first = pl.multiple_of((part * 2 + core) * width, width)
        term = dot_last(gathered[part], weight[:, pl.ds(first, width)])
        total = term if total is None else total + term
    return total


def project_kernel(top, top_other, low, weight, out):
    core = lax.rem(lax.axis_index("head"), 2)
    out[0:MB] = project(project(None, top, weight, core), top_other, weight, 1 - core)
    out[MB:] = project(None, low, weight, core)


def rows_kernel(partial, low_other, weight, attended, stats, near, far):
    core = lax.rem(lax.axis_index("head"), 2)
    low = project(partial[MB:], low_other, weight, 1 - core)
    lane = lax.broadcasted_iota(jnp.int32, (MB, MB), 1)
    for block, total in ((0, partial[0:MB]), (1, low)):
        rows = slice(block * MB, (block + 1) * MB)
        grad = bf16(total)
        near[rows] = grad
        parts = stats[rows]
        for head in range(HEADS):
            cols = slice(head * DH, (head + 1) * DH)
            row_dot = jnp.sum(f32(grad[:, cols]) * f32(attended[rows, cols]), axis=1, keepdims=True)
            parts = put_parts(parts, lane, 6 + 3 * head, row_dot)
        across = bf16(parts.T[0:EXTRA])
        near[ROWS:, rows] = across
        if block == 0:
            far[0:MB] = grad
        far[MB:, rows] = across


def own_kernel(
    signed, attended, query, grad, key_win, value_win, grad_query, key_part, value_part
):
    for head in range(HEADS):
        cols = pl.ds(head * DH, DH)
        grad_head = grad[0:ROWS, cols]
        row_dot = jnp.sum(f32(grad_head) * f32(attended[:, cols]), axis=1, keepdims=True)
        grad_prob = dot_last(grad_head, value_win[:, cols])
        probs = signed[head]
        scaled = jnp.where(probs > 0.0, grad_prob * keep_scale, 0.0)
        dscore = bf16(jnp.abs(probs) * (scaled - row_dot))
        dropped = bf16(jnp.maximum(probs[:, FAR:], 0.0) * keep_scale)
        grad_query[:, cols] = bf16(dot(dscore, key_win[:, cols]) * score_scale)
        key_part[:, cols] = dot_first(dscore[:, FAR:], query[:, cols])
        value_part[:, cols] = dot_first(dropped, grad_head)


def finish_kernel(
    scores, keeps, value, near_query, far_query, near_grad, far_grad, key_part, value_part,
    grad_key, grad_value,
):
    for head in range(HEADS):
        cols = pl.ds(head * DH, DH)
        key_sum = key_part[:, cols]
        value_sum = value_part[:, cols]
        for queries, grads, first, count in (
            (near_query, near_grad, 0, ROWS), (far_query, far_grad, ROWS, MB)
        ):
            across = slice(first, first + count)
            grad_head = grads[0:count, cols]
            stats = f32(grads[count:, 0:count])
            prob = jnp.exp(scores[head, :, across] - take_parts(stats, 3 * head))
            keep = keeps[head, :, across]
            grad_prob = dot_last(value[:, cols], grad_head)
            dscore = bf16(prob * (grad_prob * keep - take_parts(stats, 6 + 3 * head)))
            key_sum = key_sum + dot(dscore, queries[:, cols])
            value_sum = value_sum + dot(bf16(prob * keep), grad_head)
        grad_key[:, cols] = bf16(key_sum * score_scale)
        grad_value[:, cols] = bf16(value_sum)


def call(kernel, specs, outs, flops, *args):
    shapes = [jax.ShapeDtypeStruct(shape, dtype) for shape, dtype in outs]
    moved = sum(a.size * a.dtype.itemsize for a in args)
    moved += sum(s.size * s.dtype.itemsize for s in shapes)
    return pl.pallas_call(
        kernel,
        out_shape=shapes,
        in_specs=specs,
        out_specs=[VMEM] * len(shapes),
        compiler_params=pltpu.CompilerParams(vmem_limit_bytes=16 << 20),
        cost_estimate=pl.CostEstimate(flops=flops, bytes_accessed=moved, transcendentals=0),
    )(*args)


def shifted(value, steps):
    count = lax.axis_size("blk")
    pairs = [(source, source + steps) for source in range(count) if 0 <= source + steps < count]
    return lax.ppermute(value, "blk", pairs)


def other_core(value):
    count = lax.axis_size("head")
    return lax.ppermute(value, "head", [(source, source ^ 1) for source in range(count)])


def on_device(query_rows, key_rows, value_rows, grad_out, out_weight, mask_types, drop_seed):
    half, full = jnp.bfloat16, jnp.float32
    count = lax.axis_size("head")
    parts, width = count // 2, grad_out.shape[1]
    groups = [list(range(first, count, 2)) for first in range(2)]

    def gather(rows):
        return lax.all_gather(rows, "head", axis=0, axis_index_groups=groups)

    near_keys = shifted(jnp.concatenate((key_rows, value_rows)), 1)
    far_keys = shifted(jnp.concatenate((key_rows[MB:], value_rows[MB:])), 2)
    near_query = shifted(query_rows, -1)
    far_query = shifted(query_rows[:MB], -2)
    top = gather(grad_out[:MB])
    top_other = other_core(top)
    tile = 2 * MB * MB * DH
    signed, attended, stats, key_win, value_win = call(
        forward_kernel,
        [SMEM, SMEM] + [VMEM] * 5,
        [
            ((HEADS, ROWS, WIN), full),
            ((ROWS, WIDE), half),
            ((ROWS, MB), full),
            ((WIN, WIDE), half),
            ((WIN, WIDE), half),
        ],
        40 * tile,
        mask_types, drop_seed, query_rows, key_rows, value_rows, near_keys, far_keys,
    )
    scores, keeps = call(
        later_kernel,
        [SMEM, SMEM] + [VMEM] * 3,
        [((HEADS, ROWS, FAR), full), ((HEADS, ROWS, FAR), full)],
        24 * tile,
        mask_types, drop_seed, key_rows, near_query, far_query,
    )
    low_rows, attended, scores = lax.optimization_barrier((grad_out[MB:], attended, scores))
    low = gather(low_rows)
    low_other = other_core(low)
    flops = 2 * MB * WIDE * width * parts
    (partial,) = call(
        project_kernel, [VMEM] * 4, [((ROWS, WIDE), full)], 3 * flops,
        top, top_other, low, out_weight,
    )
    near_rows, far_rows = call(
        rows_kernel,
        [VMEM] * 5,
        [((ROWS + EXTRA, WIDE), half), ((MB + EXTRA, WIDE), half)],
        flops,
        partial, low_other, out_weight, attended, stats,
    )
    near_grad = shifted(near_rows, -1)
    far_grad = shifted(far_rows, -2)
    grad_query, key_part, value_part = call(
        own_kernel,
        [VMEM] * 6,
        [((ROWS, WIDE), half), ((ROWS, WIDE), full), ((ROWS, WIDE), full)],
        80 * tile,
        signed, attended, query_rows, near_rows, key_win, value_win,
    )
    grad_key, grad_value = call(
        finish_kernel,
        [VMEM] * 9,
        [((ROWS, WIDE), half), ((ROWS, WIDE), half)],
        40 * tile,
        scores, keeps, value_rows, near_query, far_query, near_grad, far_grad, key_part, value_part,
    )
    return (grad_query, grad_key, grad_value)


def solution(mesh):
    split = P("blk", "head")
    return jax.shard_map(
        on_device,
        mesh=mesh,
        in_specs=(split, split, split, split, P("head", None), P(), P()),
        out_specs=(split, split, split),
        check_vma=False,
    )
```

```python
import functools

import jax
import jax.numpy as jnp
from jax import lax
from jax.experimental import pallas as pl
from jax.experimental.pallas import tpu as pltpu
from jax.sharding import PartitionSpec as P

DH = 128
MB = 128
HEADS = 2
ROWS = 256
SLOTS = 5
WIN = SLOTS * MB
FAR = 3 * MB
WIDE = HEADS * DH
EXTRA = 16

drop_level = 6554
keep_scale = 65536.0 / 58982.0
mix_one = 73244475
mix_two = 295559667
mix_three = 668265263
score_scale = DH**-0.5
hidden = -1e30

VMEM = pl.BlockSpec(memory_space=pltpu.VMEM)
SMEM = pl.BlockSpec(memory_space=pltpu.SMEM)


def bf16(value):
    return value.astype(jnp.bfloat16)


def f32(value):
    return value.astype(jnp.float32)


def dot_last(left, right):
    return lax.dot_general(
        left, right, (((1,), (1,)), ((), ())), preferred_element_type=jnp.float32
    )


def dot_first(left, right):
    return lax.dot_general(
        left, right, (((0,), (0,)), ((), ())), preferred_element_type=jnp.float32
    )


def dot(left, right):
    return jnp.dot(left, right, preferred_element_type=jnp.float32)


def bound_of(table, query_block, key_block):
    last = table.shape[0] - 1
    inside = (key_block >= 0) & (query_block <= last)
    kind = table[jnp.minimum(query_block, last), jnp.maximum(key_block, 0)]
    far = jnp.int32(1 << 20)
    bound = jnp.where(kind == 2, far, jnp.where(kind == 1, (query_block - key_block) * MB, -far))
    return jnp.where(inside, bound, -far)


def kept(seed, head, query_block, key_block, query_axis):
    base = query_block * MB * mix_one + key_block * MB * mix_two + head * mix_three + seed
    rows = lax.broadcasted_iota(jnp.int32, (MB, MB), query_axis) * mix_one
    cols = lax.broadcasted_iota(jnp.int32, (MB, MB), 1 - query_axis) * mix_two
    hashed = (rows + cols) + base
    for _ in range(2):
        hashed = hashed ^ lax.shift_right_logical(hashed, jnp.int32(16))
        hashed = hashed * mix_one
    hashed = hashed ^ lax.shift_right_logical(hashed, jnp.int32(16))
    return (hashed & 65535) >= drop_level


def key_minus_query(query_axis):
    return lax.broadcasted_iota(jnp.int32, (MB, MB), 1 - query_axis) - lax.broadcasted_iota(
        jnp.int32, (MB, MB), query_axis
    )


def put_parts(stats, lane, first, column):
    rest = column
    for part in range(3):
        piece = f32(bf16(rest))
        stats = jnp.where(lane == first + part, piece, stats)
        rest = rest - piece
    return stats


def take_parts(stats, first):
    return stats[first : first + 1] + stats[first + 1 : first + 2] + stats[first + 2 : first + 3]


def forward(table, seed, block, query, keys, values, signed, attended, stats):
    shard = lax.axis_index("blk")
    first_head = lax.axis_index("head") * HEADS
    count = keys(0).shape[0] // MB
    query_block = shard * 2 + block
    first_block = shard * 2 + 2 - count
    ahead = key_minus_query(0)
    lane = lax.broadcasted_iota(jnp.int32, (MB, MB), 1)
    parts = jnp.zeros((MB, MB), jnp.float32)
    for head in range(HEADS):
        cols = pl.ds(head * DH, DH)
        scores = dot_last(query[block * MB : (block + 1) * MB, cols], keys(head))
        tiles = []
        for slot in range(count):
            bound = bound_of(table, query_block, first_block + slot)
            tile = scores[:, slot * MB : (slot + 1) * MB] * score_scale
            tiles.append(jnp.where(ahead <= bound, tile, hidden))
        top = functools.reduce(jnp.maximum, tiles)
        top = jnp.max(top, axis=1, keepdims=True)
        tiles = [jnp.exp(tile - top) for tile in tiles]
        total = jnp.sum(functools.reduce(jnp.add, tiles), axis=1, keepdims=True)
        inverse = 1.0 / total
        drops = []
        for slot in range(count):
            prob = tiles[slot] * inverse
            keep = kept(seed[0], first_head + head, query_block, first_block + slot, 0)
            signed[head, :, slot * MB : (slot + 1) * MB] = jnp.where(keep, prob, -prob)
            drops.append(bf16(jnp.where(keep, prob * keep_scale, 0.0)))
        attended[:, cols] = bf16(dot(jnp.concatenate(drops, axis=1), values(head)))
        parts = put_parts(parts, lane, 3 * head, top + jnp.log(total))
    stats[...] = parts


def later(table, seed, first_query, first_key, queries, keys, scores, keeps):
    first_head = lax.axis_index("head") * HEADS
    ahead = key_minus_query(1)
    for head in range(HEADS):
        cols = pl.ds(head * DH, DH)
        tiles = dot_last(keys[:, cols], queries[:, cols]) * score_scale
        for block in range(queries.shape[0] // MB):
            across = slice(block * MB, (block + 1) * MB)
            for slot in range(keys.shape[0] // MB):
                down = slice(slot * MB, (slot + 1) * MB)
                bound = bound_of(table, first_query + block, first_key + slot)
                scores[head, down, across] = jnp.where(
                    ahead <= bound, tiles[down, across], hidden
                )
                keep = kept(seed[0], first_head + head, first_query + block, first_key + slot, 1)
                keeps[head, down, across] = jnp.where(keep, jnp.float32(keep_scale), 0.0)


def stacked(*parts):
    def of_head(head):
        cols = slice(head * DH, (head + 1) * DH)
        return jnp.concatenate([ref[rows, cols] for ref, rows in parts], axis=0)

    return of_head


def near_window(key, value, near):
    whole = slice(None)
    keys = ((near, slice(0, ROWS)), (key, whole))
    values = ((near, slice(ROWS, None)), (value, whole))
    return keys, values


def far_window(key, value, near, far):
    keys, values = near_window(key, value, near)
    return ((far, slice(0, MB)), *keys), ((far, slice(MB, None)), *values)


def near_kernel(
    table, seed, query, key, value, near, near_query, signed, attended, stats, scores, keeps
):
    keys, values = near_window(key, value, near)
    forward(table, seed, 1, query, stacked(*keys), stacked(*values), signed, attended, stats)
    shard = lax.axis_index("blk")
    later(table, seed, shard * 2 + 2, shard * 2, near_query, key, scores, keeps)


def far_kernel(
    table, seed, query, key, value, near, far, far_query, signed, attended, stats, scores, keeps
):
    keys, values = far_window(key, value, near, far)
    forward(table, seed, 0, query, stacked(*keys), stacked(*values), signed, attended, stats)
    shard = lax.axis_index("blk")
    later(table, seed, shard * 2 + 4, shard * 2 + 1, far_query, key.at[MB:], scores, keeps)


def project(total, gathered, weight, core):
    parts, _, width = gathered.shape
    for part in range(parts):
        first = pl.multiple_of((part * 2 + core) * width, width)
        term = dot_last(gathered[part], weight[:, pl.ds(first, width)])
        total = term if total is None else total + term
    return total


def project_kernel(top, top_other, low, weight, out):
    core = lax.rem(lax.axis_index("head"), 2)
    out[0:MB] = project(project(None, top, weight, core), top_other, weight, 1 - core)
    out[MB:] = project(None, low, weight, core)


def rows_kernel(
    partial, low_other, weight, attended_top, attended_low, stats_top, stats_low, near, far
):
    core = lax.rem(lax.axis_index("head"), 2)
    low = project(partial[MB:], low_other, weight, 1 - core)
    lane = lax.broadcasted_iota(jnp.int32, (MB, MB), 1)
    for block, total, attended, stats in (
        (0, partial[0:MB], attended_top, stats_top), (1, low, attended_low, stats_low)
    ):
        rows = slice(block * MB, (block + 1) * MB)
        grad = bf16(total)
        near[rows] = grad
        parts = stats[...]
        for head in range(HEADS):
            cols = slice(head * DH, (head + 1) * DH)
            row_dot = jnp.sum(f32(grad[:, cols]) * f32(attended[:, cols]), axis=1, keepdims=True)
            parts = put_parts(parts, lane, 6 + 3 * head, row_dot)
        across = bf16(parts.T[0:EXTRA])
        near[ROWS:, rows] = across
        if block == 0:
            far[0:MB] = grad
        far[MB:, rows] = across


def own_kernel(
    signed_top, signed_low, attended_top, attended_low, query, grad, key, value, near, far,
    grad_query, key_part, value_part,
):
    for head in range(HEADS):
        cols = slice(head * DH, (head + 1) * DH)
        key_sum = value_sum = None
        for block, signed, attended, (keys, values) in (
            (0, signed_top, attended_top, far_window(key, value, near, far)),
            (1, signed_low, attended_low, near_window(key, value, near)),
        ):
            rows = slice(block * MB, (block + 1) * MB)
            grad_head = grad[rows, cols]
            row_dot = jnp.sum(f32(grad_head) * f32(attended[:, cols]), axis=1, keepdims=True)
            grad_prob = dot_last(grad_head, stacked(*values)(head))
            probs = signed[head]
            first = probs.shape[1] - ROWS
            scaled = jnp.where(probs > 0.0, grad_prob * keep_scale, 0.0)
            dscore = bf16(jnp.abs(probs) * (scaled - row_dot))
            dropped = bf16(jnp.maximum(probs[:, first:], 0.0) * keep_scale)
            grad_query[rows, cols] = bf16(dot(dscore, stacked(*keys)(head)) * score_scale)
            key_term = dot_first(dscore[:, first:], query[rows, cols])
            value_term = dot_first(dropped, grad_head)
            key_sum = key_term if key_sum is None else key_sum + key_term
            value_sum = value_term if value_sum is None else value_sum + value_term
        key_part[:, cols] = key_sum
        value_part[:, cols] = value_sum


def finish_kernel(
    near_scores, near_keeps, far_scores, far_keeps, value, near_query, far_query, near_grad,
    far_grad, key_part, value_part, grad_key, grad_value,
):
    for head in range(HEADS):
        cols = pl.ds(head * DH, DH)

        def terms(scores, keeps, values, queries, grads):
            count = queries.shape[0]
            grad_head = grads[0:count, cols]
            stats = f32(grads[count:, 0:count])
            prob = jnp.exp(scores[head] - take_parts(stats, 3 * head))
            keep = keeps[head]
            grad_prob = dot_last(values, grad_head)
            dscore = bf16(prob * (grad_prob * keep - take_parts(stats, 6 + 3 * head)))
            return dot(dscore, queries[:, cols]), dot(bf16(prob * keep), grad_head)

        keys, values = terms(near_scores, near_keeps, value[:, cols], near_query, near_grad)
        far_keys, far_values = terms(far_scores, far_keeps, value[MB:, cols], far_query, far_grad)
        keys = keys + key_part[:, cols]
        values = values + value_part[:, cols]
        grad_key[0:MB, cols] = bf16(keys[0:MB] * score_scale)
        grad_key[MB:, cols] = bf16((keys[MB:] + far_keys) * score_scale)
        grad_value[0:MB, cols] = bf16(values[0:MB])
        grad_value[MB:, cols] = bf16(values[MB:] + far_values)


def call(kernel, specs, outs, flops, *args):
    shapes = [jax.ShapeDtypeStruct(shape, dtype) for shape, dtype in outs]
    moved = sum(a.size * a.dtype.itemsize for a in args)
    moved += sum(s.size * s.dtype.itemsize for s in shapes)
    return pl.pallas_call(
        kernel,
        out_shape=shapes,
        in_specs=specs,
        out_specs=[VMEM] * len(shapes),
        compiler_params=pltpu.CompilerParams(vmem_limit_bytes=16 << 20),
        cost_estimate=pl.CostEstimate(flops=flops, bytes_accessed=moved, transcendentals=0),
    )(*args)


def shifted(value, steps):
    count = lax.axis_size("blk")
    pairs = [(source, source + steps) for source in range(count) if 0 <= source + steps < count]
    return lax.ppermute(value, "blk", pairs)


def other_core(value):
    count = lax.axis_size("head")
    return lax.ppermute(value, "head", [(source, source ^ 1) for source in range(count)])


def on_device(query_rows, key_rows, value_rows, grad_out, out_weight, mask_types, drop_seed):
    half, full = jnp.bfloat16, jnp.float32
    count = lax.axis_size("head")
    parts, width = count // 2, grad_out.shape[1]
    groups = [list(range(first, count, 2)) for first in range(2)]

    def gather(rows):
        return lax.all_gather(rows, "head", axis=0, axis_index_groups=groups)

    near_keys = shifted(jnp.concatenate((key_rows, value_rows)), 1)
    near_query = shifted(query_rows, -1)
    top = gather(grad_out[:MB])
    top_other = other_core(top)
    far_keys = shifted(jnp.concatenate((near_keys[MB:ROWS], near_keys[ROWS + MB :])), 1)
    far_query = shifted(near_query[:MB], -1)
    tile = 2 * MB * MB * DH

    def outs(width, keys, queries):
        return [
            ((HEADS, MB, width), full),
            ((MB, WIDE), half),
            ((MB, MB), full),
            ((HEADS, keys, queries), full),
            ((HEADS, keys, queries), full),
        ]

    signed_low, attended_low, stats_low, near_scores, near_keeps = call(
        near_kernel, [SMEM, SMEM] + [VMEM] * 5, outs(WIN - MB, ROWS, ROWS), 48 * tile,
        mask_types, drop_seed, query_rows, key_rows, value_rows, near_keys, near_query,
    )
    signed_top, attended_top, stats_top, far_scores, far_keeps = call(
        far_kernel, [SMEM, SMEM] + [VMEM] * 6, outs(WIN, MB, MB), 48 * tile,
        mask_types, drop_seed, query_rows, key_rows, value_rows, near_keys, far_keys, far_query,
    )
    low_rows, attended_top, attended_low = lax.optimization_barrier(
        (grad_out[MB:], attended_top, attended_low)
    )
    low = gather(low_rows)
    low_other = other_core(low)
    flops = 2 * MB * WIDE * width * parts
    (partial,) = call(
        project_kernel, [VMEM] * 4, [((ROWS, WIDE), full)], 3 * flops,
        top, top_other, low, out_weight,
    )
    near_rows, far_rows = call(
        rows_kernel,
        [VMEM] * 7,
        [((ROWS + EXTRA, WIDE), half), ((MB + EXTRA, WIDE), half)],
        flops,
        partial, low_other, out_weight, attended_top, attended_low, stats_top, stats_low,
    )
    near_grad = shifted(near_rows, -1)
    far_grad = shifted(far_rows, -2)
    grad_query, key_part, value_part = call(
        own_kernel,
        [VMEM] * 10,
        [((ROWS, WIDE), half), ((ROWS, WIDE), full), ((ROWS, WIDE), full)],
        80 * tile,
        signed_top, signed_low, attended_top, attended_low, query_rows, near_rows, key_rows,
        value_rows, near_keys, far_keys,
    )
    grad_key, grad_value = call(
        finish_kernel,
        [VMEM] * 11,
        [((ROWS, WIDE), half), ((ROWS, WIDE), half)],
        40 * tile,
        near_scores, near_keeps, far_scores, far_keeps, value_rows, near_query, far_query,
        near_grad, far_grad, key_part, value_part,
    )
    return (grad_query, grad_key, grad_value)


def solution(mesh):
    split = P("blk", "head")
    return jax.shard_map(
        on_device,
        mesh=mesh,
        in_specs=(split, split, split, split, P("head", None), P(), P()),
        out_specs=(split, split, split),
        check_vma=False,
    )
```

```python
import functools

import jax
import jax.numpy as jnp
from jax import lax
from jax.experimental import pallas as pl
from jax.experimental.pallas import tpu as pltpu
from jax.sharding import PartitionSpec as P

DH = 128
MB = 128
HEADS = 2
ROWS = 256
SLOTS = 5
WIN = SLOTS * MB
FAR = 3 * MB
WIDE = HEADS * DH
EXTRA = 16

drop_level = 6554
keep_scale = 65536.0 / 58982.0
mix_one = 73244475
mix_two = 295559667
mix_three = 668265263
score_scale = DH**-0.5
hidden = -1e30

VMEM = pl.BlockSpec(memory_space=pltpu.VMEM)
SMEM = pl.BlockSpec(memory_space=pltpu.SMEM)


def bf16(value):
    return value.astype(jnp.bfloat16)


def f32(value):
    return value.astype(jnp.float32)


def dot_last(left, right):
    return lax.dot_general(
        left, right, (((1,), (1,)), ((), ())), preferred_element_type=jnp.float32
    )


def dot_first(left, right):
    return lax.dot_general(
        left, right, (((0,), (0,)), ((), ())), preferred_element_type=jnp.float32
    )


def dot(left, right):
    return jnp.dot(left, right, preferred_element_type=jnp.float32)


def bound_of(table, query_block, key_block):
    last = table.shape[0] - 1
    inside = (key_block >= 0) & (query_block <= last)
    kind = table[jnp.minimum(query_block, last), jnp.maximum(key_block, 0)]
    far = jnp.int32(1 << 20)
    bound = jnp.where(kind == 2, far, jnp.where(kind == 1, (query_block - key_block) * MB, -far))
    return jnp.where(inside, bound, -far)


def kept(seed, head, query_block, key_block, query_axis):
    base = query_block * MB * mix_one + key_block * MB * mix_two + head * mix_three + seed
    rows = lax.broadcasted_iota(jnp.int32, (MB, MB), query_axis) * mix_one
    cols = lax.broadcasted_iota(jnp.int32, (MB, MB), 1 - query_axis) * mix_two
    hashed = (rows + cols) + base
    for _ in range(2):
        hashed = hashed ^ lax.shift_right_logical(hashed, jnp.int32(16))
        hashed = hashed * mix_one
    hashed = hashed ^ lax.shift_right_logical(hashed, jnp.int32(16))
    return (hashed & 65535) >= drop_level


def key_minus_query(query_axis):
    return lax.broadcasted_iota(jnp.int32, (MB, MB), 1 - query_axis) - lax.broadcasted_iota(
        jnp.int32, (MB, MB), query_axis
    )


def put_parts(stats, lane, first, column):
    rest = column
    for part in range(3):
        piece = f32(bf16(rest))
        stats = jnp.where(lane == first + part, piece, stats)
        rest = rest - piece
    return stats


def take_parts(stats, first):
    return stats[first : first + 1] + stats[first + 1 : first + 2] + stats[first + 2 : first + 3]


def forward(table, seed, block, query, keys, values, signed, attended, stats):
    shard = lax.axis_index("blk")
    first_head = lax.axis_index("head") * HEADS
    count = keys(0).shape[0] // MB
    query_block = shard * 2 + block
    first_block = shard * 2 + 2 - count
    ahead = key_minus_query(0)
    lane = lax.broadcasted_iota(jnp.int32, (MB, MB), 1)
    parts = jnp.zeros((MB, MB), jnp.float32)
    for head in range(HEADS):
        cols = pl.ds(head * DH, DH)
        scores = dot_last(query[block * MB : (block + 1) * MB, cols], keys(head))
        tiles = []
        for slot in range(count):
            bound = bound_of(table, query_block, first_block + slot)
            tile = scores[:, slot * MB : (slot + 1) * MB] * score_scale
            tiles.append(jnp.where(ahead <= bound, tile, hidden))
        top = functools.reduce(jnp.maximum, tiles)
        top = jnp.max(top, axis=1, keepdims=True)
        tiles = [jnp.exp(tile - top) for tile in tiles]
        total = jnp.sum(functools.reduce(jnp.add, tiles), axis=1, keepdims=True)
        inverse = 1.0 / total
        drops = []
        for slot in range(count):
            prob = tiles[slot] * inverse
            keep = kept(seed[0], first_head + head, query_block, first_block + slot, 0)
            signed[head, :, slot * MB : (slot + 1) * MB] = jnp.where(keep, prob, -prob)
            drops.append(bf16(jnp.where(keep, prob * keep_scale, 0.0)))
        attended[:, cols] = bf16(dot(jnp.concatenate(drops, axis=1), values(head)))
        parts = put_parts(parts, lane, 3 * head, top + jnp.log(total))
    stats[...] = parts


def later(table, seed, first_query, first_key, queries, keys, scores, keeps):
    first_head = lax.axis_index("head") * HEADS
    ahead = key_minus_query(1)
    for head in range(HEADS):
        cols = pl.ds(head * DH, DH)
        tiles = dot_last(keys[:, cols], queries[:, cols]) * score_scale
        for block in range(queries.shape[0] // MB):
            across = slice(block * MB, (block + 1) * MB)
            for slot in range(keys.shape[0] // MB):
                down = slice(slot * MB, (slot + 1) * MB)
                bound = bound_of(table, first_query + block, first_key + slot)
                scores[head, down, across] = jnp.where(
                    ahead <= bound, tiles[down, across], hidden
                )
                keep = kept(seed[0], first_head + head, first_query + block, first_key + slot, 1)
                keeps[head, down, across] = jnp.where(keep, jnp.float32(keep_scale), 0.0)


def stacked(*parts):
    def of_head(head):
        cols = slice(head * DH, (head + 1) * DH)
        return jnp.concatenate([ref[rows, cols] for ref, rows in parts], axis=0)

    return of_head


def near_window(key, value, near):
    whole = slice(None)
    keys = ((near, slice(0, ROWS)), (key, whole))
    values = ((near, slice(ROWS, None)), (value, whole))
    return keys, values


def far_window(key, value, near, far):
    keys, values = near_window(key, value, near)
    return ((far, slice(0, MB)), *keys), ((far, slice(MB, None)), *values)


def near_kernel(table, seed, query, key, value, near, signed, attended, stats):
    keys, values = near_window(key, value, near)
    forward(table, seed, 1, query, stacked(*keys), stacked(*values), signed, attended, stats)


def far_kernel(table, seed, query, key, value, near, far, signed, attended, stats):
    keys, values = far_window(key, value, near, far)
    forward(table, seed, 0, query, stacked(*keys), stacked(*values), signed, attended, stats)


def later_kernel(
    table, seed, key, near_query, far_query, near_scores, near_keeps, far_scores, far_keeps
):
    block = lax.axis_index("blk") * 2
    later(table, seed, block + 2, block, near_query, key, near_scores, near_keeps)
    later(table, seed, block + 4, block + 1, far_query, key.at[MB:], far_scores, far_keeps)


def project(total, gathered, weight, core):
    parts, _, width = gathered.shape
    for part in range(parts):
        first = pl.multiple_of((part * 2 + core) * width, width)
        term = dot_last(gathered[part], weight[:, pl.ds(first, width)])
        total = term if total is None else total + term
    return total


def project_kernel(top, top_other, low, weight, out):
    core = lax.rem(lax.axis_index("head"), 2)
    out[0:MB] = project(project(None, top, weight, core), top_other, weight, 1 - core)
    out[MB:] = project(None, low, weight, core)


def rows_kernel(
    partial, low_other, weight, attended_top, attended_low, stats_top, stats_low, near, far
):
    core = lax.rem(lax.axis_index("head"), 2)
    low = project(partial[MB:], low_other, weight, 1 - core)
    lane = lax.broadcasted_iota(jnp.int32, (MB, MB), 1)
    for block, total, attended, stats in (
        (0, partial[0:MB], attended_top, stats_top), (1, low, attended_low, stats_low)
    ):
        rows = slice(block * MB, (block + 1) * MB)
        grad = bf16(total)
        near[rows] = grad
        parts = stats[...]
        for head in range(HEADS):
            cols = slice(head * DH, (head + 1) * DH)
            row_dot = jnp.sum(f32(grad[:, cols]) * f32(attended[:, cols]), axis=1, keepdims=True)
            parts = put_parts(parts, lane, 6 + 3 * head, row_dot)
        across = bf16(parts.T[0:EXTRA])
        near[ROWS:, rows] = across
        if block == 0:
            far[0:MB] = grad
        far[MB:, rows] = across


def own_kernel(
    signed_top, signed_low, attended_top, attended_low, query, grad, key, value, near, far,
    grad_query, key_part, value_part,
):
    for head in range(HEADS):
        cols = slice(head * DH, (head + 1) * DH)
        key_sum = value_sum = None
        for block, signed, attended, (keys, values) in (
            (0, signed_top, attended_top, far_window(key, value, near, far)),
            (1, signed_low, attended_low, near_window(key, value, near)),
        ):
            rows = slice(block * MB, (block + 1) * MB)
            grad_head = grad[rows, cols]
            row_dot = jnp.sum(f32(grad_head) * f32(attended[:, cols]), axis=1, keepdims=True)
            grad_prob = dot_last(grad_head, stacked(*values)(head))
            probs = signed[head]
            first = probs.shape[1] - ROWS
            scaled = jnp.where(probs > 0.0, grad_prob * keep_scale, 0.0)
            dscore = bf16(jnp.abs(probs) * (scaled - row_dot))
            dropped = bf16(jnp.maximum(probs[:, first:], 0.0) * keep_scale)
            grad_query[rows, cols] = bf16(dot(dscore, stacked(*keys)(head)) * score_scale)
            key_term = dot_first(dscore[:, first:], query[rows, cols])
            value_term = dot_first(dropped, grad_head)
            key_sum = key_term if key_sum is None else key_sum + key_term
            value_sum = value_term if value_sum is None else value_sum + value_term
        key_part[:, cols] = key_sum
        value_part[:, cols] = value_sum


def finish_kernel(
    near_scores, near_keeps, far_scores, far_keeps, value, near_query, far_query, near_grad,
    far_grad, key_part, value_part, grad_key, grad_value,
):
    for head in range(HEADS):
        cols = pl.ds(head * DH, DH)

        def terms(scores, keeps, values, queries, grads):
            count = queries.shape[0]
            grad_head = grads[0:count, cols]
            stats = f32(grads[count:, 0:count])
            prob = jnp.exp(scores[head] - take_parts(stats, 3 * head))
            keep = keeps[head]
            grad_prob = dot_last(values, grad_head)
            dscore = bf16(prob * (grad_prob * keep - take_parts(stats, 6 + 3 * head)))
            return dot(dscore, queries[:, cols]), dot(bf16(prob * keep), grad_head)

        keys, values = terms(near_scores, near_keeps, value[:, cols], near_query, near_grad)
        far_keys, far_values = terms(far_scores, far_keeps, value[MB:, cols], far_query, far_grad)
        keys = keys + key_part[:, cols]
        values = values + value_part[:, cols]
        grad_key[0:MB, cols] = bf16(keys[0:MB] * score_scale)
        grad_key[MB:, cols] = bf16((keys[MB:] + far_keys) * score_scale)
        grad_value[0:MB, cols] = bf16(values[0:MB])
        grad_value[MB:, cols] = bf16(values[MB:] + far_values)


def call(kernel, specs, outs, microseconds, *args):
    shapes = [jax.ShapeDtypeStruct(shape, dtype) for shape, dtype in outs]
    moved = sum(a.size * a.dtype.itemsize for a in args)
    moved += sum(s.size * s.dtype.itemsize for s in shapes)
    flops = int(microseconds * 1.15e9)
    return pl.pallas_call(
        kernel,
        out_shape=shapes,
        in_specs=specs,
        out_specs=[VMEM] * len(shapes),
        compiler_params=pltpu.CompilerParams(vmem_limit_bytes=16 << 20),
        cost_estimate=pl.CostEstimate(flops=flops, bytes_accessed=moved, transcendentals=0),
    )(*args)


def shifted(value, steps):
    count = lax.axis_size("blk")
    pairs = [(source, source + steps) for source in range(count) if 0 <= source + steps < count]
    return lax.ppermute(value, "blk", pairs)


def other_core(value):
    count = lax.axis_size("head")
    return lax.ppermute(value, "head", [(source, source ^ 1) for source in range(count)])


def on_device(query_rows, key_rows, value_rows, grad_out, out_weight, mask_types, drop_seed):
    half, full = jnp.bfloat16, jnp.float32
    count = lax.axis_size("head")
    groups = [list(range(first, count, 2)) for first in range(2)]

    def gather(rows):
        return lax.all_gather(rows, "head", axis=0, axis_index_groups=groups)

    near_keys = shifted(jnp.concatenate((key_rows, value_rows)), 1)
    top = gather(grad_out[:MB])
    top, sent_query = lax.optimization_barrier((top, query_rows))
    near_query = shifted(sent_query, -1)
    far_query = shifted(sent_query[:MB], -2)
    top, near_keys = lax.optimization_barrier((top, near_keys))
    top_other = other_core(top)
    far_keys = shifted(jnp.concatenate((near_keys[MB:ROWS], near_keys[ROWS + MB :])), 1)
    low_rows, near_keys = lax.optimization_barrier((grad_out[MB:], near_keys))
    low = gather(low_rows)
    low, near_keys = lax.optimization_barrier((low, near_keys))
    low_other = other_core(low)

    def outs(keys):
        return [((HEADS, MB, keys), full), ((MB, WIDE), half), ((MB, MB), full)]

    signed_low, attended_low, stats_low = call(
        near_kernel, [SMEM, SMEM] + [VMEM] * 4, outs(WIN - MB), 1.8,
        mask_types, drop_seed, query_rows, key_rows, value_rows, near_keys,
    )
    signed_top, attended_top, stats_top = call(
        far_kernel, [SMEM, SMEM] + [VMEM] * 5, outs(WIN), 2.0,
        mask_types, drop_seed, query_rows, key_rows, value_rows, near_keys, far_keys,
    )
    (partial,) = call(
        project_kernel, [VMEM] * 4, [((ROWS, WIDE), full)], 1.2, top, top_other, low, out_weight
    )
    near_rows, far_rows = call(
        rows_kernel,
        [VMEM] * 7,
        [((ROWS + EXTRA, WIDE), half), ((MB + EXTRA, WIDE), half)],
        0.7,
        partial, low_other, out_weight, attended_top, attended_low, stats_top, stats_low,
    )
    near_grad = shifted(near_rows, -1)
    far_grad = shifted(far_rows, -2)
    grad_query, key_part, value_part = call(
        own_kernel,
        [VMEM] * 10,
        [((ROWS, WIDE), half), ((ROWS, WIDE), full), ((ROWS, WIDE), full)],
        1.7,
        signed_top, signed_low, attended_top, attended_low, query_rows, near_rows, key_rows,
        value_rows, near_keys, far_keys,
    )
    later_key, _ = lax.optimization_barrier((key_rows, near_rows))
    scores = call(
        later_kernel, [SMEM, SMEM] + [VMEM] * 3,
        [((HEADS, ROWS, ROWS), full)] * 2 + [((HEADS, MB, MB), full)] * 2, 2.0,
        mask_types, drop_seed, later_key, near_query, far_query,
    )
    grad_key, grad_value = call(
        finish_kernel,
        [VMEM] * 11,
        [((ROWS, WIDE), half), ((ROWS, WIDE), half)],
        1.3,
        *scores, value_rows, near_query, far_query, near_grad, far_grad, key_part, value_part,
    )
    return (grad_query, grad_key, grad_value)


def solution(mesh):
    split = P("blk", "head")
    return jax.shard_map(
        on_device,
        mesh=mesh,
        in_specs=(split, split, split, split, P("head", None), P(), P()),
        out_specs=(split, split, split),
        check_vma=False,
    )
```

```python
import functools

import jax
import jax.numpy as jnp
from jax import lax
from jax.experimental import pallas as pl
from jax.experimental.pallas import tpu as pltpu
from jax.sharding import PartitionSpec as P

DH = 128
MB = 128
HEADS = 2
ROWS = 256
SLOTS = 5
WIN = SLOTS * MB
FAR = 3 * MB
WIDE = HEADS * DH
EXTRA = 16

drop_level = 6554
keep_scale = 65536.0 / 58982.0
mix_one = 73244475
mix_two = 295559667
mix_three = 668265263
score_scale = DH**-0.5
hidden = -1e30

VMEM = pl.BlockSpec(memory_space=pltpu.VMEM)
SMEM = pl.BlockSpec(memory_space=pltpu.SMEM)


def bf16(value):
    return value.astype(jnp.bfloat16)


def f32(value):
    return value.astype(jnp.float32)


def dot_last(left, right):
    return lax.dot_general(
        left, right, (((1,), (1,)), ((), ())), preferred_element_type=jnp.float32
    )


def dot_first(left, right):
    return lax.dot_general(
        left, right, (((0,), (0,)), ((), ())), preferred_element_type=jnp.float32
    )


def dot(left, right):
    return jnp.dot(left, right, preferred_element_type=jnp.float32)


def bound_of(table, query_block, key_block):
    last = table.shape[0] - 1
    inside = (key_block >= 0) & (query_block <= last)
    kind = table[jnp.minimum(query_block, last), jnp.maximum(key_block, 0)]
    far = jnp.int32(1 << 20)
    bound = jnp.where(kind == 2, far, jnp.where(kind == 1, (query_block - key_block) * MB, -far))
    return jnp.where(inside, bound, -far)


def kept(seed, head, query_block, key_block, query_axis):
    base = query_block * MB * mix_one + key_block * MB * mix_two + head * mix_three + seed
    rows = lax.broadcasted_iota(jnp.int32, (MB, MB), query_axis) * mix_one
    cols = lax.broadcasted_iota(jnp.int32, (MB, MB), 1 - query_axis) * mix_two
    hashed = (rows + cols) + base
    for _ in range(2):
        hashed = hashed ^ lax.shift_right_logical(hashed, jnp.int32(16))
        hashed = hashed * mix_one
    hashed = hashed ^ lax.shift_right_logical(hashed, jnp.int32(16))
    return (hashed & 65535) >= drop_level


def key_minus_query(query_axis):
    return lax.broadcasted_iota(jnp.int32, (MB, MB), 1 - query_axis) - lax.broadcasted_iota(
        jnp.int32, (MB, MB), query_axis
    )


def put_parts(stats, lane, first, column):
    rest = column
    for part in range(3):
        piece = f32(bf16(rest))
        stats = jnp.where(lane == first + part, piece, stats)
        rest = rest - piece
    return stats


def take_parts(stats, first):
    return stats[first : first + 1] + stats[first + 1 : first + 2] + stats[first + 2 : first + 3]


def forward(table, seed, block, query, keys, values, signed, attended, stats):
    shard = lax.axis_index("blk")
    first_head = lax.axis_index("head") * HEADS
    count = keys(0).shape[0] // MB
    query_block = shard * 2 + block
    first_block = shard * 2 + 2 - count
    ahead = key_minus_query(0)
    lane = lax.broadcasted_iota(jnp.int32, (MB, MB), 1)
    parts = jnp.zeros((MB, MB), jnp.float32)
    for head in range(HEADS):
        cols = pl.ds(head * DH, DH)
        scores = dot_last(query[block * MB : (block + 1) * MB, cols], keys(head))
        tiles = []
        for slot in range(count):
            bound = bound_of(table, query_block, first_block + slot)
            tile = scores[:, slot * MB : (slot + 1) * MB] * score_scale
            tiles.append(jnp.where(ahead <= bound, tile, hidden))
        top = functools.reduce(jnp.maximum, tiles)
        top = jnp.max(top, axis=1, keepdims=True)
        tiles = [jnp.exp(tile - top) for tile in tiles]
        total = jnp.sum(functools.reduce(jnp.add, tiles), axis=1, keepdims=True)
        inverse = 1.0 / total
        drops = []
        for slot in range(count):
            prob = tiles[slot] * inverse
            keep = kept(seed[0], first_head + head, query_block, first_block + slot, 0)
            signed[head, :, slot * MB : (slot + 1) * MB] = jnp.where(keep, prob, -prob)
            drops.append(bf16(jnp.where(keep, prob * keep_scale, 0.0)))
        attended[:, cols] = bf16(dot(jnp.concatenate(drops, axis=1), values(head)))
        parts = put_parts(parts, lane, 3 * head, top + jnp.log(total))
    stats[...] = parts


def later(table, seed, first_query, first_key, queries, keys, scores, keeps):
    first_head = lax.axis_index("head") * HEADS
    ahead = key_minus_query(1)
    for head in range(HEADS):
        cols = pl.ds(head * DH, DH)
        tiles = dot_last(keys[:, cols], queries[:, cols]) * score_scale
        for block in range(queries.shape[0] // MB):
            across = slice(block * MB, (block + 1) * MB)
            for slot in range(keys.shape[0] // MB):
                down = slice(slot * MB, (slot + 1) * MB)
                bound = bound_of(table, first_query + block, first_key + slot)
                scores[head, down, across] = jnp.where(
                    ahead <= bound, tiles[down, across], hidden
                )
                keep = kept(seed[0], first_head + head, first_query + block, first_key + slot, 1)
                keeps[head, down, across] = jnp.where(keep, jnp.float32(keep_scale), 0.0)


def stacked(*parts):
    def of_head(head):
        cols = slice(head * DH, (head + 1) * DH)
        return jnp.concatenate([ref[rows, cols] for ref, rows in parts], axis=0)

    return of_head


def near_window(key, value, near):
    whole = slice(None)
    keys = ((near, slice(0, ROWS)), (key, whole))
    values = ((near, slice(ROWS, None)), (value, whole))
    return keys, values


def far_window(key, value, near, far):
    keys, values = near_window(key, value, near)
    return ((far, slice(0, MB)), *keys), ((far, slice(MB, None)), *values)


def near_kernel(table, seed, query, key, value, near, signed, attended, stats):
    keys, values = near_window(key, value, near)
    forward(table, seed, 1, query, stacked(*keys), stacked(*values), signed, attended, stats)


def far_kernel(table, seed, query, key, value, near, far, signed, attended, stats):
    keys, values = far_window(key, value, near, far)
    forward(table, seed, 0, query, stacked(*keys), stacked(*values), signed, attended, stats)


def later_kernel(
    table, seed, key, near_query, far_query, near_scores, near_keeps, far_scores, far_keeps
):
    block = lax.axis_index("blk") * 2
    later(table, seed, block + 2, block, near_query, key, near_scores, near_keeps)
    later(table, seed, block + 4, block + 1, far_query, key.at[MB:], far_scores, far_keeps)


def project(total, gathered, weight, core):
    parts, _, width = gathered.shape
    for part in range(parts):
        first = pl.multiple_of((part * 2 + core) * width, width)
        term = dot_last(gathered[part], weight[:, pl.ds(first, width)])
        total = term if total is None else total + term
    return total


def project_kernel(gathered, weight, out):
    out[...] = project(None, gathered, weight, lax.rem(lax.axis_index("head"), 2))


def rows_kernel(
    partial, other, weight, attended_top, attended_low, stats_top, stats_low, near, far
):
    core = lax.rem(lax.axis_index("head"), 2)
    whole = project(partial[...], other, weight, 1 - core)
    lane = lax.broadcasted_iota(jnp.int32, (MB, MB), 1)
    for block, total, attended, stats in (
        (0, whole[0:MB], attended_top, stats_top), (1, whole[MB:], attended_low, stats_low)
    ):
        rows = slice(block * MB, (block + 1) * MB)
        grad = bf16(total)
        near[rows] = grad
        parts = stats[...]
        for head in range(HEADS):
            cols = slice(head * DH, (head + 1) * DH)
            row_dot = jnp.sum(f32(grad[:, cols]) * f32(attended[:, cols]), axis=1, keepdims=True)
            parts = put_parts(parts, lane, 6 + 3 * head, row_dot)
        across = bf16(parts.T[0:EXTRA])
        near[ROWS:, rows] = across
        if block == 0:
            far[0:MB] = grad
        far[MB:, rows] = across


def own_kernel(
    signed_top, signed_low, attended_top, attended_low, query, grad, key, value, near, far,
    grad_query, key_part, value_part,
):
    for head in range(HEADS):
        cols = slice(head * DH, (head + 1) * DH)
        key_sum = value_sum = None
        for block, signed, attended, (keys, values) in (
            (0, signed_top, attended_top, far_window(key, value, near, far)),
            (1, signed_low, attended_low, near_window(key, value, near)),
        ):
            rows = slice(block * MB, (block + 1) * MB)
            grad_head = grad[rows, cols]
            row_dot = jnp.sum(f32(grad_head) * f32(attended[:, cols]), axis=1, keepdims=True)
            grad_prob = dot_last(grad_head, stacked(*values)(head))
            probs = signed[head]
            first = probs.shape[1] - ROWS
            scaled = jnp.where(probs > 0.0, grad_prob * keep_scale, 0.0)
            dscore = bf16(jnp.abs(probs) * (scaled - row_dot))
            dropped = bf16(jnp.maximum(probs[:, first:], 0.0) * keep_scale)
            grad_query[rows, cols] = bf16(dot(dscore, stacked(*keys)(head)) * score_scale)
            key_term = dot_first(dscore[:, first:], query[rows, cols])
            value_term = dot_first(dropped, grad_head)
            key_sum = key_term if key_sum is None else key_sum + key_term
            value_sum = value_term if value_sum is None else value_sum + value_term
        key_part[:, cols] = key_sum
        value_part[:, cols] = value_sum


def finish_kernel(
    near_scores, near_keeps, far_scores, far_keeps, value, near_query, far_query, near_grad,
    far_grad, key_part, value_part, grad_key, grad_value,
):
    for head in range(HEADS):
        cols = pl.ds(head * DH, DH)

        def terms(scores, keeps, values, queries, grads):
            count = queries.shape[0]
            grad_head = grads[0:count, cols]
            stats = f32(grads[count:, 0:count])
            prob = jnp.exp(scores[head] - take_parts(stats, 3 * head))
            keep = keeps[head]
            grad_prob = dot_last(values, grad_head)
            dscore = bf16(prob * (grad_prob * keep - take_parts(stats, 6 + 3 * head)))
            return dot(dscore, queries[:, cols]), dot(bf16(prob * keep), grad_head)

        keys, values = terms(near_scores, near_keeps, value[:, cols], near_query, near_grad)
        far_keys, far_values = terms(far_scores, far_keeps, value[MB:, cols], far_query, far_grad)
        keys = keys + key_part[:, cols]
        values = values + value_part[:, cols]
        grad_key[0:MB, cols] = bf16(keys[0:MB] * score_scale)
        grad_key[MB:, cols] = bf16((keys[MB:] + far_keys) * score_scale)
        grad_value[0:MB, cols] = bf16(values[0:MB])
        grad_value[MB:, cols] = bf16(values[MB:] + far_values)


def call(kernel, specs, outs, microseconds, *args):
    shapes = [jax.ShapeDtypeStruct(shape, dtype) for shape, dtype in outs]
    moved = sum(a.size * a.dtype.itemsize for a in args)
    moved += sum(s.size * s.dtype.itemsize for s in shapes)
    flops = int(microseconds * 1.15e9)
    return pl.pallas_call(
        kernel,
        out_shape=shapes,
        in_specs=specs,
        out_specs=[VMEM] * len(shapes),
        compiler_params=pltpu.CompilerParams(vmem_limit_bytes=16 << 20),
        cost_estimate=pl.CostEstimate(flops=flops, bytes_accessed=moved, transcendentals=0),
    )(*args)


def shifted(value, steps):
    count = lax.axis_size("blk")
    pairs = [(source, source + steps) for source in range(count) if 0 <= source + steps < count]
    return lax.ppermute(value, "blk", pairs)


def other_core(value):
    count = lax.axis_size("head")
    return lax.ppermute(value, "head", [(source, source ^ 1) for source in range(count)])


def on_device(query_rows, key_rows, value_rows, grad_out, out_weight, mask_types, drop_seed):
    half, full = jnp.bfloat16, jnp.float32
    count = lax.axis_size("head")
    groups = [list(range(first, count, 2)) for first in range(2)]

    copies = jnp.broadcast_to(grad_out[None], (count // 2, *grad_out.shape))
    gathered = lax.all_to_all(copies, "head", 0, 0, axis_index_groups=groups)
    near_keys = shifted(jnp.concatenate((key_rows, value_rows)), 1)
    near_query = shifted(query_rows, -1)
    far_keys = shifted(jnp.concatenate((key_rows[MB:], value_rows[MB:])), 2)
    far_query = shifted(query_rows[:MB], -2)

    def outs(keys):
        return [((HEADS, MB, keys), full), ((MB, WIDE), half), ((MB, MB), full)]

    signed_low, attended_low, stats_low = call(
        near_kernel, [SMEM, SMEM] + [VMEM] * 4, outs(WIN - MB), 1.8,
        mask_types, drop_seed, query_rows, key_rows, value_rows, near_keys,
    )
    signed_top, attended_top, stats_top = call(
        far_kernel, [SMEM, SMEM] + [VMEM] * 5, outs(WIN), 2.0,
        mask_types, drop_seed, query_rows, key_rows, value_rows, near_keys, far_keys,
    )
    gathered, attended_low, attended_top, near_query, far_query = lax.optimization_barrier(
        (gathered, attended_low, attended_top, near_query, far_query)
    )
    other = other_core(gathered)
    (partial,) = call(
        project_kernel, [VMEM] * 2, [((ROWS, WIDE), full)], 0.7, gathered, out_weight
    )
    near_rows, far_rows = call(
        rows_kernel,
        [VMEM] * 7,
        [((ROWS + EXTRA, WIDE), half), ((MB + EXTRA, WIDE), half)],
        1.0,
        partial, other, out_weight, attended_top, attended_low, stats_top, stats_low,
    )
    near_grad = shifted(near_rows, -1)
    far_grad = shifted(far_rows, -2)
    grad_query, key_part, value_part = call(
        own_kernel,
        [VMEM] * 10,
        [((ROWS, WIDE), half), ((ROWS, WIDE), full), ((ROWS, WIDE), full)],
        1.7,
        signed_top, signed_low, attended_top, attended_low, query_rows, near_rows, key_rows,
        value_rows, near_keys, far_keys,
    )
    later_key, _ = lax.optimization_barrier((key_rows, near_rows))
    scores = call(
        later_kernel, [SMEM, SMEM] + [VMEM] * 3,
        [((HEADS, ROWS, ROWS), full)] * 2 + [((HEADS, MB, MB), full)] * 2, 2.0,
        mask_types, drop_seed, later_key, near_query, far_query,
    )
    grad_key, grad_value = call(
        finish_kernel,
        [VMEM] * 11,
        [((ROWS, WIDE), half), ((ROWS, WIDE), half)],
        1.3,
        *scores, value_rows, near_query, far_query, near_grad, far_grad, key_part, value_part,
    )
    return (grad_query, grad_key, grad_value)


def solution(mesh):
    split = P("blk", "head")
    return jax.shard_map(
        on_device,
        mesh=mesh,
        in_specs=(split, split, split, split, P("head", None), P(), P()),
        out_specs=(split, split, split),
        check_vma=False,
    )
```

```python
import functools

import jax
import jax.numpy as jnp
from jax import lax
from jax.experimental import pallas as pl
from jax.experimental.pallas import tpu as pltpu
from jax.sharding import PartitionSpec as P

DH = 128
MB = 128
HEADS = 2
ROWS = 256
SLOTS = 5
WIN = SLOTS * MB
FAR = 3 * MB
WIDE = HEADS * DH
EXTRA = 16

drop_level = 6554
keep_scale = 65536.0 / 58982.0
mix_one = 73244475
mix_two = 295559667
mix_three = 668265263
score_scale = DH**-0.5
hidden = -1e30

VMEM = pl.BlockSpec(memory_space=pltpu.VMEM)
SMEM = pl.BlockSpec(memory_space=pltpu.SMEM)


def bf16(value):
    return value.astype(jnp.bfloat16)


def f32(value):
    return value.astype(jnp.float32)


def dot_last(left, right):
    return lax.dot_general(
        left, right, (((1,), (1,)), ((), ())), preferred_element_type=jnp.float32
    )


def dot_first(left, right):
    return lax.dot_general(
        left, right, (((0,), (0,)), ((), ())), preferred_element_type=jnp.float32
    )


def dot(left, right):
    return jnp.dot(left, right, preferred_element_type=jnp.float32)


def bound_of(table, query_block, key_block):
    last = table.shape[0] - 1
    inside = (key_block >= 0) & (query_block <= last)
    kind = table[jnp.minimum(query_block, last), jnp.maximum(key_block, 0)]
    far = jnp.int32(1 << 20)
    bound = jnp.where(kind == 2, far, jnp.where(kind == 1, (query_block - key_block) * MB, -far))
    return jnp.where(inside, bound, -far)


def kept(seed, head, query_block, key_block, query_axis):
    base = query_block * MB * mix_one + key_block * MB * mix_two + head * mix_three + seed
    rows = lax.broadcasted_iota(jnp.int32, (MB, MB), query_axis) * mix_one
    cols = lax.broadcasted_iota(jnp.int32, (MB, MB), 1 - query_axis) * mix_two
    hashed = (rows + cols) + base
    for _ in range(2):
        hashed = hashed ^ lax.shift_right_logical(hashed, jnp.int32(16))
        hashed = hashed * mix_one
    hashed = hashed ^ lax.shift_right_logical(hashed, jnp.int32(16))
    return (hashed & 65535) >= drop_level


def key_minus_query(query_axis):
    return lax.broadcasted_iota(jnp.int32, (MB, MB), 1 - query_axis) - lax.broadcasted_iota(
        jnp.int32, (MB, MB), query_axis
    )


def put_parts(stats, lane, first, column):
    rest = column
    for part in range(3):
        piece = f32(bf16(rest))
        stats = jnp.where(lane == first + part, piece, stats)
        rest = rest - piece
    return stats


def take_parts(stats, first):
    return stats[first : first + 1] + stats[first + 1 : first + 2] + stats[first + 2 : first + 3]


def forward(table, seed, block, query, keys, values, signed, attended, stats):
    shard = lax.axis_index("blk")
    first_head = lax.axis_index("head") * HEADS
    count = keys(0).shape[0] // MB
    query_block = shard * 2 + block
    first_block = shard * 2 + 2 - count
    ahead = key_minus_query(0)
    lane = lax.broadcasted_iota(jnp.int32, (MB, MB), 1)
    parts = jnp.zeros((MB, MB), jnp.float32)
    for head in range(HEADS):
        cols = pl.ds(head * DH, DH)
        scores = dot_last(query[block * MB : (block + 1) * MB, cols], keys(head))
        tiles = []
        for slot in range(count):
            bound = bound_of(table, query_block, first_block + slot)
            tile = scores[:, slot * MB : (slot + 1) * MB] * score_scale
            tiles.append(jnp.where(ahead <= bound, tile, hidden))
        top = functools.reduce(jnp.maximum, tiles)
        top = jnp.max(top, axis=1, keepdims=True)
        tiles = [jnp.exp(tile - top) for tile in tiles]
        total = jnp.sum(functools.reduce(jnp.add, tiles), axis=1, keepdims=True)
        inverse = 1.0 / total
        drops = []
        for slot in range(count):
            prob = tiles[slot] * inverse
            keep = kept(seed[0], first_head + head, query_block, first_block + slot, 0)
            signed[head, :, slot * MB : (slot + 1) * MB] = jnp.where(keep, prob, -prob)
            drops.append(bf16(jnp.where(keep, prob * keep_scale, 0.0)))
        attended[:, cols] = bf16(dot(jnp.concatenate(drops, axis=1), values(head)))
        parts = put_parts(parts, lane, 3 * head, top + jnp.log(total))
    stats[...] = parts


def later(table, seed, first_query, first_key, queries, keys, scores, keeps):
    first_head = lax.axis_index("head") * HEADS
    ahead = key_minus_query(1)
    for head in range(HEADS):
        cols = pl.ds(head * DH, DH)
        tiles = dot_last(keys[:, cols], queries[:, cols]) * score_scale
        for block in range(queries.shape[0] // MB):
            across = slice(block * MB, (block + 1) * MB)
            for slot in range(keys.shape[0] // MB):
                down = slice(slot * MB, (slot + 1) * MB)
                bound = bound_of(table, first_query + block, first_key + slot)
                scores[head, down, across] = jnp.where(
                    ahead <= bound, tiles[down, across], hidden
                )
                keep = kept(seed[0], first_head + head, first_query + block, first_key + slot, 1)
                keeps[head, down, across] = jnp.where(keep, jnp.float32(keep_scale), 0.0)


def stacked(*parts):
    def of_head(head):
        cols = slice(head * DH, (head + 1) * DH)
        return jnp.concatenate([ref[rows, cols] for ref, rows in parts], axis=0)

    return of_head


def near_window(key, value, near):
    whole = slice(None)
    keys = ((near, slice(0, ROWS)), (key, whole))
    values = ((near, slice(ROWS, None)), (value, whole))
    return keys, values


def far_window(key, value, near, far):
    keys, values = near_window(key, value, near)
    return ((far, slice(0, MB)), *keys), ((far, slice(MB, None)), *values)


def near_kernel(table, seed, query, key, value, near, signed, attended, stats):
    keys, values = near_window(key, value, near)
    forward(table, seed, 1, query, stacked(*keys), stacked(*values), signed, attended, stats)


def far_kernel(table, seed, query, key, value, near, far, signed, attended, stats):
    keys, values = far_window(key, value, near, far)
    forward(table, seed, 0, query, stacked(*keys), stacked(*values), signed, attended, stats)


def later_kernel(
    table, seed, key, near_query, far_query, near_scores, near_keeps, far_scores, far_keeps
):
    block = lax.axis_index("blk") * 2
    later(table, seed, block + 2, block, near_query, key, near_scores, near_keeps)
    later(table, seed, block + 4, block + 1, far_query, key.at[MB:], far_scores, far_keeps)


def project(total, gathered, weight, core):
    parts, _, width = gathered.shape
    for part in range(parts):
        first = pl.multiple_of((part * 2 + core) * width, width)
        term = dot_last(gathered[part], weight[:, pl.ds(first, width)])
        total = term if total is None else total + term
    return total


def project_kernel(gathered, weight, out):
    out[...] = project(None, gathered, weight, lax.rem(lax.axis_index("head"), 2))


def rows_kernel(
    partial, other, weight, attended_top, attended_low, stats_top, stats_low, near, far
):
    core = lax.rem(lax.axis_index("head"), 2)
    whole = project(partial[...], other, weight, 1 - core)
    lane = lax.broadcasted_iota(jnp.int32, (MB, MB), 1)
    for block, total, attended, stats in (
        (0, whole[0:MB], attended_top, stats_top), (1, whole[MB:], attended_low, stats_low)
    ):
        rows = slice(block * MB, (block + 1) * MB)
        grad = bf16(total)
        near[rows] = grad
        parts = stats[...]
        for head in range(HEADS):
            cols = slice(head * DH, (head + 1) * DH)
            row_dot = jnp.sum(f32(grad[:, cols]) * f32(attended[:, cols]), axis=1, keepdims=True)
            parts = put_parts(parts, lane, 6 + 3 * head, row_dot)
        across = bf16(parts.T[0:EXTRA])
        near[ROWS:, rows] = across
        if block == 0:
            far[0:MB] = grad
        far[MB:, rows] = across


def own_kernel(
    signed_top, signed_low, attended_top, attended_low, query, grad, key, value, near, far,
    grad_query, key_part, value_part,
):
    for head in range(HEADS):
        cols = slice(head * DH, (head + 1) * DH)
        key_sum = value_sum = None
        for block, signed, attended, (keys, values) in (
            (0, signed_top, attended_top, far_window(key, value, near, far)),
            (1, signed_low, attended_low, near_window(key, value, near)),
        ):
            rows = slice(block * MB, (block + 1) * MB)
            grad_head = grad[rows, cols]
            row_dot = jnp.sum(f32(grad_head) * f32(attended[:, cols]), axis=1, keepdims=True)
            grad_prob = dot_last(grad_head, stacked(*values)(head))
            probs = signed[head]
            first = probs.shape[1] - ROWS
            scaled = jnp.where(probs > 0.0, grad_prob * keep_scale, 0.0)
            dscore = bf16(jnp.abs(probs) * (scaled - row_dot))
            dropped = bf16(jnp.maximum(probs[:, first:], 0.0) * keep_scale)
            grad_query[rows, cols] = bf16(dot(dscore, stacked(*keys)(head)) * score_scale)
            key_term = dot_first(dscore[:, first:], query[rows, cols])
            value_term = dot_first(dropped, grad_head)
            key_sum = key_term if key_sum is None else key_sum + key_term
            value_sum = value_term if value_sum is None else value_sum + value_term
        key_part[:, cols] = key_sum
        value_part[:, cols] = value_sum


def finish_kernel(
    near_scores, near_keeps, far_scores, far_keeps, value, near_query, far_query, near_grad,
    far_grad, key_part, value_part, grad_key, grad_value,
):
    for head in range(HEADS):
        cols = pl.ds(head * DH, DH)

        def terms(scores, keeps, values, queries, grads):
            count = queries.shape[0]
            grad_head = grads[0:count, cols]
            stats = f32(grads[count:, 0:count])
            prob = jnp.exp(scores[head] - take_parts(stats, 3 * head))
            keep = keeps[head]
            grad_prob = dot_last(values, grad_head)
            dscore = bf16(prob * (grad_prob * keep - take_parts(stats, 6 + 3 * head)))
            return dot(dscore, queries[:, cols]), dot(bf16(prob * keep), grad_head)

        keys, values = terms(near_scores, near_keeps, value[:, cols], near_query, near_grad)
        far_keys, far_values = terms(far_scores, far_keeps, value[MB:, cols], far_query, far_grad)
        keys = keys + key_part[:, cols]
        values = values + value_part[:, cols]
        grad_key[0:MB, cols] = bf16(keys[0:MB] * score_scale)
        grad_key[MB:, cols] = bf16((keys[MB:] + far_keys) * score_scale)
        grad_value[0:MB, cols] = bf16(values[0:MB])
        grad_value[MB:, cols] = bf16(values[MB:] + far_values)


def call(kernel, specs, outs, microseconds, *args):
    shapes = [jax.ShapeDtypeStruct(shape, dtype) for shape, dtype in outs]
    moved = sum(a.size * a.dtype.itemsize for a in args)
    moved += sum(s.size * s.dtype.itemsize for s in shapes)
    flops = int(microseconds * 1.15e9)
    return pl.pallas_call(
        kernel,
        out_shape=shapes,
        in_specs=specs,
        out_specs=[VMEM] * len(shapes),
        compiler_params=pltpu.CompilerParams(vmem_limit_bytes=16 << 20),
        cost_estimate=pl.CostEstimate(flops=flops, bytes_accessed=moved, transcendentals=0),
    )(*args)


def shifted(value, steps):
    count = lax.axis_size("blk")
    pairs = [(source, source + steps) for source in range(count) if 0 <= source + steps < count]
    return lax.ppermute(value, "blk", pairs)


def other_core(value):
    count = lax.axis_size("head")
    return lax.ppermute(value, "head", [(source, source ^ 1) for source in range(count)])


def on_device(query_rows, key_rows, value_rows, grad_out, out_weight, mask_types, drop_seed):
    half, full = jnp.bfloat16, jnp.float32
    count = lax.axis_size("head")
    groups = [list(range(first, count, 2)) for first in range(2)]

    own_keys, own_grad = lax.optimization_barrier(
        (jnp.concatenate((key_rows, value_rows)), grad_out)
    )
    near_keys = shifted(own_keys, 1)
    copies = jnp.broadcast_to(own_grad[None], (count // 2, *grad_out.shape))
    gathered = lax.all_to_all(copies, "head", 0, 0, axis_index_groups=groups)
    near_query = shifted(query_rows, -1)
    far_keys = shifted(jnp.concatenate((key_rows[MB:], value_rows[MB:])), 2)
    far_query = shifted(query_rows[:MB], -2)
    gathered, near_keys, far_keys, near_query, far_query = lax.optimization_barrier(
        (gathered, near_keys, far_keys, near_query, far_query)
    )

    def outs(keys):
        return [((HEADS, MB, keys), full), ((MB, WIDE), half), ((MB, MB), full)]

    signed_low, attended_low, stats_low = call(
        near_kernel, [SMEM, SMEM] + [VMEM] * 4, outs(WIN - MB), 1.8,
        mask_types, drop_seed, query_rows, key_rows, value_rows, near_keys,
    )
    signed_top, attended_top, stats_top = call(
        far_kernel, [SMEM, SMEM] + [VMEM] * 5, outs(WIN), 2.0,
        mask_types, drop_seed, query_rows, key_rows, value_rows, near_keys, far_keys,
    )
    other = other_core(gathered)
    (partial,) = call(
        project_kernel, [VMEM] * 2, [((ROWS, WIDE), full)], 0.7, gathered, out_weight
    )
    near_rows, far_rows = call(
        rows_kernel,
        [VMEM] * 7,
        [((ROWS + EXTRA, WIDE), half), ((MB + EXTRA, WIDE), half)],
        1.0,
        partial, other, out_weight, attended_top, attended_low, stats_top, stats_low,
    )
    near_grad = shifted(near_rows, -1)
    far_grad = shifted(far_rows, -2)
    grad_query, key_part, value_part = call(
        own_kernel,
        [VMEM] * 10,
        [((ROWS, WIDE), half), ((ROWS, WIDE), full), ((ROWS, WIDE), full)],
        1.7,
        signed_top, signed_low, attended_top, attended_low, query_rows, near_rows, key_rows,
        value_rows, near_keys, far_keys,
    )
    later_key, _ = lax.optimization_barrier((key_rows, near_rows))
    scores = call(
        later_kernel, [SMEM, SMEM] + [VMEM] * 3,
        [((HEADS, ROWS, ROWS), full)] * 2 + [((HEADS, MB, MB), full)] * 2, 2.0,
        mask_types, drop_seed, later_key, near_query, far_query,
    )
    grad_key, grad_value = call(
        finish_kernel,
        [VMEM] * 11,
        [((ROWS, WIDE), half), ((ROWS, WIDE), half)],
        1.3,
        *scores, value_rows, near_query, far_query, near_grad, far_grad, key_part, value_part,
    )
    return (grad_query, grad_key, grad_value)


def solution(mesh):
    split = P("blk", "head")
    return jax.shard_map(
        on_device,
        mesh=mesh,
        in_specs=(split, split, split, split, P("head", None), P(), P()),
        out_specs=(split, split, split),
        check_vma=False,
    )
```

```python
import functools

import jax
import jax.numpy as jnp
from jax import lax
from jax.experimental import pallas as pl
from jax.experimental.pallas import tpu as pltpu
from jax.sharding import PartitionSpec as P

DH = 128
MB = 128
HEADS = 2
ROWS = 256
SLOTS = 5
WIN = SLOTS * MB
FAR = 3 * MB
WIDE = HEADS * DH
STATS = 8

drop_level = 6554
keep_scale = 65536.0 / 58982.0
mix_one = 73244475
mix_two = 295559667
mix_three = 668265263
score_scale = DH**-0.5
hidden = -1e30

VMEM = pl.BlockSpec(memory_space=pltpu.VMEM)
SMEM = pl.BlockSpec(memory_space=pltpu.SMEM)


def bf16(value):
    return value.astype(jnp.bfloat16)


def f32(value):
    return value.astype(jnp.float32)


def dot_last(left, right):
    return lax.dot_general(
        left, right, (((1,), (1,)), ((), ())), preferred_element_type=jnp.float32
    )


def dot_first(left, right):
    return lax.dot_general(
        left, right, (((0,), (0,)), ((), ())), preferred_element_type=jnp.float32
    )


def dot(left, right):
    return jnp.dot(left, right, preferred_element_type=jnp.float32)


def bound_of(table, query_block, key_block):
    last = table.shape[0] - 1
    inside = (key_block >= 0) & (query_block <= last)
    kind = table[jnp.minimum(query_block, last), jnp.maximum(key_block, 0)]
    far = jnp.int32(1 << 20)
    bound = jnp.where(kind == 2, far, jnp.where(kind == 1, (query_block - key_block) * MB, -far))
    return jnp.where(inside, bound, -far)


def kept(seed, head, query_block, key_block, query_axis):
    base = query_block * MB * mix_one + key_block * MB * mix_two + head * mix_three + seed
    rows = lax.broadcasted_iota(jnp.int32, (MB, MB), query_axis) * mix_one
    cols = lax.broadcasted_iota(jnp.int32, (MB, MB), 1 - query_axis) * mix_two
    hashed = (rows + cols) + base
    for _ in range(2):
        hashed = hashed ^ lax.shift_right_logical(hashed, jnp.int32(16))
        hashed = hashed * mix_one
    hashed = hashed ^ lax.shift_right_logical(hashed, jnp.int32(16))
    return (hashed & 65535) >= drop_level


def key_minus_query(query_axis):
    return lax.broadcasted_iota(jnp.int32, (MB, MB), 1 - query_axis) - lax.broadcasted_iota(
        jnp.int32, (MB, MB), query_axis
    )


def forward(table, seed, block, query, keys, values, grad, signed, attended):
    shard = lax.axis_index("blk")
    first_head = lax.axis_index("head") * HEADS
    count = keys(0).shape[0] // MB
    query_block = shard * 2 + block
    first_block = shard * 2 + 2 - count
    ahead = key_minus_query(0)
    lane = lax.broadcasted_iota(jnp.int32, (MB, MB), 1)
    rows = slice(block * MB, (block + 1) * MB)
    stats = jnp.zeros((MB, MB), jnp.float32)
    for head in range(HEADS):
        cols = pl.ds(head * DH, DH)
        scores = dot_last(query[rows, cols], keys(head))
        tiles = []
        for slot in range(count):
            bound = bound_of(table, query_block, first_block + slot)
            tile = scores[:, slot * MB : (slot + 1) * MB] * score_scale
            tiles.append(jnp.where(ahead <= bound, tile, hidden))
        top = functools.reduce(jnp.maximum, tiles)
        top = jnp.max(top, axis=1, keepdims=True)
        tiles = [jnp.exp(tile - top) for tile in tiles]
        total = jnp.sum(functools.reduce(jnp.add, tiles), axis=1, keepdims=True)
        inverse = 1.0 / total
        drops = []
        for slot in range(count):
            prob = tiles[slot] * inverse
            keep = kept(seed[0], first_head + head, query_block, first_block + slot, 0)
            signed[head, :, slot * MB : (slot + 1) * MB] = jnp.where(keep, prob, -prob)
            drops.append(bf16(jnp.where(keep, prob * keep_scale, 0.0)))
        mixed = bf16(dot(jnp.concatenate(drops, axis=1), values(head)))
        attended[rows, cols] = mixed
        row_dot = jnp.sum(f32(grad[rows, cols]) * f32(mixed), axis=1, keepdims=True)
        stats = jnp.where(lane == head, top + jnp.log(total), stats)
        stats = jnp.where(lane == HEADS + head, row_dot, stats)
    return stats.T[0:STATS]


def later(table, seed, first_query, first_key, queries, keys, scores, keeps):
    first_head = lax.axis_index("head") * HEADS
    ahead = key_minus_query(1)
    for head in range(HEADS):
        cols = pl.ds(head * DH, DH)
        tiles = dot_last(keys[:, cols], queries[:, cols]) * score_scale
        for block in range(queries.shape[0] // MB):
            across = slice(block * MB, (block + 1) * MB)
            for slot in range(keys.shape[0] // MB):
                down = slice(slot * MB, (slot + 1) * MB)
                bound = bound_of(table, first_query + block, first_key + slot)
                scores[head, down, across] = jnp.where(
                    ahead <= bound, tiles[down, across], hidden
                )
                keep = kept(seed[0], first_head + head, first_query + block, first_key + slot, 1)
                keeps[head, down, across] = jnp.where(keep, jnp.float32(keep_scale), 0.0)


def stacked(*parts):
    def of_head(head):
        cols = slice(head * DH, (head + 1) * DH)
        return jnp.concatenate([ref[rows, cols] for ref, rows in parts], axis=0)

    return of_head


def near_window(key, value, near):
    whole = slice(None)
    keys = ((near, slice(0, ROWS)), (key, whole))
    values = ((near, slice(ROWS, None)), (value, whole))
    return keys, values


def far_window(key, value, near, far):
    keys, values = near_window(key, value, near)
    return ((far, slice(0, MB)), *keys), ((far, slice(MB, None)), *values)


def forward_kernel(
    table, seed, query, key, value, near, far, grad,
    signed_top, signed_low, attended, near_stats, far_stats,
):
    keys, values = far_window(key, value, near, far)
    stats = forward(
        table, seed, 0, query, stacked(*keys), stacked(*values), grad, signed_top, attended
    )
    near_stats[:, 0:MB] = stats
    far_stats[...] = stats
    keys, values = near_window(key, value, near)
    near_stats[:, MB:] = forward(
        table, seed, 1, query, stacked(*keys), stacked(*values), grad, signed_low, attended
    )


def later_kernel(
    table, seed, key, near_query, far_query, near_scores, near_keeps, far_scores, far_keeps
):
    block = lax.axis_index("blk") * 2
    later(table, seed, block + 2, block, near_query, key, near_scores, near_keeps)
    later(table, seed, block + 4, block + 1, far_query, key.at[MB:], far_scores, far_keeps)


def project(total, gathered, weight, core):
    parts, _, width = gathered.shape
    for part in range(parts):
        first = pl.multiple_of((part * 2 + core) * width, width)
        term = dot_last(gathered[part], weight[:, pl.ds(first, width)])
        total = term if total is None else total + term
    return total


def cut_kernel(weight, out):
    core = lax.rem(lax.axis_index("head"), 2)
    parts = lax.axis_size("head") // 2
    width = out.shape[1] // parts
    for part in range(parts):
        first = pl.multiple_of((part * 2 + 1 - core) * width, width)
        out[:, part * width : (part + 1) * width] = weight[:, pl.ds(first, width)]


def project_other_kernel(gathered, weight, out):
    parts, _, width = gathered.shape
    total = dot_last(gathered[0], weight[:, 0:width])
    for part in range(1, parts):
        total = total + dot_last(gathered[part], weight[:, part * width : (part + 1) * width])
    out[...] = bf16(total)


def project_own_kernel(gathered, weight, out):
    out[...] = project(None, gathered, weight, lax.rem(lax.axis_index("head"), 2))


def rows_kernel(own, received, grad, grad_top):
    whole = bf16(own[...] + f32(received[...]))
    grad[...] = whole
    grad_top[...] = whole[0:MB]


def own_kernel(
    signed_top, signed_low, attended, query, grad, key, value, near, far,
    grad_query, key_part, value_part,
):
    for head in range(HEADS):
        cols = slice(head * DH, (head + 1) * DH)
        key_sum = value_sum = None
        for block, signed, (keys, values) in (
            (0, signed_top, far_window(key, value, near, far)),
            (1, signed_low, near_window(key, value, near)),
        ):
            rows = slice(block * MB, (block + 1) * MB)
            grad_head = grad[rows, cols]
            row_dot = jnp.sum(f32(grad_head) * f32(attended[rows, cols]), axis=1, keepdims=True)
            grad_prob = dot_last(grad_head, stacked(*values)(head))
            probs = signed[head]
            first = probs.shape[1] - ROWS
            scaled = jnp.where(probs > 0.0, grad_prob * keep_scale, 0.0)
            dscore = bf16(jnp.abs(probs) * (scaled - row_dot))
            dropped = bf16(jnp.maximum(probs[:, first:], 0.0) * keep_scale)
            grad_query[rows, cols] = bf16(dot(dscore, stacked(*keys)(head)) * score_scale)
            key_term = dot_first(dscore[:, first:], query[rows, cols])
            value_term = dot_first(dropped, grad_head)
            key_sum = key_term if key_sum is None else key_sum + key_term
            value_sum = value_term if value_sum is None else value_sum + value_term
        key_part[:, cols] = key_sum
        value_part[:, cols] = value_sum


def finish_kernel(
    near_scores, near_keeps, far_scores, far_keeps, value, near_query, far_query, near_grad,
    far_grad, near_stats, far_stats, key_part, value_part, grad_key, grad_value,
):
    for head in range(HEADS):
        cols = pl.ds(head * DH, DH)

        def terms(scores, keeps, values, queries, grads, stats):
            grad_head = grads[:, cols]
            prob = jnp.exp(scores[head] - stats[head : head + 1])
            keep = keeps[head]
            grad_prob = dot_last(values, grad_head)
            dscore = bf16(prob * (grad_prob * keep - stats[HEADS + head : HEADS + head + 1]))
            return dot(dscore, queries[:, cols]), dot(bf16(prob * keep), grad_head)

        keys, values = terms(
            near_scores, near_keeps, value[:, cols], near_query, near_grad, near_stats
        )
        far_keys, far_values = terms(
            far_scores, far_keeps, value[MB:, cols], far_query, far_grad, far_stats
        )
        keys = keys + key_part[:, cols]
        values = values + value_part[:, cols]
        grad_key[0:MB, cols] = bf16(keys[0:MB] * score_scale)
        grad_key[MB:, cols] = bf16((keys[MB:] + far_keys) * score_scale)
        grad_value[0:MB, cols] = bf16(values[0:MB])
        grad_value[MB:, cols] = bf16(values[MB:] + far_values)


def call(kernel, specs, outs, microseconds, *args):
    shapes = [jax.ShapeDtypeStruct(shape, dtype) for shape, dtype in outs]
    moved = sum(a.size * a.dtype.itemsize for a in args)
    moved += sum(s.size * s.dtype.itemsize for s in shapes)
    flops = int(microseconds * 1.15e9)
    return pl.pallas_call(
        kernel,
        out_shape=shapes,
        in_specs=specs,
        out_specs=[VMEM] * len(shapes),
        compiler_params=pltpu.CompilerParams(vmem_limit_bytes=16 << 20),
        cost_estimate=pl.CostEstimate(flops=flops, bytes_accessed=min(moved, flops), transcendentals=0),
    )(*args)


def shifted(value, steps):
    count = lax.axis_size("blk")
    pairs = [(source, source + steps) for source in range(count) if 0 <= source + steps < count]
    return lax.ppermute(value, "blk", pairs)


def other_core(value):
    count = lax.axis_size("head")
    return lax.ppermute(value, "head", [(source, source ^ 1) for source in range(count)])


def on_device(query_rows, key_rows, value_rows, grad_out, out_weight, mask_types, drop_seed):
    half, full = jnp.bfloat16, jnp.float32
    count = lax.axis_size("head")
    groups = [list(range(first, count, 2)) for first in range(2)]

    copies = jnp.broadcast_to(grad_out[None], (count // 2, *grad_out.shape))
    gathered = lax.all_to_all(copies, "head", 0, 0, axis_index_groups=groups)
    near_keys = shifted(jnp.concatenate((key_rows, value_rows)), 1)
    near_query = shifted(query_rows, -1)
    far_keys = shifted(jnp.concatenate((key_rows[MB:], value_rows[MB:])), 2)
    far_query = shifted(query_rows[:MB], -2)

    width = (count // 2) * grad_out.shape[1]
    (theirs,) = call(cut_kernel, [VMEM], [((WIDE, width), half)], 0.0, out_weight)
    other_weight = other_core(theirs)
    gathered, other_weight, far_keys, near_query, far_query = lax.optimization_barrier(
        (gathered, other_weight, far_keys, near_query, far_query)
    )
    (sent,) = call(
        project_other_kernel, [VMEM] * 2, [((ROWS, WIDE), half)], 0.0, gathered, other_weight
    )
    received = other_core(sent)
    (own,) = call(
        project_own_kernel, [VMEM] * 2, [((ROWS, WIDE), full)], 0.0, gathered, out_weight
    )
    grad, grad_top = call(
        rows_kernel, [VMEM] * 2, [((ROWS, WIDE), half), ((MB, WIDE), half)], 0.0, own, received
    )
    near_grad = shifted(grad, -1)
    far_grad = shifted(grad_top, -2)
    signed_top, signed_low, attended, near_sums, far_sums = call(
        forward_kernel,
        [SMEM, SMEM] + [VMEM] * 6,
        [
            ((HEADS, MB, WIN), full),
            ((HEADS, MB, WIN - MB), full),
            ((ROWS, WIDE), half),
            ((STATS, ROWS), full),
            ((STATS, MB), full),
        ],
        0.0,
        mask_types, drop_seed, query_rows, key_rows, value_rows, near_keys, far_keys, grad,
    )
    near_stats = shifted(near_sums, -1)
    far_stats = shifted(far_sums, -2)
    grad_query, key_part, value_part = call(
        own_kernel,
        [VMEM] * 9,
        [((ROWS, WIDE), half), ((ROWS, WIDE), full), ((ROWS, WIDE), full)],
        0.0,
        signed_top, signed_low, attended, query_rows, grad, key_rows, value_rows, near_keys,
        far_keys,
    )
    later_key, _ = lax.optimization_barrier((key_rows, near_sums))
    scores = call(
        later_kernel, [SMEM, SMEM] + [VMEM] * 3,
        [((HEADS, ROWS, ROWS), full)] * 2 + [((HEADS, MB, MB), full)] * 2, 0.0,
        mask_types, drop_seed, later_key, near_query, far_query,
    )
    grad_key, grad_value = call(
        finish_kernel,
        [VMEM] * 13,
        [((ROWS, WIDE), half), ((ROWS, WIDE), half)],
        1.3,
        *scores, value_rows, near_query, far_query, near_grad, far_grad, near_stats, far_stats,
        key_part, value_part,
    )
    return (grad_query, grad_key, grad_value)


def solution(mesh):
    split = P("blk", "head")
    return jax.shard_map(
        on_device,
        mesh=mesh,
        in_specs=(split, split, split, split, P("head", None), P(), P()),
        out_specs=(split, split, split),
        check_vma=False,
    )
```

```python
import functools

import jax
import jax.numpy as jnp
from jax import lax
from jax.experimental import pallas as pl
from jax.experimental.pallas import tpu as pltpu
from jax.sharding import PartitionSpec as P

DH = 128
MB = 128
HEADS = 2
ROWS = 256
SLOTS = 5
WIN = SLOTS * MB
FAR = 3 * MB
WIDE = HEADS * DH
STATS = 8

drop_level = 6554
keep_scale = 65536.0 / 58982.0
mix_one = 73244475
mix_two = 295559667
mix_three = 668265263
score_scale = DH**-0.5
hidden = -1e30

VMEM = pl.BlockSpec(memory_space=pltpu.VMEM)
SMEM = pl.BlockSpec(memory_space=pltpu.SMEM)


def bf16(value):
    return value.astype(jnp.bfloat16)


def f32(value):
    return value.astype(jnp.float32)


def dot_last(left, right):
    return lax.dot_general(
        left, right, (((1,), (1,)), ((), ())), preferred_element_type=jnp.float32
    )


def dot_first(left, right):
    return lax.dot_general(
        left, right, (((0,), (0,)), ((), ())), preferred_element_type=jnp.float32
    )


def dot(left, right):
    return jnp.dot(left, right, preferred_element_type=jnp.float32)


def bound_of(table, query_block, key_block):
    last = table.shape[0] - 1
    inside = (key_block >= 0) & (query_block <= last)
    kind = table[jnp.minimum(query_block, last), jnp.maximum(key_block, 0)]
    far = jnp.int32(1 << 20)
    bound = jnp.where(kind == 2, far, jnp.where(kind == 1, (query_block - key_block) * MB, -far))
    return jnp.where(inside, bound, -far)


def kept(seed, head, query_block, key_block, query_axis):
    base = query_block * MB * mix_one + key_block * MB * mix_two + head * mix_three + seed
    rows = lax.broadcasted_iota(jnp.int32, (MB, MB), query_axis) * mix_one
    cols = lax.broadcasted_iota(jnp.int32, (MB, MB), 1 - query_axis) * mix_two
    hashed = (rows + cols) + base
    for _ in range(2):
        hashed = hashed ^ lax.shift_right_logical(hashed, jnp.int32(16))
        hashed = hashed * mix_one
    hashed = hashed ^ lax.shift_right_logical(hashed, jnp.int32(16))
    return (hashed & 65535) >= drop_level


def key_minus_query(query_axis):
    return lax.broadcasted_iota(jnp.int32, (MB, MB), 1 - query_axis) - lax.broadcasted_iota(
        jnp.int32, (MB, MB), query_axis
    )


def forward(table, seed, block, query, keys, values, grad, signed, attended):
    shard = lax.axis_index("blk")
    first_head = lax.axis_index("head") * HEADS
    count = keys(0).shape[0] // MB
    query_block = shard * 2 + block
    first_block = shard * 2 + 2 - count
    ahead = key_minus_query(0)
    lane = lax.broadcasted_iota(jnp.int32, (MB, MB), 1)
    rows = slice(block * MB, (block + 1) * MB)
    stats = jnp.zeros((MB, MB), jnp.float32)
    for head in range(HEADS):
        cols = pl.ds(head * DH, DH)
        scores = dot_last(query[rows, cols], keys(head))
        tiles = []
        for slot in range(count):
            bound = bound_of(table, query_block, first_block + slot)
            tile = scores[:, slot * MB : (slot + 1) * MB] * score_scale
            tiles.append(jnp.where(ahead <= bound, tile, hidden))
        top = functools.reduce(jnp.maximum, tiles)
        top = jnp.max(top, axis=1, keepdims=True)
        tiles = [jnp.exp(tile - top) for tile in tiles]
        total = jnp.sum(functools.reduce(jnp.add, tiles), axis=1, keepdims=True)
        inverse = 1.0 / total
        drops = []
        for slot in range(count):
            prob = tiles[slot] * inverse
            keep = kept(seed[0], first_head + head, query_block, first_block + slot, 0)
            signed[head, :, slot * MB : (slot + 1) * MB] = jnp.where(keep, prob, -prob)
            drops.append(bf16(jnp.where(keep, prob * keep_scale, 0.0)))
        mixed = bf16(dot(jnp.concatenate(drops, axis=1), values(head)))
        attended[rows, cols] = mixed
        row_dot = jnp.sum(f32(grad[rows, cols]) * f32(mixed), axis=1, keepdims=True)
        stats = jnp.where(lane == head, top + jnp.log(total), stats)
        stats = jnp.where(lane == HEADS + head, row_dot, stats)
    return stats.T[0:STATS]


def later(table, seed, first_query, first_key, queries, keys, scores, keeps):
    first_head = lax.axis_index("head") * HEADS
    ahead = key_minus_query(1)
    for head in range(HEADS):
        cols = pl.ds(head * DH, DH)
        tiles = dot_last(keys[:, cols], queries[:, cols]) * score_scale
        for block in range(queries.shape[0] // MB):
            across = slice(block * MB, (block + 1) * MB)
            for slot in range(keys.shape[0] // MB):
                down = slice(slot * MB, (slot + 1) * MB)
                bound = bound_of(table, first_query + block, first_key + slot)
                scores[head, down, across] = jnp.where(
                    ahead <= bound, tiles[down, across], hidden
                )
                keep = kept(seed[0], first_head + head, first_query + block, first_key + slot, 1)
                keeps[head, down, across] = jnp.where(keep, jnp.float32(keep_scale), 0.0)


def stacked(*parts):
    def of_head(head):
        cols = slice(head * DH, (head + 1) * DH)
        return jnp.concatenate([ref[rows, cols] for ref, rows in parts], axis=0)

    return of_head


def near_window(key, value, near):
    whole = slice(None)
    keys = ((near, slice(0, ROWS)), (key, whole))
    values = ((near, slice(ROWS, None)), (value, whole))
    return keys, values


def far_window(key, value, near, far):
    keys, values = near_window(key, value, near)
    return ((far, slice(0, MB)), *keys), ((far, slice(MB, None)), *values)


def forward_kernel(
    table, seed, query, key, value, near, far, grad,
    signed_top, signed_low, attended, near_stats, far_stats,
):
    keys, values = far_window(key, value, near, far)
    stats = forward(
        table, seed, 0, query, stacked(*keys), stacked(*values), grad, signed_top, attended
    )
    near_stats[:, 0:MB] = stats
    far_stats[...] = stats
    keys, values = near_window(key, value, near)
    near_stats[:, MB:] = forward(
        table, seed, 1, query, stacked(*keys), stacked(*values), grad, signed_low, attended
    )


def later_kernel(
    table, seed, key, near_query, far_query, near_scores, near_keeps, far_scores, far_keeps
):
    block = lax.axis_index("blk") * 2
    later(table, seed, block + 2, block, near_query, key, near_scores, near_keeps)
    later(table, seed, block + 4, block + 1, far_query, key.at[MB:], far_scores, far_keeps)


def project(total, gathered, weight, core):
    parts, _, width = gathered.shape
    for part in range(parts):
        first = pl.multiple_of((part * 2 + core) * width, width)
        term = dot_last(gathered[part], weight[:, pl.ds(first, width)])
        total = term if total is None else total + term
    return total


def cut_kernel(weight, out):
    core = lax.rem(lax.axis_index("head"), 2)
    parts = lax.axis_size("head") // 2
    width = out.shape[1] // parts
    for part in range(parts):
        first = pl.multiple_of((part * 2 + 1 - core) * width, width)
        out[:, part * width : (part + 1) * width] = weight[:, pl.ds(first, width)]


def project_other_kernel(gathered, weight, out):
    parts, _, width = gathered.shape
    total = dot_last(gathered[0], weight[:, 0:width])
    for part in range(1, parts):
        total = total + dot_last(gathered[part], weight[:, part * width : (part + 1) * width])
    out[...] = bf16(total)


def project_own_kernel(gathered, weight, out):
    out[...] = project(None, gathered, weight, lax.rem(lax.axis_index("head"), 2))


def rows_kernel(own, received, grad, grad_top):
    whole = bf16(own[...] + f32(received[...]))
    grad[...] = whole
    grad_top[...] = whole[0:MB]


def own_kernel(
    signed_top, signed_low, attended, query, grad, key, value, near, far,
    grad_query, key_part, value_part,
):
    for head in range(HEADS):
        cols = slice(head * DH, (head + 1) * DH)
        key_sum = value_sum = None
        for block, signed, (keys, values) in (
            (0, signed_top, far_window(key, value, near, far)),
            (1, signed_low, near_window(key, value, near)),
        ):
            rows = slice(block * MB, (block + 1) * MB)
            grad_head = grad[rows, cols]
            row_dot = jnp.sum(f32(grad_head) * f32(attended[rows, cols]), axis=1, keepdims=True)
            grad_prob = dot_last(grad_head, stacked(*values)(head))
            probs = signed[head]
            first = probs.shape[1] - ROWS
            scaled = jnp.where(probs > 0.0, grad_prob * keep_scale, 0.0)
            dscore = bf16(jnp.abs(probs) * (scaled - row_dot))
            dropped = bf16(jnp.maximum(probs[:, first:], 0.0) * keep_scale)
            grad_query[rows, cols] = bf16(dot(dscore, stacked(*keys)(head)) * score_scale)
            key_term = dot_first(dscore[:, first:], query[rows, cols])
            value_term = dot_first(dropped, grad_head)
            key_sum = key_term if key_sum is None else key_sum + key_term
            value_sum = value_term if value_sum is None else value_sum + value_term
        key_part[:, cols] = key_sum
        value_part[:, cols] = value_sum


def finish_kernel(
    near_scores, near_keeps, far_scores, far_keeps, value, near_query, far_query, near_grad,
    far_grad, near_stats, far_stats, key_part, value_part, grad_key, grad_value,
):
    for head in range(HEADS):
        cols = pl.ds(head * DH, DH)

        def terms(scores, keeps, values, queries, grads, stats):
            grad_head = grads[:, cols]
            prob = jnp.exp(scores[head] - stats[head : head + 1])
            keep = keeps[head]
            grad_prob = dot_last(values, grad_head)
            dscore = bf16(prob * (grad_prob * keep - stats[HEADS + head : HEADS + head + 1]))
            return dot(dscore, queries[:, cols]), dot(bf16(prob * keep), grad_head)

        keys, values = terms(
            near_scores, near_keeps, value[:, cols], near_query, near_grad, near_stats
        )
        far_keys, far_values = terms(
            far_scores, far_keeps, value[MB:, cols], far_query, far_grad, far_stats
        )
        keys = keys + key_part[:, cols]
        values = values + value_part[:, cols]
        grad_key[0:MB, cols] = bf16(keys[0:MB] * score_scale)
        grad_key[MB:, cols] = bf16((keys[MB:] + far_keys) * score_scale)
        grad_value[0:MB, cols] = bf16(values[0:MB])
        grad_value[MB:, cols] = bf16(values[MB:] + far_values)


def call(kernel, specs, outs, microseconds, *args):
    shapes = [jax.ShapeDtypeStruct(shape, dtype) for shape, dtype in outs]
    moved = sum(a.size * a.dtype.itemsize for a in args)
    moved += sum(s.size * s.dtype.itemsize for s in shapes)
    flops = int(microseconds * 1.15e9)
    return pl.pallas_call(
        kernel,
        out_shape=shapes,
        in_specs=specs,
        out_specs=[VMEM] * len(shapes),
        compiler_params=pltpu.CompilerParams(vmem_limit_bytes=16 << 20),
        cost_estimate=pl.CostEstimate(flops=flops, bytes_accessed=min(moved, flops), transcendentals=0),
    )(*args)


def shifted(value, steps):
    count = lax.axis_size("blk")
    pairs = [(source, source + steps) for source in range(count) if 0 <= source + steps < count]
    return lax.ppermute(value, "blk", pairs)


def other_core(value):
    count = lax.axis_size("head")
    return lax.ppermute(value, "head", [(source, source ^ 1) for source in range(count)])


def on_device(query_rows, key_rows, value_rows, grad_out, out_weight, mask_types, drop_seed):
    half, full = jnp.bfloat16, jnp.float32
    count = lax.axis_size("head")
    groups = [list(range(first, count, 2)) for first in range(2)]

    copies = jnp.broadcast_to(grad_out[None], (count // 2, *grad_out.shape))
    gathered = lax.all_to_all(copies, "head", 0, 0, axis_index_groups=groups)
    near_query = shifted(query_rows, -1)
    far_keys = shifted(jnp.concatenate((key_rows[MB:], value_rows[MB:])), 2)
    far_query = shifted(query_rows[:MB], -2)

    width = (count // 2) * grad_out.shape[1]
    (theirs,) = call(cut_kernel, [VMEM], [((WIDE, width), half)], 0.0, out_weight)
    other_weight = other_core(theirs)
    own_keys = jnp.concatenate((key_rows, value_rows))
    gathered, other_weight, far_keys, near_query, far_query, own_keys = lax.optimization_barrier(
        (gathered, other_weight, far_keys, near_query, far_query, own_keys)
    )
    near_keys = shifted(own_keys, 1)
    (sent,) = call(
        project_other_kernel, [VMEM] * 2, [((ROWS, WIDE), half)], 0.0, gathered, other_weight
    )
    received = other_core(sent)
    (own,) = call(
        project_own_kernel, [VMEM] * 2, [((ROWS, WIDE), full)], 0.0, gathered, out_weight
    )
    grad, grad_top = call(
        rows_kernel, [VMEM] * 2, [((ROWS, WIDE), half), ((MB, WIDE), half)], 0.0, own, received
    )
    near_grad = shifted(grad, -1)
    far_grad = shifted(grad_top, -2)
    signed_top, signed_low, attended, near_sums, far_sums = call(
        forward_kernel,
        [SMEM, SMEM] + [VMEM] * 6,
        [
            ((HEADS, MB, WIN), full),
            ((HEADS, MB, WIN - MB), full),
            ((ROWS, WIDE), half),
            ((STATS, ROWS), full),
            ((STATS, MB), full),
        ],
        0.0,
        mask_types, drop_seed, query_rows, key_rows, value_rows, near_keys, far_keys, grad,
    )
    near_stats = shifted(near_sums, -1)
    far_stats = shifted(far_sums, -2)
    grad_query, key_part, value_part = call(
        own_kernel,
        [VMEM] * 9,
        [((ROWS, WIDE), half), ((ROWS, WIDE), full), ((ROWS, WIDE), full)],
        0.0,
        signed_top, signed_low, attended, query_rows, grad, key_rows, value_rows, near_keys,
        far_keys,
    )
    later_key, _ = lax.optimization_barrier((key_rows, near_sums))
    scores = call(
        later_kernel, [SMEM, SMEM] + [VMEM] * 3,
        [((HEADS, ROWS, ROWS), full)] * 2 + [((HEADS, MB, MB), full)] * 2, 0.0,
        mask_types, drop_seed, later_key, near_query, far_query,
    )
    grad_key, grad_value = call(
        finish_kernel,
        [VMEM] * 13,
        [((ROWS, WIDE), half), ((ROWS, WIDE), half)],
        1.3,
        *scores, value_rows, near_query, far_query, near_grad, far_grad, near_stats, far_stats,
        key_part, value_part,
    )
    return (grad_query, grad_key, grad_value)


def solution(mesh):
    split = P("blk", "head")
    return jax.shard_map(
        on_device,
        mesh=mesh,
        in_specs=(split, split, split, split, P("head", None), P(), P()),
        out_specs=(split, split, split),
        check_vma=False,
    )
```

```python
import functools

import jax
import jax.numpy as jnp
from jax import lax
from jax.experimental import pallas as pl
from jax.experimental.pallas import tpu as pltpu
from jax.sharding import PartitionSpec as P

DH = 128
MB = 128
HEADS = 2
ROWS = 256
SLOTS = 5
WIN = SLOTS * MB
FAR = 3 * MB
WIDE = HEADS * DH
STATS = 8

drop_level = 6554
keep_scale = 65536.0 / 58982.0
mix_one = 73244475
mix_two = 295559667
mix_three = 668265263
score_scale = DH**-0.5
hidden = -1e30

VMEM = pl.BlockSpec(memory_space=pltpu.VMEM)
SMEM = pl.BlockSpec(memory_space=pltpu.SMEM)


def bf16(value):
    return value.astype(jnp.bfloat16)


def f32(value):
    return value.astype(jnp.float32)


def dot_last(left, right):
    return lax.dot_general(
        left, right, (((1,), (1,)), ((), ())), preferred_element_type=jnp.float32
    )


def dot_first(left, right):
    return lax.dot_general(
        left, right, (((0,), (0,)), ((), ())), preferred_element_type=jnp.float32
    )


def dot(left, right):
    return jnp.dot(left, right, preferred_element_type=jnp.float32)


def bound_of(table, query_block, key_block):
    last = table.shape[0] - 1
    inside = (key_block >= 0) & (query_block <= last)
    kind = table[jnp.minimum(query_block, last), jnp.maximum(key_block, 0)]
    far = jnp.int32(1 << 20)
    bound = jnp.where(kind == 2, far, jnp.where(kind == 1, (query_block - key_block) * MB, -far))
    return jnp.where(inside, bound, -far)


def kept(seed, head, query_block, key_block, query_axis):
    base = query_block * MB * mix_one + key_block * MB * mix_two + head * mix_three + seed
    rows = lax.broadcasted_iota(jnp.int32, (MB, MB), query_axis) * mix_one
    cols = lax.broadcasted_iota(jnp.int32, (MB, MB), 1 - query_axis) * mix_two
    hashed = (rows + cols) + base
    for _ in range(2):
        hashed = hashed ^ lax.shift_right_logical(hashed, jnp.int32(16))
        hashed = hashed * mix_one
    hashed = hashed ^ lax.shift_right_logical(hashed, jnp.int32(16))
    return (hashed & 65535) >= drop_level


def key_minus_query(query_axis):
    return lax.broadcasted_iota(jnp.int32, (MB, MB), 1 - query_axis) - lax.broadcasted_iota(
        jnp.int32, (MB, MB), query_axis
    )


def forward(table, seed, block, query, keys, values, grad, signed, attended):
    shard = lax.axis_index("blk")
    first_head = lax.axis_index("head") * HEADS
    count = keys(0).shape[0] // MB
    query_block = shard * 2 + block
    first_block = shard * 2 + 2 - count
    ahead = key_minus_query(0)
    lane = lax.broadcasted_iota(jnp.int32, (MB, MB), 1)
    rows = slice(block * MB, (block + 1) * MB)
    stats = jnp.zeros((MB, MB), jnp.float32)
    for head in range(HEADS):
        cols = pl.ds(head * DH, DH)
        scores = dot_last(query[rows, cols], keys(head))
        tiles = []
        for slot in range(count):
            bound = bound_of(table, query_block, first_block + slot)
            tile = scores[:, slot * MB : (slot + 1) * MB] * score_scale
            tiles.append(jnp.where(ahead <= bound, tile, hidden))
        top = functools.reduce(jnp.maximum, tiles)
        top = jnp.max(top, axis=1, keepdims=True)
        tiles = [jnp.exp(tile - top) for tile in tiles]
        total = jnp.sum(functools.reduce(jnp.add, tiles), axis=1, keepdims=True)
        inverse = 1.0 / total
        drops = []
        for slot in range(count):
            prob = tiles[slot] * inverse
            keep = kept(seed[0], first_head + head, query_block, first_block + slot, 0)
            signed[head, :, slot * MB : (slot + 1) * MB] = jnp.where(keep, prob, -prob)
            drops.append(bf16(jnp.where(keep, prob * keep_scale, 0.0)))
        mixed = bf16(dot(jnp.concatenate(drops, axis=1), values(head)))
        attended[rows, cols] = mixed
        row_dot = jnp.sum(f32(grad[rows, cols]) * f32(mixed), axis=1, keepdims=True)
        stats = jnp.where(lane == head, top + jnp.log(total), stats)
        stats = jnp.where(lane == HEADS + head, row_dot, stats)
    return stats.T[0:STATS]


def later(table, seed, first_query, first_key, queries, keys, scores, keeps):
    first_head = lax.axis_index("head") * HEADS
    ahead = key_minus_query(1)
    for head in range(HEADS):
        cols = pl.ds(head * DH, DH)
        tiles = dot_last(keys[:, cols], queries[:, cols]) * score_scale
        for block in range(queries.shape[0] // MB):
            across = slice(block * MB, (block + 1) * MB)
            for slot in range(keys.shape[0] // MB):
                down = slice(slot * MB, (slot + 1) * MB)
                bound = bound_of(table, first_query + block, first_key + slot)
                scores[head, down, across] = jnp.where(
                    ahead <= bound, tiles[down, across], hidden
                )
                keep = kept(seed[0], first_head + head, first_query + block, first_key + slot, 1)
                keeps[head, down, across] = jnp.where(keep, jnp.float32(keep_scale), 0.0)


def stacked(*parts):
    def of_head(head):
        cols = slice(head * DH, (head + 1) * DH)
        return jnp.concatenate([ref[rows, cols] for ref, rows in parts], axis=0)

    return of_head


def near_window(key, value, near):
    whole = slice(None)
    keys = ((near, slice(0, ROWS)), (key, whole))
    values = ((near, slice(ROWS, None)), (value, whole))
    return keys, values


def far_window(key, value, near, far):
    keys, values = near_window(key, value, near)
    return ((far, slice(0, MB)), *keys), ((far, slice(MB, None)), *values)


def forward_kernel(
    table, seed, query, key, value, near, far, grad,
    signed_top, signed_low, attended, near_stats, far_stats,
):
    keys, values = far_window(key, value, near, far)
    stats = forward(
        table, seed, 0, query, stacked(*keys), stacked(*values), grad, signed_top, attended
    )
    near_stats[:, 0:MB] = stats
    far_stats[...] = stats
    keys, values = near_window(key, value, near)
    near_stats[:, MB:] = forward(
        table, seed, 1, query, stacked(*keys), stacked(*values), grad, signed_low, attended
    )


def later_kernel(
    table, seed, key, near_query, far_query, near_scores, near_keeps, far_scores, far_keeps
):
    block = lax.axis_index("blk") * 2
    later(table, seed, block + 2, block, near_query, key, near_scores, near_keeps)
    later(table, seed, block + 4, block + 1, far_query, key.at[MB:], far_scores, far_keeps)


def project(total, gathered, weight, core):
    parts, _, width = gathered.shape
    for part in range(parts):
        first = pl.multiple_of((part * 2 + core) * width, width)
        term = dot_last(gathered[part], weight[:, pl.ds(first, width)])
        total = term if total is None else total + term
    return total


def cut_kernel(weight, out):
    core = lax.rem(lax.axis_index("head"), 2)
    parts = lax.axis_size("head") // 2
    width = out.shape[1] // parts
    for part in range(parts):
        first = pl.multiple_of((part * 2 + 1 - core) * width, width)
        out[:, part * width : (part + 1) * width] = weight[:, pl.ds(first, width)]


def project_other_kernel(gathered, weight, out):
    parts, _, width = gathered.shape
    total = dot_last(gathered[0], weight[:, 0:width])
    for part in range(1, parts):
        total = total + dot_last(gathered[part], weight[:, part * width : (part + 1) * width])
    out[...] = bf16(total)


def project_own_kernel(gathered, weight, out):
    out[...] = project(None, gathered, weight, lax.rem(lax.axis_index("head"), 2))


def rows_kernel(own, received, grad, grad_top):
    whole = bf16(own[...] + f32(received[...]))
    grad[...] = whole
    grad_top[...] = whole[0:MB]


def own_kernel(
    signed_top, signed_low, attended, query, grad, key, value, near, far,
    grad_query, key_part, value_part,
):
    for head in range(HEADS):
        cols = slice(head * DH, (head + 1) * DH)
        key_sum = value_sum = None
        for block, signed, (keys, values) in (
            (0, signed_top, far_window(key, value, near, far)),
            (1, signed_low, near_window(key, value, near)),
        ):
            rows = slice(block * MB, (block + 1) * MB)
            grad_head = grad[rows, cols]
            row_dot = jnp.sum(f32(grad_head) * f32(attended[rows, cols]), axis=1, keepdims=True)
            grad_prob = dot_last(grad_head, stacked(*values)(head))
            probs = signed[head]
            first = probs.shape[1] - ROWS
            scaled = jnp.where(probs > 0.0, grad_prob * keep_scale, 0.0)
            dscore = bf16(jnp.abs(probs) * (scaled - row_dot))
            dropped = bf16(jnp.maximum(probs[:, first:], 0.0) * keep_scale)
            grad_query[rows, cols] = bf16(dot(dscore, stacked(*keys)(head)) * score_scale)
            key_term = dot_first(dscore[:, first:], query[rows, cols])
            value_term = dot_first(dropped, grad_head)
            key_sum = key_term if key_sum is None else key_sum + key_term
            value_sum = value_term if value_sum is None else value_sum + value_term
        key_part[:, cols] = key_sum
        value_part[:, cols] = value_sum


def finish_kernel(
    near_scores, near_keeps, far_scores, far_keeps, value, near_query, far_query, near_grad,
    far_grad, near_stats, far_stats, key_part, value_part, grad_key, grad_value,
):
    for head in range(HEADS):
        cols = pl.ds(head * DH, DH)

        def terms(scores, keeps, values, queries, grads, stats):
            grad_head = grads[:, cols]
            prob = jnp.exp(scores[head] - stats[head : head + 1])
            keep = keeps[head]
            grad_prob = dot_last(values, grad_head)
            dscore = bf16(prob * (grad_prob * keep - stats[HEADS + head : HEADS + head + 1]))
            return dot(dscore, queries[:, cols]), dot(bf16(prob * keep), grad_head)

        keys, values = terms(
            near_scores, near_keeps, value[:, cols], near_query, near_grad, near_stats
        )
        far_keys, far_values = terms(
            far_scores, far_keeps, value[MB:, cols], far_query, far_grad, far_stats
        )
        keys = keys + key_part[:, cols]
        values = values + value_part[:, cols]
        grad_key[0:MB, cols] = bf16(keys[0:MB] * score_scale)
        grad_key[MB:, cols] = bf16((keys[MB:] + far_keys) * score_scale)
        grad_value[0:MB, cols] = bf16(values[0:MB])
        grad_value[MB:, cols] = bf16(values[MB:] + far_values)


def call(kernel, specs, outs, microseconds, *args):
    shapes = [jax.ShapeDtypeStruct(shape, dtype) for shape, dtype in outs]
    moved = sum(a.size * a.dtype.itemsize for a in args)
    moved += sum(s.size * s.dtype.itemsize for s in shapes)
    flops = int(microseconds * 1.15e9)
    return pl.pallas_call(
        kernel,
        out_shape=shapes,
        in_specs=specs,
        out_specs=[VMEM] * len(shapes),
        compiler_params=pltpu.CompilerParams(vmem_limit_bytes=16 << 20),
        cost_estimate=pl.CostEstimate(flops=flops, bytes_accessed=min(moved, flops), transcendentals=0),
    )(*args)


def shifted(value, steps):
    count = lax.axis_size("blk")
    pairs = [(source, source + steps) for source in range(count) if 0 <= source + steps < count]
    return lax.ppermute(value, "blk", pairs)


def other_core(value):
    count = lax.axis_size("head")
    return lax.ppermute(value, "head", [(source, source ^ 1) for source in range(count)])


def on_device(query_rows, key_rows, value_rows, grad_out, out_weight, mask_types, drop_seed):
    half, full = jnp.bfloat16, jnp.float32
    count = lax.axis_size("head")
    groups = [list(range(first, count, 2)) for first in range(2)]

    copies = jnp.broadcast_to(grad_out[None], (count // 2, *grad_out.shape))
    gathered = lax.all_to_all(copies, "head", 0, 0, axis_index_groups=groups)
    near_query = shifted(query_rows, -1)
    far_keys = shifted(jnp.concatenate((key_rows[MB:], value_rows[MB:])), 2)
    far_query = shifted(query_rows[:MB], -2)

    width = (count // 2) * grad_out.shape[1]
    (theirs,) = call(cut_kernel, [VMEM], [((WIDE, width), half)], 0.0, out_weight)
    other_weight = other_core(theirs)
    own_keys = jnp.concatenate((key_rows, value_rows))
    far_keys, near_query, far_query, own_keys = lax.optimization_barrier(
        (far_keys, near_query, far_query, own_keys)
    )
    near_keys = shifted(own_keys, 1)
    gathered, other_weight, far_keys = lax.optimization_barrier(
        (gathered, other_weight, far_keys)
    )
    (sent,) = call(
        project_other_kernel, [VMEM] * 2, [((ROWS, WIDE), half)], 0.0, gathered, other_weight
    )
    received = other_core(sent)
    (own,) = call(
        project_own_kernel, [VMEM] * 2, [((ROWS, WIDE), full)], 0.0, gathered, out_weight
    )
    grad, grad_top = call(
        rows_kernel, [VMEM] * 2, [((ROWS, WIDE), half), ((MB, WIDE), half)], 0.0, own, received
    )
    near_grad = shifted(grad, -1)
    far_grad = shifted(grad_top, -2)
    signed_top, signed_low, attended, near_sums, far_sums = call(
        forward_kernel,
        [SMEM, SMEM] + [VMEM] * 6,
        [
            ((HEADS, MB, WIN), full),
            ((HEADS, MB, WIN - MB), full),
            ((ROWS, WIDE), half),
            ((STATS, ROWS), full),
            ((STATS, MB), full),
        ],
        0.0,
        mask_types, drop_seed, query_rows, key_rows, value_rows, near_keys, far_keys, grad,
    )
    near_stats = shifted(near_sums, -1)
    far_stats = shifted(far_sums, -2)
    grad_query, key_part, value_part = call(
        own_kernel,
        [VMEM] * 9,
        [((ROWS, WIDE), half), ((ROWS, WIDE), full), ((ROWS, WIDE), full)],
        0.0,
        signed_top, signed_low, attended, query_rows, grad, key_rows, value_rows, near_keys,
        far_keys,
    )
    later_key, _ = lax.optimization_barrier((key_rows, near_sums))
    scores = call(
        later_kernel, [SMEM, SMEM] + [VMEM] * 3,
        [((HEADS, ROWS, ROWS), full)] * 2 + [((HEADS, MB, MB), full)] * 2, 0.0,
        mask_types, drop_seed, later_key, near_query, far_query,
    )
    grad_key, grad_value = call(
        finish_kernel,
        [VMEM] * 13,
        [((ROWS, WIDE), half), ((ROWS, WIDE), half)],
        1.3,
        *scores, value_rows, near_query, far_query, near_grad, far_grad, near_stats, far_stats,
        key_part, value_part,
    )
    return (grad_query, grad_key, grad_value)


def solution(mesh):
    split = P("blk", "head")
    return jax.shard_map(
        on_device,
        mesh=mesh,
        in_specs=(split, split, split, split, P("head", None), P(), P()),
        out_specs=(split, split, split),
        check_vma=False,
    )
```

```python
import functools

import jax
import jax.numpy as jnp
from jax import lax
from jax.experimental import pallas as pl
from jax.experimental.pallas import tpu as pltpu
from jax.sharding import PartitionSpec as P

DH = 128
MB = 128
HEADS = 2
ROWS = 256
SLOTS = 5
WIN = SLOTS * MB
FAR = 3 * MB
WIDE = HEADS * DH
STATS = 8

drop_level = 6554
keep_scale = 65536.0 / 58982.0
mix_one = 73244475
mix_two = 295559667
mix_three = 668265263
score_scale = DH**-0.5
hidden = -1e30

VMEM = pl.BlockSpec(memory_space=pltpu.VMEM)
SMEM = pl.BlockSpec(memory_space=pltpu.SMEM)


def bf16(value):
    return value.astype(jnp.bfloat16)


def f32(value):
    return value.astype(jnp.float32)


def dot_last(left, right):
    return lax.dot_general(
        left, right, (((1,), (1,)), ((), ())), preferred_element_type=jnp.float32
    )


def dot_first(left, right):
    return lax.dot_general(
        left, right, (((0,), (0,)), ((), ())), preferred_element_type=jnp.float32
    )


def dot(left, right):
    return jnp.dot(left, right, preferred_element_type=jnp.float32)


def bound_of(table, query_block, key_block):
    last = table.shape[0] - 1
    inside = (key_block >= 0) & (query_block <= last)
    kind = table[jnp.minimum(query_block, last), jnp.maximum(key_block, 0)]
    far = jnp.int32(1 << 20)
    bound = jnp.where(kind == 2, far, jnp.where(kind == 1, (query_block - key_block) * MB, -far))
    return jnp.where(inside, bound, -far)


def kept(seed, head, query_block, key_block, query_axis):
    base = query_block * MB * mix_one + key_block * MB * mix_two + head * mix_three + seed
    rows = lax.broadcasted_iota(jnp.int32, (MB, MB), query_axis) * mix_one
    cols = lax.broadcasted_iota(jnp.int32, (MB, MB), 1 - query_axis) * mix_two
    hashed = (rows + cols) + base
    for _ in range(2):
        hashed = hashed ^ lax.shift_right_logical(hashed, jnp.int32(16))
        hashed = hashed * mix_one
    hashed = hashed ^ lax.shift_right_logical(hashed, jnp.int32(16))
    return (hashed & 65535) >= drop_level


def key_minus_query(query_axis):
    return lax.broadcasted_iota(jnp.int32, (MB, MB), 1 - query_axis) - lax.broadcasted_iota(
        jnp.int32, (MB, MB), query_axis
    )


def forward(table, seed, block, query, keys, values, grad, signed, attended):
    shard = lax.axis_index("blk")
    first_head = lax.axis_index("head") * HEADS
    count = keys(0).shape[0] // MB
    query_block = shard * 2 + block
    first_block = shard * 2 + 2 - count
    ahead = key_minus_query(0)
    lane = lax.broadcasted_iota(jnp.int32, (MB, MB), 1)
    rows = slice(block * MB, (block + 1) * MB)
    stats = jnp.zeros((MB, MB), jnp.float32)
    for head in range(HEADS):
        cols = pl.ds(head * DH, DH)
        scores = dot_last(query[rows, cols], keys(head))
        tiles = []
        for slot in range(count):
            bound = bound_of(table, query_block, first_block + slot)
            tile = scores[:, slot * MB : (slot + 1) * MB] * score_scale
            tiles.append(jnp.where(ahead <= bound, tile, hidden))
        top = functools.reduce(jnp.maximum, tiles)
        top = jnp.max(top, axis=1, keepdims=True)
        tiles = [jnp.exp(tile - top) for tile in tiles]
        total = jnp.sum(functools.reduce(jnp.add, tiles), axis=1, keepdims=True)
        inverse = 1.0 / total
        drops = []
        for slot in range(count):
            prob = tiles[slot] * inverse
            keep = kept(seed[0], first_head + head, query_block, first_block + slot, 0)
            signed[head, :, slot * MB : (slot + 1) * MB] = jnp.where(keep, prob, -prob)
            drops.append(bf16(jnp.where(keep, prob * keep_scale, 0.0)))
        mixed = bf16(dot(jnp.concatenate(drops, axis=1), values(head)))
        attended[rows, cols] = mixed
        row_dot = jnp.sum(f32(grad[rows, cols]) * f32(mixed), axis=1, keepdims=True)
        stats = jnp.where(lane == head, top + jnp.log(total), stats)
        stats = jnp.where(lane == HEADS + head, row_dot, stats)
    return stats.T[0:STATS]


def later(table, seed, first_query, first_key, queries, keys, scores, keeps):
    first_head = lax.axis_index("head") * HEADS
    ahead = key_minus_query(1)
    for head in range(HEADS):
        cols = pl.ds(head * DH, DH)
        tiles = dot_last(keys[:, cols], queries[:, cols]) * score_scale
        for block in range(queries.shape[0] // MB):
            across = slice(block * MB, (block + 1) * MB)
            for slot in range(keys.shape[0] // MB):
                down = slice(slot * MB, (slot + 1) * MB)
                bound = bound_of(table, first_query + block, first_key + slot)
                scores[head, down, across] = jnp.where(
                    ahead <= bound, tiles[down, across], hidden
                )
                keep = kept(seed[0], first_head + head, first_query + block, first_key + slot, 1)
                keeps[head, down, across] = jnp.where(keep, jnp.float32(keep_scale), 0.0)


def stacked(*parts):
    def of_head(head):
        cols = slice(head * DH, (head + 1) * DH)
        return jnp.concatenate([ref[rows, cols] for ref, rows in parts], axis=0)

    return of_head


def near_window(key, value, near):
    whole = slice(None)
    keys = ((near, slice(0, ROWS)), (key, whole))
    values = ((near, slice(ROWS, None)), (value, whole))
    return keys, values


def far_window(key, value, near, far):
    keys, values = near_window(key, value, near)
    return ((far, slice(0, MB)), *keys), ((far, slice(MB, None)), *values)


def forward_kernel(
    table, seed, query, key, value, near, far, grad,
    signed_top, signed_low, attended, near_stats, far_stats,
):
    keys, values = far_window(key, value, near, far)
    stats = forward(
        table, seed, 0, query, stacked(*keys), stacked(*values), grad, signed_top, attended
    )
    near_stats[:, 0:MB] = stats
    far_stats[...] = stats
    keys, values = near_window(key, value, near)
    near_stats[:, MB:] = forward(
        table, seed, 1, query, stacked(*keys), stacked(*values), grad, signed_low, attended
    )


def later_kernel(
    table, seed, key, near_query, far_query, near_scores, near_keeps, far_scores, far_keeps
):
    block = lax.axis_index("blk") * 2
    later(table, seed, block + 2, block, near_query, key, near_scores, near_keeps)
    later(table, seed, block + 4, block + 1, far_query, key.at[MB:], far_scores, far_keeps)


def project(total, gathered, weight, core):
    parts, _, width = gathered.shape
    for part in range(parts):
        first = pl.multiple_of((part * 2 + core) * width, width)
        term = dot_last(gathered[part], weight[:, pl.ds(first, width)])
        total = term if total is None else total + term
    return total


def cut_kernel(weight, out):
    core = lax.rem(lax.axis_index("head"), 2)
    parts = lax.axis_size("head") // 2
    width = out.shape[1] // parts
    for part in range(parts):
        first = pl.multiple_of((part * 2 + 1 - core) * width, width)
        out[:, part * width : (part + 1) * width] = weight[:, pl.ds(first, width)]


def project_other_kernel(gathered, weight, out):
    parts, _, width = gathered.shape
    total = dot_last(gathered[0], weight[:, 0:width])
    for part in range(1, parts):
        total = total + dot_last(gathered[part], weight[:, part * width : (part + 1) * width])
    out[...] = bf16(total)


def project_own_kernel(gathered, weight, out):
    out[...] = project(None, gathered, weight, lax.rem(lax.axis_index("head"), 2))


def rows_kernel(own, received, grad, grad_top):
    whole = bf16(own[...] + f32(received[...]))
    grad[...] = whole
    grad_top[...] = whole[0:MB]


def own_kernel(
    signed_top, signed_low, attended, query, grad, key, value, near, far,
    grad_query, key_part, value_part,
):
    for head in range(HEADS):
        cols = slice(head * DH, (head + 1) * DH)
        key_sum = value_sum = None
        for block, signed, (keys, values) in (
            (0, signed_top, far_window(key, value, near, far)),
            (1, signed_low, near_window(key, value, near)),
        ):
            rows = slice(block * MB, (block + 1) * MB)
            grad_head = grad[rows, cols]
            row_dot = jnp.sum(f32(grad_head) * f32(attended[rows, cols]), axis=1, keepdims=True)
            grad_prob = dot_last(grad_head, stacked(*values)(head))
            probs = signed[head]
            first = probs.shape[1] - ROWS
            scaled = jnp.where(probs > 0.0, grad_prob * keep_scale, 0.0)
            dscore = bf16(jnp.abs(probs) * (scaled - row_dot))
            dropped = bf16(jnp.maximum(probs[:, first:], 0.0) * keep_scale)
            grad_query[rows, cols] = bf16(dot(dscore, stacked(*keys)(head)) * score_scale)
            key_term = dot_first(dscore[:, first:], query[rows, cols])
            value_term = dot_first(dropped, grad_head)
            key_sum = key_term if key_sum is None else key_sum + key_term
            value_sum = value_term if value_sum is None else value_sum + value_term
        key_part[:, cols] = key_sum
        value_part[:, cols] = value_sum


def finish_kernel(
    near_scores, near_keeps, far_scores, far_keeps, value, near_query, far_query, near_grad,
    far_grad, near_stats, far_stats, key_part, value_part, grad_key, grad_value,
):
    for head in range(HEADS):
        cols = pl.ds(head * DH, DH)

        def terms(scores, keeps, values, queries, grads, stats):
            grad_head = grads[:, cols]
            prob = jnp.exp(scores[head] - stats[head : head + 1])
            keep = keeps[head]
            grad_prob = dot_last(values, grad_head)
            dscore = bf16(prob * (grad_prob * keep - stats[HEADS + head : HEADS + head + 1]))
            return dot(dscore, queries[:, cols]), dot(bf16(prob * keep), grad_head)

        keys, values = terms(
            near_scores, near_keeps, value[:, cols], near_query, near_grad, near_stats
        )
        far_keys, far_values = terms(
            far_scores, far_keeps, value[MB:, cols], far_query, far_grad, far_stats
        )
        keys = keys + key_part[:, cols]
        values = values + value_part[:, cols]
        grad_key[0:MB, cols] = bf16(keys[0:MB] * score_scale)
        grad_key[MB:, cols] = bf16((keys[MB:] + far_keys) * score_scale)
        grad_value[0:MB, cols] = bf16(values[0:MB])
        grad_value[MB:, cols] = bf16(values[MB:] + far_values)


def call(kernel, specs, outs, microseconds, *args):
    shapes = [jax.ShapeDtypeStruct(shape, dtype) for shape, dtype in outs]
    moved = sum(a.size * a.dtype.itemsize for a in args)
    moved += sum(s.size * s.dtype.itemsize for s in shapes)
    flops = int(microseconds * 1.15e9)
    return pl.pallas_call(
        kernel,
        out_shape=shapes,
        in_specs=specs,
        out_specs=[VMEM] * len(shapes),
        compiler_params=pltpu.CompilerParams(vmem_limit_bytes=16 << 20),
        cost_estimate=pl.CostEstimate(flops=flops, bytes_accessed=min(moved, flops), transcendentals=0),
    )(*args)


def shifted(value, steps):
    count = lax.axis_size("blk")
    pairs = [(source, source + steps) for source in range(count) if 0 <= source + steps < count]
    return lax.ppermute(value, "blk", pairs)


def other_core(value):
    count = lax.axis_size("head")
    return lax.ppermute(value, "head", [(source, source ^ 1) for source in range(count)])


def on_device(query_rows, key_rows, value_rows, grad_out, out_weight, mask_types, drop_seed):
    half, full = jnp.bfloat16, jnp.float32
    count = lax.axis_size("head")
    groups = [list(range(first, count, 2)) for first in range(2)]

    copies = jnp.broadcast_to(grad_out[None], (count // 2, *grad_out.shape))
    gathered = lax.all_to_all(copies, "head", 0, 0, axis_index_groups=groups)
    near_query = shifted(query_rows, -1)
    far_keys = shifted(jnp.concatenate((key_rows[MB:], value_rows[MB:])), 2)
    far_query = shifted(query_rows[:MB], -2)

    width = (count // 2) * grad_out.shape[1]
    (theirs,) = call(cut_kernel, [VMEM], [((WIDE, width), half)], 0.0, out_weight)
    other_weight = other_core(theirs)
    own_keys = jnp.concatenate((key_rows, value_rows))
    near_query, far_query, own_keys = lax.optimization_barrier((near_query, far_query, own_keys))
    near_keys = shifted(own_keys, 1)
    gathered, other_weight, far_keys = lax.optimization_barrier(
        (gathered, other_weight, far_keys)
    )
    (sent,) = call(
        project_other_kernel, [VMEM] * 2, [((ROWS, WIDE), half)], 0.0, gathered, other_weight
    )
    received = other_core(sent)
    (own,) = call(
        project_own_kernel, [VMEM] * 2, [((ROWS, WIDE), full)], 0.0, gathered, out_weight
    )
    grad, grad_top = call(
        rows_kernel, [VMEM] * 2, [((ROWS, WIDE), half), ((MB, WIDE), half)], 0.0, own, received
    )
    near_grad = shifted(grad, -1)
    far_grad = shifted(grad_top, -2)
    signed_top, signed_low, attended, near_sums, far_sums = call(
        forward_kernel,
        [SMEM, SMEM] + [VMEM] * 6,
        [
            ((HEADS, MB, WIN), full),
            ((HEADS, MB, WIN - MB), full),
            ((ROWS, WIDE), half),
            ((STATS, ROWS), full),
            ((STATS, MB), full),
        ],
        0.0,
        mask_types, drop_seed, query_rows, key_rows, value_rows, near_keys, far_keys, grad,
    )
    near_stats = shifted(near_sums, -1)
    far_stats = shifted(far_sums, -2)
    grad_query, key_part, value_part = call(
        own_kernel,
        [VMEM] * 9,
        [((ROWS, WIDE), half), ((ROWS, WIDE), full), ((ROWS, WIDE), full)],
        0.0,
        signed_top, signed_low, attended, query_rows, grad, key_rows, value_rows, near_keys,
        far_keys,
    )
    later_key, _ = lax.optimization_barrier((key_rows, near_sums))
    scores = call(
        later_kernel, [SMEM, SMEM] + [VMEM] * 3,
        [((HEADS, ROWS, ROWS), full)] * 2 + [((HEADS, MB, MB), full)] * 2, 0.0,
        mask_types, drop_seed, later_key, near_query, far_query,
    )
    grad_key, grad_value = call(
        finish_kernel,
        [VMEM] * 13,
        [((ROWS, WIDE), half), ((ROWS, WIDE), half)],
        1.3,
        *scores, value_rows, near_query, far_query, near_grad, far_grad, near_stats, far_stats,
        key_part, value_part,
    )
    return (grad_query, grad_key, grad_value)


def solution(mesh):
    split = P("blk", "head")
    return jax.shard_map(
        on_device,
        mesh=mesh,
        in_specs=(split, split, split, split, P("head", None), P(), P()),
        out_specs=(split, split, split),
        check_vma=False,
    )
```

```python
import functools

import jax
import jax.numpy as jnp
from jax import lax
from jax.experimental import pallas as pl
from jax.experimental.pallas import tpu as pltpu
from jax.sharding import PartitionSpec as P

DH = 128
MB = 128
HEADS = 2
ROWS = 256
SLOTS = 5
WIN = SLOTS * MB
FAR = 3 * MB
WIDE = HEADS * DH
STATS = 8

drop_level = 6554
keep_scale = 65536.0 / 58982.0
mix_one = 73244475
mix_two = 295559667
mix_three = 668265263
score_scale = DH**-0.5
hidden = -1e30

VMEM = pl.BlockSpec(memory_space=pltpu.VMEM)
SMEM = pl.BlockSpec(memory_space=pltpu.SMEM)


def bf16(value):
    return value.astype(jnp.bfloat16)


def f32(value):
    return value.astype(jnp.float32)


def dot_last(left, right):
    return lax.dot_general(
        left, right, (((1,), (1,)), ((), ())), preferred_element_type=jnp.float32
    )


def dot_first(left, right):
    return lax.dot_general(
        left, right, (((0,), (0,)), ((), ())), preferred_element_type=jnp.float32
    )


def dot(left, right):
    return jnp.dot(left, right, preferred_element_type=jnp.float32)


def bound_of(table, query_block, key_block):
    last = table.shape[0] - 1
    inside = (key_block >= 0) & (query_block <= last)
    kind = table[jnp.minimum(query_block, last), jnp.maximum(key_block, 0)]
    far = jnp.int32(1 << 20)
    bound = jnp.where(kind == 2, far, jnp.where(kind == 1, (query_block - key_block) * MB, -far))
    return jnp.where(inside, bound, -far)


def kept(seed, head, query_block, key_block, query_axis):
    base = query_block * MB * mix_one + key_block * MB * mix_two + head * mix_three + seed
    rows = lax.broadcasted_iota(jnp.int32, (MB, MB), query_axis) * mix_one
    cols = lax.broadcasted_iota(jnp.int32, (MB, MB), 1 - query_axis) * mix_two
    hashed = (rows + cols) + base
    for _ in range(2):
        hashed = hashed ^ lax.shift_right_logical(hashed, jnp.int32(16))
        hashed = hashed * mix_one
    hashed = hashed ^ lax.shift_right_logical(hashed, jnp.int32(16))
    return (hashed & 65535) >= drop_level


def key_minus_query(query_axis):
    return lax.broadcasted_iota(jnp.int32, (MB, MB), 1 - query_axis) - lax.broadcasted_iota(
        jnp.int32, (MB, MB), query_axis
    )


def forward(table, seed, block, query, keys, values, grad, signed, attended):
    shard = lax.axis_index("blk")
    first_head = lax.axis_index("head") * HEADS
    count = keys(0).shape[0] // MB
    query_block = shard * 2 + block
    first_block = shard * 2 + 2 - count
    ahead = key_minus_query(0)
    lane = lax.broadcasted_iota(jnp.int32, (MB, MB), 1)
    rows = slice(block * MB, (block + 1) * MB)
    stats = jnp.zeros((MB, MB), jnp.float32)
    for head in range(HEADS):
        cols = pl.ds(head * DH, DH)
        scores = dot_last(query[rows, cols], keys(head))
        tiles = []
        for slot in range(count):
            bound = bound_of(table, query_block, first_block + slot)
            tile = scores[:, slot * MB : (slot + 1) * MB] * score_scale
            tiles.append(jnp.where(ahead <= bound, tile, hidden))
        top = functools.reduce(jnp.maximum, tiles)
        top = jnp.max(top, axis=1, keepdims=True)
        tiles = [jnp.exp(tile - top) for tile in tiles]
        total = jnp.sum(functools.reduce(jnp.add, tiles), axis=1, keepdims=True)
        inverse = 1.0 / total
        drops = []
        for slot in range(count):
            prob = tiles[slot] * inverse
            keep = kept(seed[0], first_head + head, query_block, first_block + slot, 0)
            signed[head, :, slot * MB : (slot + 1) * MB] = jnp.where(keep, prob, -prob)
            drops.append(bf16(jnp.where(keep, prob * keep_scale, 0.0)))
        mixed = bf16(dot(jnp.concatenate(drops, axis=1), values(head)))
        attended[rows, cols] = mixed
        row_dot = jnp.sum(f32(grad[rows, cols]) * f32(mixed), axis=1, keepdims=True)
        stats = jnp.where(lane == head, top + jnp.log(total), stats)
        stats = jnp.where(lane == HEADS + head, row_dot, stats)
    return stats.T[0:STATS]


def later(table, seed, first_query, first_key, queries, keys, scores, keeps):
    first_head = lax.axis_index("head") * HEADS
    ahead = key_minus_query(1)
    for head in range(HEADS):
        cols = pl.ds(head * DH, DH)
        tiles = dot_last(keys[:, cols], queries[:, cols]) * score_scale
        for block in range(queries.shape[0] // MB):
            across = slice(block * MB, (block + 1) * MB)
            for slot in range(keys.shape[0] // MB):
                down = slice(slot * MB, (slot + 1) * MB)
                bound = bound_of(table, first_query + block, first_key + slot)
                scores[head, down, across] = jnp.where(
                    ahead <= bound, tiles[down, across], hidden
                )
                keep = kept(seed[0], first_head + head, first_query + block, first_key + slot, 1)
                keeps[head, down, across] = jnp.where(keep, jnp.float32(keep_scale), 0.0)


def stacked(*parts):
    def of_head(head):
        cols = slice(head * DH, (head + 1) * DH)
        return jnp.concatenate([ref[rows, cols] for ref, rows in parts], axis=0)

    return of_head


def near_window(key, value, near):
    whole = slice(None)
    keys = ((near, slice(0, ROWS)), (key, whole))
    values = ((near, slice(ROWS, None)), (value, whole))
    return keys, values


def far_window(key, value, near, far):
    keys, values = near_window(key, value, near)
    return ((far, slice(0, MB)), *keys), ((far, slice(MB, None)), *values)


def forward_kernel(
    table, seed, query, key, value, near, far, grad,
    signed_top, signed_low, attended, near_stats, far_stats,
):
    keys, values = far_window(key, value, near, far)
    stats = forward(
        table, seed, 0, query, stacked(*keys), stacked(*values), grad, signed_top, attended
    )
    near_stats[:, 0:MB] = stats
    far_stats[...] = stats
    keys, values = near_window(key, value, near)
    near_stats[:, MB:] = forward(
        table, seed, 1, query, stacked(*keys), stacked(*values), grad, signed_low, attended
    )


def later_kernel(
    table, seed, key, near_query, far_query, near_scores, near_keeps, far_scores, far_keeps
):
    block = lax.axis_index("blk") * 2
    later(table, seed, block + 2, block, near_query, key, near_scores, near_keeps)
    later(table, seed, block + 4, block + 1, far_query, key.at[MB:], far_scores, far_keeps)


def project(total, gathered, weight, core):
    parts, _, width = gathered.shape
    for part in range(parts):
        first = pl.multiple_of((part * 2 + core) * width, width)
        term = dot_last(gathered[part], weight[:, pl.ds(first, width)])
        total = term if total is None else total + term
    return total


def cut_kernel(weight, out):
    core = lax.rem(lax.axis_index("head"), 2)
    parts = lax.axis_size("head") // 2
    width = out.shape[1] // parts
    for part in range(parts):
        first = pl.multiple_of((part * 2 + 1 - core) * width, width)
        out[:, part * width : (part + 1) * width] = weight[:, pl.ds(first, width)]


def project_other_kernel(gathered, weight, out):
    parts, _, width = gathered.shape
    total = dot_last(gathered[0], weight[:, 0:width])
    for part in range(1, parts):
        total = total + dot_last(gathered[part], weight[:, part * width : (part + 1) * width])
    out[...] = bf16(total)


def project_own_kernel(gathered, weight, out):
    out[...] = project(None, gathered, weight, lax.rem(lax.axis_index("head"), 2))


def rows_kernel(own, received, grad, grad_top):
    whole = bf16(own[...] + f32(received[...]))
    grad[...] = whole
    grad_top[...] = whole[0:MB]


def own_kernel(
    signed_top, signed_low, attended, query, grad, key, value, near, far,
    grad_query, key_part, value_part,
):
    for head in range(HEADS):
        cols = slice(head * DH, (head + 1) * DH)
        key_sum = value_sum = None
        for block, signed, (keys, values) in (
            (0, signed_top, far_window(key, value, near, far)),
            (1, signed_low, near_window(key, value, near)),
        ):
            rows = slice(block * MB, (block + 1) * MB)
            grad_head = grad[rows, cols]
            row_dot = jnp.sum(f32(grad_head) * f32(attended[rows, cols]), axis=1, keepdims=True)
            grad_prob = dot_last(grad_head, stacked(*values)(head))
            probs = signed[head]
            first = probs.shape[1] - ROWS
            scaled = jnp.where(probs > 0.0, grad_prob * keep_scale, 0.0)
            dscore = bf16(jnp.abs(probs) * (scaled - row_dot))
            dropped = bf16(jnp.maximum(probs[:, first:], 0.0) * keep_scale)
            grad_query[rows, cols] = bf16(dot(dscore, stacked(*keys)(head)) * score_scale)
            key_term = dot_first(dscore[:, first:], query[rows, cols])
            value_term = dot_first(dropped, grad_head)
            key_sum = key_term if key_sum is None else key_sum + key_term
            value_sum = value_term if value_sum is None else value_sum + value_term
        key_part[:, cols] = key_sum
        value_part[:, cols] = value_sum


def finish_kernel(
    near_scores, near_keeps, far_scores, far_keeps, value, near_query, far_query, near_grad,
    far_grad, near_stats, far_stats, key_part, value_part, grad_key, grad_value,
):
    for head in range(HEADS):
        cols = pl.ds(head * DH, DH)

        def terms(scores, keeps, values, queries, grads, stats):
            grad_head = grads[:, cols]
            prob = jnp.exp(scores[head] - stats[head : head + 1])
            keep = keeps[head]
            grad_prob = dot_last(values, grad_head)
            dscore = bf16(prob * (grad_prob * keep - stats[HEADS + head : HEADS + head + 1]))
            return dot(dscore, queries[:, cols]), dot(bf16(prob * keep), grad_head)

        keys, values = terms(
            near_scores, near_keeps, value[:, cols], near_query, near_grad, near_stats
        )
        far_keys, far_values = terms(
            far_scores, far_keeps, value[MB:, cols], far_query, far_grad, far_stats
        )
        keys = keys + key_part[:, cols]
        values = values + value_part[:, cols]
        grad_key[0:MB, cols] = bf16(keys[0:MB] * score_scale)
        grad_key[MB:, cols] = bf16((keys[MB:] + far_keys) * score_scale)
        grad_value[0:MB, cols] = bf16(values[0:MB])
        grad_value[MB:, cols] = bf16(values[MB:] + far_values)


def call(kernel, specs, outs, microseconds, *args):
    shapes = [jax.ShapeDtypeStruct(shape, dtype) for shape, dtype in outs]
    moved = sum(a.size * a.dtype.itemsize for a in args)
    moved += sum(s.size * s.dtype.itemsize for s in shapes)
    flops = int(microseconds * 1.15e9)
    return pl.pallas_call(
        kernel,
        out_shape=shapes,
        in_specs=specs,
        out_specs=[VMEM] * len(shapes),
        compiler_params=pltpu.CompilerParams(vmem_limit_bytes=16 << 20),
        cost_estimate=pl.CostEstimate(flops=flops, bytes_accessed=min(moved, flops), transcendentals=0),
    )(*args)


def shifted(value, steps):
    count = lax.axis_size("blk")
    pairs = [(source, source + steps) for source in range(count) if 0 <= source + steps < count]
    return lax.ppermute(value, "blk", pairs)


def other_core(value):
    count = lax.axis_size("head")
    return lax.ppermute(value, "head", [(source, source ^ 1) for source in range(count)])


def on_device(query_rows, key_rows, value_rows, grad_out, out_weight, mask_types, drop_seed):
    half, full = jnp.bfloat16, jnp.float32
    count = lax.axis_size("head")
    groups = [list(range(first, count, 2)) for first in range(2)]

    copies = jnp.broadcast_to(grad_out[None], (count // 2, *grad_out.shape))
    gathered = lax.all_to_all(copies, "head", 0, 0, axis_index_groups=groups)
    near_query = shifted(query_rows, -1)
    far_keys = shifted(jnp.concatenate((key_rows[MB:], value_rows[MB:])), 2)
    far_query = shifted(query_rows[:MB], -2)

    width = (count // 2) * grad_out.shape[1]
    own_keys = jnp.concatenate((key_rows, value_rows))
    near_query, far_query, own_keys, weight = lax.optimization_barrier(
        (near_query, far_query, own_keys, out_weight)
    )
    (theirs,) = call(cut_kernel, [VMEM], [((WIDE, width), half)], 0.0, weight)
    other_weight = other_core(theirs)
    near_keys = shifted(own_keys, 1)
    gathered, other_weight = lax.optimization_barrier((gathered, other_weight))
    (sent,) = call(
        project_other_kernel, [VMEM] * 2, [((ROWS, WIDE), half)], 0.0, gathered, other_weight
    )
    received = other_core(sent)
    (own,) = call(
        project_own_kernel, [VMEM] * 2, [((ROWS, WIDE), full)], 0.0, gathered, out_weight
    )
    grad, grad_top = call(
        rows_kernel, [VMEM] * 2, [((ROWS, WIDE), half), ((MB, WIDE), half)], 0.0, own, received
    )
    near_grad = shifted(grad, -1)
    far_grad = shifted(grad_top, -2)
    signed_top, signed_low, attended, near_sums, far_sums = call(
        forward_kernel,
        [SMEM, SMEM] + [VMEM] * 6,
        [
            ((HEADS, MB, WIN), full),
            ((HEADS, MB, WIN - MB), full),
            ((ROWS, WIDE), half),
            ((STATS, ROWS), full),
            ((STATS, MB), full),
        ],
        0.0,
        mask_types, drop_seed, query_rows, key_rows, value_rows, near_keys, far_keys, grad,
    )
    near_stats = shifted(near_sums, -1)
    far_stats = shifted(far_sums, -2)
    grad_query, key_part, value_part = call(
        own_kernel,
        [VMEM] * 9,
        [((ROWS, WIDE), half), ((ROWS, WIDE), full), ((ROWS, WIDE), full)],
        0.0,
        signed_top, signed_low, attended, query_rows, grad, key_rows, value_rows, near_keys,
        far_keys,
    )
    later_key, _ = lax.optimization_barrier((key_rows, near_sums))
    scores = call(
        later_kernel, [SMEM, SMEM] + [VMEM] * 3,
        [((HEADS, ROWS, ROWS), full)] * 2 + [((HEADS, MB, MB), full)] * 2, 0.0,
        mask_types, drop_seed, later_key, near_query, far_query,
    )
    grad_key, grad_value = call(
        finish_kernel,
        [VMEM] * 13,
        [((ROWS, WIDE), half), ((ROWS, WIDE), half)],
        1.3,
        *scores, value_rows, near_query, far_query, near_grad, far_grad, near_stats, far_stats,
        key_part, value_part,
    )
    return (grad_query, grad_key, grad_value)


def solution(mesh):
    split = P("blk", "head")
    return jax.shard_map(
        on_device,
        mesh=mesh,
        in_specs=(split, split, split, split, P("head", None), P(), P()),
        out_specs=(split, split, split),
        check_vma=False,
    )
```
